512 devices in a mesh: ctx: 64 (over x, y, core), head: 8 (over z).
Axes of the slice: x: 4, y: 8, z: 8, core: 2. Of those that a mesh axis runs over, the one named last changes fastest.
Arguments:
- query_rows: bfloat16 [65536, 1024], P(('ctx', 'head')), may hold values from -6 to 6
- key_rows: bfloat16 [65536, 1024], P(('ctx', 'head')), may hold values from -6 to 6
- value_rows: bfloat16 [65536, 2048], P(('ctx', 'head')), may hold values from -6 to 6
- gate_rows: bfloat16 [65536, 2048], P(('ctx', 'head')), may hold values from -6 to 6
- log_decay: bfloat16 [65536, 16], P(('ctx', 'head')), may hold values from -0.8 to 0, as said below
- write_strength: bfloat16 [65536, 16], P(('ctx', 'head')), may hold values from 0 to 1, as said below
- conv_query: bfloat16 [4, 1024], P(None, 'head'), may hold values from -3 to 3
- conv_key: bfloat16 [4, 1024], P(None, 'head'), may hold values from -3 to 3
- conv_value: bfloat16 [4, 2048], P(None, 'head'), may hold values from -3 to 3
- norm_gain: float32 [128], replicated, may hold values from 0.1 to 1.9
Outputs:
- layer_out: bfloat16 [65536, 2048], P(('ctx', 'head'))
The draws below stay inside these ranges and needn't reach their ends.
Inputs may be any that keep to these rules, and one draw needn't show every extreme that they name: log_decay holds natural logarithms of decay factors. write_strength lies strictly between 0 and 1.
All inputs are finite; a program needn't handle non-finite values.
Results may differ from the reference program's by a relative error of at most 0.001.
Values may be sent and summed in bfloat16 or wider, within the bound.
A program may use at most 128 MiB of HBM per device.

```python
import jax
import jax.numpy as jnp
from jax import lax

DK = 128
DV = 128
KW = 4
HK = 8
HV = 16
BLOCK = 64
CONTEXT_LENGTH = 65536


def head_kinds(key, heads):
    picker = jax.random.fold_in(key, 11)
    return jax.random.randint(picker, (heads,), 0, 2) == 1


def draw_log_decay(key, part):
    quickly = head_kinds(key, HV)
    approximate_cost = jax.random.uniform(jax.random.fold_in(key, 21), (CONTEXT_LENGTH, HV), jnp.float32, 0.5, 1.5)
    slow_rate = jax.random.uniform(jax.random.fold_in(key, 22), (HV,), jnp.float32, 0.2, 0.6) / CONTEXT_LENGTH
    fast_rate = 1.0 / jax.random.uniform(jax.random.fold_in(key, 23), (HV,), jnp.float32, 30.0, 50.0)
    fading_factors = jnp.where(quickly, fast_rate, slow_rate)
    position_indices = jax.random.randint(jax.random.fold_in(key, 24), (3, HV), 0, CONTEXT_LENGTH)
    position_window = jnp.any(jnp.arange(CONTEXT_LENGTH)[None, :, None] == position_indices[:, None, :], axis=0)
    fading_logits = jnp.log(jax.random.uniform(jax.random.fold_in(key, 25), (CONTEXT_LENGTH, HV), jnp.float32, 0.5, 0.8))
    return (-fading_factors[None, :] * approximate_cost + jnp.where(position_window, fading_logits, 0.0)).astype(jnp.bfloat16)


def draw_write_strength(key, part):
    quickly = head_kinds(key, HV)
    approximate_cost = jax.random.uniform(jax.random.fold_in(key, 31), (CONTEXT_LENGTH, HV), jnp.float32, 0.5, 1.5)
    slow_level = jnp.minimum(jax.random.uniform(jax.random.fold_in(key, 32), (HV,), jnp.float32, 0.2, 0.8) * DK / CONTEXT_LENGTH, 0.3)
    fast_level = jax.random.uniform(jax.random.fold_in(key, 33), (HV,), jnp.float32, 0.3, 0.6)
    return (jnp.where(quickly, fast_level, slow_level)[None, :] * approximate_cost).astype(jnp.bfloat16)


def block_levels(own_key, dims, shards, low, largest):
    def one(axis_at, parts):
        heights = jax.random.uniform(jax.random.fold_in(jax.random.fold_in(own_key, 6), axis_at), (parts,), jnp.float32, low / len(shards), largest / len(shards))
        return jnp.repeat(jnp.exp(heights), dims[axis_at] // parts).reshape((-1,) + (1,) * (len(dims) - axis_at - 1))

    factor_of = one(*shards[0])
    for cut in shards[1:]:
        factor_of = factor_of * one(*cut)
    return factor_of


def scatter_about(key, shape, scale, most, split=(), held_as=jnp.bfloat16):
    factor_of = block_levels(key, shape, split, -0.22, 0.18) if split else 1.0
    values = jax.random.normal(key, shape, jnp.float32) * scale * factor_of
    return jnp.minimum(jnp.maximum(values, -most), most).astype(held_as)


def setup_inputs(seed: int = 0) -> dict:
    arg_keys = jax.random.split(jax.random.key(seed), 11)
    return {
        "query_rows": scatter_about(arg_keys[0], (CONTEXT_LENGTH, HK * DK), 1.0, 6.0, ((0, 512),)),
        "key_rows": scatter_about(arg_keys[1], (CONTEXT_LENGTH, HK * DK), 1.0, 6.0, ((0, 512),)),
        "value_rows": scatter_about(arg_keys[2], (CONTEXT_LENGTH, HV * DV), 1.0, 6.0, ((0, 512),)),
        "gate_rows": scatter_about(arg_keys[3], (CONTEXT_LENGTH, HV * DV), 1.0, 6.0, ((0, 512),)),
        "log_decay": draw_log_decay(jax.random.fold_in(arg_keys[10], 71), 0),
        "write_strength": draw_write_strength(jax.random.fold_in(arg_keys[10], 71), 0),
        "conv_query": scatter_about(arg_keys[6], (KW, HK * DK), 0.5, 3.0, ((1, 8),)),
        "conv_key": scatter_about(arg_keys[7], (KW, HK * DK), 0.5, 3.0, ((1, 8),)),
        "conv_value": scatter_about(arg_keys[8], (KW, HV * DV), 0.5, 3.0, ((1, 8),)),
        "norm_gain": jnp.clip(1.0 + 0.18 * jax.random.normal(arg_keys[9], (DV,), jnp.float32), 0.1, 1.9),
    }


HIGHEST_PRECISION = lax.Precision.HIGHEST
EPSILON = 1e-06

def forward_substitution(coupling, targets):
    block_len = coupling.shape[-1]
    axis_rows = targets.ndim - 2

    def advance(position, solved):
        position = jnp.asarray(position).astype(jnp.int32)
        coefficient = lax.dynamic_slice_in_dim(coupling, position, 1, axis_rows)
        accumulated = jnp.einsum('...ij,...jf->...if', coefficient, solved, precision=HIGHEST_PRECISION)
        current = lax.dynamic_slice_in_dim(targets, position, 1, axis_rows) - accumulated
        return lax.dynamic_update_slice_in_dim(solved, current, position, axis_rows)
    return lax.fori_loop(0, block_len, advance, jnp.zeros_like(targets))

def causal_conv(inputs, earlier_rows, weights):
    kernel_width = weights.shape[0]
    count_rows = inputs.shape[0]
    joined = jnp.concatenate([earlier_rows, inputs], axis=0)
    result = joined[kernel_width - 1:] * weights[kernel_width - 1]
    for offset in range(1, kernel_width):
        result = result + joined[kernel_width - 1 - offset:kernel_width - 1 - offset + count_rows] * weights[kernel_width - 1 - offset]
    return jax.nn.silu(result)

def unit_heads(mixed, heads):
    shaped = mixed.reshape(mixed.shape[0], heads, -1)
    return shaped / jnp.sqrt(lax.optimization_barrier(jnp.sum(shaped * shaped, axis=-1, keepdims=True)) + EPSILON)

def into_blocks(array, block_len):
    count_rows, heads, inner_dim = array.shape
    return array.reshape(count_rows // block_len, block_len, heads, inner_dim).transpose(0, 2, 1, 3)

def block_scalars(array, block_len):
    count_rows, heads = array.shape
    return array.astype(jnp.float32).reshape(count_rows // block_len, block_len, heads).transpose(0, 2, 1)

def block_terms(queries, keys, values, log_gate, strength):
    block_len = queries.shape[2]
    key_dim = keys.shape[-1]
    cumulative = jnp.cumsum(log_gate, axis=-1)
    rows_index = jnp.arange(block_len)[:, None]
    cols_index = jnp.arange(block_len)[None, :]
    causal = rows_index >= cols_index
    strictly = rows_index > cols_index
    spread = jnp.where(causal, cumulative[..., :, None] - cumulative[..., None, :], 0.0)
    decays = jnp.where(causal, jnp.exp(spread), 0.0)
    key_key = jnp.einsum('nhid,nhjd->nhij', keys, keys, precision=HIGHEST_PRECISION)
    coupling = jnp.where(strictly, strength[..., None] * decays * key_key, 0.0)
    targets = jnp.concatenate([(strength * jnp.exp(cumulative))[..., None] * keys, strength[..., None] * values], axis=-1)
    solved = forward_substitution(coupling, targets)
    key_part = solved[..., :key_dim]
    value_part = solved[..., key_dim:]
    query_key = jnp.einsum('nhid,nhjd->nhij', queries, keys, precision=HIGHEST_PRECISION)
    within = query_key * decays
    query_decay = jnp.exp(cumulative)[..., None] * queries
    closing_logarithm = cumulative[..., -1:]
    key_decay = jnp.exp(closing_logarithm - cumulative)[..., None] * keys
    end_decay = jnp.exp(closing_logarithm[..., 0])
    return (key_part, value_part, within, query_decay, key_decay, end_decay)

def block_apply(memory, pieces):
    key_part, value_part, within, query_decay, key_decay, end_decay = pieces
    corrected = value_part - jnp.einsum('hcd,hde->hce', key_part, memory, precision=HIGHEST_PRECISION)
    result = jnp.einsum('hcd,hde->hce', query_decay, memory, precision=HIGHEST_PRECISION)
    result = result + jnp.einsum('hij,hje->hie', within, corrected, precision=HIGHEST_PRECISION)
    memory = end_decay[:, None, None] * memory + jnp.einsum('hcd,hce->hde', key_decay, corrected, precision=HIGHEST_PRECISION)
    return (memory, result)

def gated_norm(outputs, gate, gain):
    meansq = lax.optimization_barrier(jnp.mean(outputs * outputs, axis=-1, keepdims=True))
    scaled = outputs / jnp.sqrt(meansq + EPSILON) * gain * jax.nn.silu(gate)
    return scaled.astype(jnp.bfloat16).reshape(outputs.shape[0], -1)

def reference(query_rows, key_rows, value_rows, gate_rows, log_decay, write_strength, conv_query, conv_key, conv_value, norm_gain):
    blocks = CONTEXT_LENGTH // BLOCK
    per_key = HV // HK
    key_width = HK * DK

    def split_rows(array):
        return array.reshape(blocks, BLOCK, array.shape[-1])
    stacked = (split_rows(query_rows), split_rows(key_rows), split_rows(value_rows), split_rows(gate_rows), split_rows(log_decay), split_rows(write_strength))
    weights_all = jnp.concatenate([conv_query, conv_key, conv_value], axis=1).astype(jnp.float32)

    def advance(carry, pieces):
        earlier_rows, memory = carry
        query_piece, key_piece, value_piece, gate_piece, decay_piece, strength_piece = pieces
        joined = jnp.concatenate([query_piece, key_piece, value_piece], axis=1).astype(jnp.float32)
        mixed = causal_conv(joined, earlier_rows, weights_all)
        next_rows = jnp.concatenate([earlier_rows, joined], axis=0)[BLOCK:]
        query_heads = jnp.repeat(unit_heads(mixed[:, :key_width], HK) * DK ** (-0.5), per_key, axis=1)
        key_heads = jnp.repeat(unit_heads(mixed[:, key_width:2 * key_width], HK), per_key, axis=1)
        value_heads = mixed[:, 2 * key_width:].reshape(BLOCK, HV, DV)
        terms = block_terms(into_blocks(query_heads, BLOCK), into_blocks(key_heads, BLOCK), into_blocks(value_heads, BLOCK), block_scalars(decay_piece, BLOCK), block_scalars(strength_piece, BLOCK))
        single = tuple((member[0] for member in terms))
        memory, result = block_apply(memory, single)
        outputs = result.transpose(1, 0, 2)
        gate = gate_piece.astype(jnp.float32).reshape(BLOCK, HV, DV)
        return ((next_rows, memory), gated_norm(outputs, gate, norm_gain))
    start_rows = jnp.zeros((KW - 1, 2 * key_width + HV * DV), jnp.float32)
    start_memory = jnp.zeros((HV, DK, DV), jnp.float32)
    produced = lax.scan(advance, (start_rows, start_memory), stacked)[1]
    return produced.reshape(CONTEXT_LENGTH, HV * DV)
```

```python
import jax
import jax.numpy as jnp
from jax import lax
from jax.sharding import PartitionSpec as P

DK = 128
DV = 128
HK = 8
HV = 16
BLOCK = 64


HIGHEST_PRECISION = lax.Precision.HIGHEST
EPSILON = 1e-06


def passed_along(value, axis, steps):
    count = lax.axis_size(axis)
    leading, last = (max(0, -steps), min(count, count - steps))
    return lax.ppermute(value, axis, [(source, source + steps) for source in range(leading, last)])


def matmul(spec, left, right):
    return jnp.einsum(spec, left, right, precision=HIGHEST_PRECISION)


def unit_lower_inverse(strict):
    size = strict.shape[-1]
    rows_index = jnp.arange(size)[:, None]
    cols_index = jnp.arange(size)[None, :]
    inverse = jnp.broadcast_to(jnp.eye(size, dtype=strict.dtype), strict.shape)
    width = 1
    while width < size:
        pick = (
            (rows_index // (2 * width) == cols_index // (2 * width))
            & ((rows_index // width) % 2 == 1)
            & ((cols_index // width) % 2 == 0)
        )
        lower = jnp.where(pick, strict, 0.0)
        step = matmul("...ij,...jk->...ik", inverse, matmul("...ij,...jk->...ik", lower, inverse))
        inverse = inverse - lax.optimization_barrier(step)
        width *= 2
    return inverse


def forward_substitution(coupling, targets):
    return matmul("...ij,...jf->...if", unit_lower_inverse(coupling), targets)


def causal_conv(inputs, earlier_rows, weights):
    kernel_width = weights.shape[0]
    count_rows = inputs.shape[0]
    joined = jnp.concatenate([earlier_rows, inputs], axis=0)
    result = joined[kernel_width - 1 :] * weights[kernel_width - 1]
    for offset in range(1, kernel_width):
        result = (
            result
            + joined[kernel_width - 1 - offset : kernel_width - 1 - offset + count_rows]
            * weights[kernel_width - 1 - offset]
        )
    return jax.nn.silu(result)


def unit_heads(mixed, heads):
    shaped = mixed.reshape(mixed.shape[0], heads, -1)
    return shaped / jnp.sqrt(jnp.sum(shaped * shaped, axis=-1, keepdims=True) + EPSILON)


def into_blocks(array, block_len):
    count_rows, heads, inner_dim = array.shape
    return array.reshape(count_rows // block_len, block_len, heads, inner_dim).transpose(0, 2, 1, 3)


def block_scalars(array, block_len):
    count_rows, heads = array.shape
    return (
        array.astype(jnp.float32)
        .reshape(count_rows // block_len, block_len, heads)
        .transpose(0, 2, 1)
    )


def block_terms(queries, keys, values, log_gate, strength):
    block_len = queries.shape[2]
    key_dim = keys.shape[-1]
    cumulative = jnp.cumsum(log_gate, axis=-1)
    rows_index = jnp.arange(block_len)[:, None]
    cols_index = jnp.arange(block_len)[None, :]
    causal = rows_index >= cols_index
    strictly = rows_index > cols_index
    spread = jnp.where(causal, cumulative[..., :, None] - cumulative[..., None, :], 0.0)
    decays = jnp.where(causal, jnp.exp(spread), 0.0)
    key_key = jnp.einsum("nhid,nhjd->nhij", keys, keys, precision=HIGHEST_PRECISION)
    coupling = jnp.where(strictly, strength[..., None] * decays * key_key, 0.0)
    targets = jnp.concatenate(
        [(strength * jnp.exp(cumulative))[..., None] * keys, strength[..., None] * values], axis=-1
    )
    solved = forward_substitution(coupling, targets)
    key_part = solved[..., :key_dim]
    value_part = solved[..., key_dim:]
    query_key = jnp.einsum("nhid,nhjd->nhij", queries, keys, precision=HIGHEST_PRECISION)
    within = query_key * decays
    query_decay = jnp.exp(cumulative)[..., None] * queries
    closing_logarithm = cumulative[..., -1:]
    key_decay = jnp.exp(closing_logarithm - cumulative)[..., None] * keys
    end_decay = jnp.exp(closing_logarithm[..., 0])
    return (key_part, value_part, within, query_decay, key_decay, end_decay)


def block_apply(memory, pieces):
    key_part, value_part, within, query_decay, key_decay, end_decay = pieces
    corrected = value_part - jnp.einsum(
        "hcd,hde->hce", key_part, memory, precision=HIGHEST_PRECISION
    )
    result = jnp.einsum("hcd,hde->hce", query_decay, memory, precision=HIGHEST_PRECISION)
    result = result + jnp.einsum("hij,hje->hie", within, corrected, precision=HIGHEST_PRECISION)
    memory = end_decay[:, None, None] * memory + jnp.einsum(
        "hcd,hce->hde", key_decay, corrected, precision=HIGHEST_PRECISION
    )
    return (memory, result)


def gated_norm(outputs, gate, gain):
    meansq = jnp.mean(outputs * outputs, axis=-1, keepdims=True)
    scaled = outputs / jnp.sqrt(meansq + EPSILON) * gain * jax.nn.silu(gate)
    return scaled.astype(jnp.bfloat16).reshape(outputs.shape[0], -1)


def compose_maps(later_map, earlier_map):
    return jnp.einsum("hij,hjk->hik", later_map, earlier_map, precision=HIGHEST_PRECISION)


def on_device(
    query_rows,
    key_rows,
    value_rows,
    gate_rows,
    log_decay,
    write_strength,
    conv_query,
    conv_key,
    conv_value,
    norm_gain,
):
    device_query, local_key, local_value, local_gate, local_decay, local_strength = (
        lax.all_to_all(query_rows, "head", split_axis=1, concat_axis=0, tiled=True),
        lax.all_to_all(key_rows, "head", split_axis=1, concat_axis=0, tiled=True),
        lax.all_to_all(value_rows, "head", split_axis=1, concat_axis=0, tiled=True),
        lax.all_to_all(gate_rows, "head", split_axis=1, concat_axis=0, tiled=True),
        lax.all_to_all(log_decay, "head", split_axis=1, concat_axis=0, tiled=True),
        lax.all_to_all(write_strength, "head", split_axis=1, concat_axis=0, tiled=True),
    )
    joined = jnp.concatenate([device_query, local_key, local_value], axis=1)
    kernel_width = conv_query.shape[0]
    count_rows = joined.shape[0]
    tail_rows = passed_along(joined[count_rows - (kernel_width - 1) :], "ctx", 1)
    weights_all = jnp.concatenate([conv_query, conv_key, conv_value], axis=1).astype(jnp.float32)
    mixed = causal_conv(joined.astype(jnp.float32), tail_rows.astype(jnp.float32), weights_all)
    key_width = device_query.shape[1]
    head_keys = key_width // DK
    per_key = HV // HK
    query_heads = jnp.repeat(
        unit_heads(mixed[:, :key_width], head_keys) * DK ** (-0.5), per_key, axis=1
    )
    key_heads = jnp.repeat(
        unit_heads(mixed[:, key_width : 2 * key_width], head_keys), per_key, axis=1
    )
    value_heads = mixed[:, 2 * key_width :].reshape(count_rows, -1, DV)
    terms = block_terms(
        into_blocks(query_heads, BLOCK),
        into_blocks(key_heads, BLOCK),
        into_blocks(value_heads, BLOCK),
        block_scalars(local_decay, BLOCK),
        block_scalars(local_strength, BLOCK),
    )
    key_part, value_part, within, query_decay, key_decay, end_decay = terms
    heads_here = key_part.shape[1]
    identity_mat = jnp.broadcast_to(jnp.eye(DK, dtype=jnp.float32), (heads_here, DK, DK))
    trans = end_decay[..., None, None] * identity_mat - matmul(
        "nhcd,nhce->nhde", key_decay, key_part
    )
    bias = matmul("nhcd,nhce->nhde", key_decay, value_part)
    blocks_here = trans.shape[0]
    span = 1
    while span < blocks_here:
        earlier_trans = jnp.concatenate(
            [jnp.broadcast_to(identity_mat, (span,) + identity_mat.shape), trans[:-span]], axis=0
        )
        earlier_bias = jnp.concatenate([jnp.zeros_like(bias[:span]), bias[:-span]], axis=0)
        trans, bias = (
            matmul("nhij,nhjk->nhik", trans, earlier_trans),
            matmul("nhij,nhjk->nhik", trans, earlier_bias) + bias,
        )
        span *= 2
    total_trans, total_bias = trans[-1], bias[-1]
    place = lax.axis_index("ctx")
    count = lax.axis_size("ctx")
    span = 1
    while span < count:
        if 2 * span < count:
            arrived = passed_along(jnp.stack([total_trans, total_bias]), "ctx", span)
            total_trans, total_bias = (
                jnp.where(place >= span, compose_maps(total_trans, arrived[0]), total_trans),
                compose_maps(total_trans, arrived[1]) + total_bias,
            )
        else:
            total_bias = compose_maps(total_trans, passed_along(total_bias, "ctx", span)) + total_bias
        span *= 2
    initial = passed_along(total_bias, "ctx", 1)
    earlier_trans = jnp.concatenate([identity_mat[None], trans[:-1]], axis=0)
    earlier_bias = jnp.concatenate([jnp.zeros_like(bias[:1]), bias[:-1]], axis=0)
    starts = matmul("nhij,hjk->nhik", earlier_trans, initial) + earlier_bias
    corrected = value_part - matmul("nhcd,nhde->nhce", key_part, starts)
    produced = matmul("nhcd,nhde->nhce", query_decay, starts) + matmul(
        "nhij,nhje->nhie", within, corrected
    )
    outputs = produced.transpose(0, 2, 1, 3).reshape(count_rows, heads_here, DV)
    gate = local_gate.astype(jnp.float32).reshape(count_rows, heads_here, DV)
    normed = gated_norm(outputs, gate, norm_gain)
    return lax.all_to_all(normed, "head", split_axis=0, concat_axis=1, tiled=True)


def solution(mesh):
    in_specs = (
        P(("ctx", "head"), None),
        P(("ctx", "head"), None),
        P(("ctx", "head"), None),
        P(("ctx", "head"), None),
        P(("ctx", "head"), None),
        P(("ctx", "head"), None),
        P(None, "head"),
        P(None, "head"),
        P(None, "head"),
        P(),
    )
    out_specs = P(("ctx", "head"), None)
    return jax.shard_map(
        on_device, mesh=mesh, in_specs=in_specs, out_specs=out_specs, check_vma=False
    )
```

```python
import jax
import jax.numpy as jnp
from jax import lax
from jax.sharding import PartitionSpec as P

DK = 128
DV = 128
HK = 8
HV = 16
BLOCK = 64


HIGHEST_PRECISION = lax.Precision.HIGHEST
EPSILON = 1e-06


def passed_along(value, axis, steps):
    count = lax.axis_size(axis)
    leading, last = (max(0, -steps), min(count, count - steps))
    return lax.ppermute(value, axis, [(source, source + steps) for source in range(leading, last)])


def matmul(spec, left, right):
    return jnp.einsum(spec, left, right, precision=HIGHEST_PRECISION)


def unit_lower_inverse(strict):
    size = strict.shape[-1]
    rows_index = jnp.arange(size)[:, None]
    cols_index = jnp.arange(size)[None, :]
    inverse = jnp.broadcast_to(jnp.eye(size, dtype=strict.dtype), strict.shape)
    width = 1
    while width < size:
        pick = (
            (rows_index // (2 * width) == cols_index // (2 * width))
            & ((rows_index // width) % 2 == 1)
            & ((cols_index // width) % 2 == 0)
        )
        lower = jnp.where(pick, strict, 0.0)
        step = matmul("...ij,...jk->...ik", inverse, matmul("...ij,...jk->...ik", lower, inverse))
        inverse = inverse - lax.optimization_barrier(step)
        width *= 2
    return inverse


def forward_substitution(coupling, targets):
    return matmul("...ij,...jf->...if", unit_lower_inverse(coupling), targets)


def causal_conv(inputs, earlier_rows, weights):
    kernel_width = weights.shape[0]
    count_rows = inputs.shape[0]
    joined = jnp.concatenate([earlier_rows, inputs], axis=0)
    result = joined[kernel_width - 1 :] * weights[kernel_width - 1]
    for offset in range(1, kernel_width):
        result = (
            result
            + joined[kernel_width - 1 - offset : kernel_width - 1 - offset + count_rows]
            * weights[kernel_width - 1 - offset]
        )
    return jax.nn.silu(result)


def unit_heads(mixed, heads):
    shaped = mixed.reshape(mixed.shape[0], heads, -1)
    return shaped / jnp.sqrt(jnp.sum(shaped * shaped, axis=-1, keepdims=True) + EPSILON)


def into_blocks(array, block_len):
    count_rows, heads, inner_dim = array.shape
    return array.reshape(count_rows // block_len, block_len, heads, inner_dim).transpose(0, 2, 1, 3)


def block_scalars(array, block_len):
    count_rows, heads = array.shape
    return (
        array.astype(jnp.float32)
        .reshape(count_rows // block_len, block_len, heads)
        .transpose(0, 2, 1)
    )


def block_terms(queries, keys, values, log_gate, strength):
    block_len = queries.shape[2]
    key_dim = keys.shape[-1]
    cumulative = jnp.cumsum(log_gate, axis=-1)
    rows_index = jnp.arange(block_len)[:, None]
    cols_index = jnp.arange(block_len)[None, :]
    causal = rows_index >= cols_index
    strictly = rows_index > cols_index
    spread = jnp.where(causal, cumulative[..., :, None] - cumulative[..., None, :], 0.0)
    decays = jnp.where(causal, jnp.exp(spread), 0.0)
    key_key = jnp.einsum("nhid,nhjd->nhij", keys, keys, precision=HIGHEST_PRECISION)
    coupling = jnp.where(strictly, strength[..., None] * decays * key_key, 0.0)
    targets = jnp.concatenate(
        [(strength * jnp.exp(cumulative))[..., None] * keys, strength[..., None] * values], axis=-1
    )
    solved = forward_substitution(coupling, targets)
    key_part = solved[..., :key_dim]
    value_part = solved[..., key_dim:]
    query_key = jnp.einsum("nhid,nhjd->nhij", queries, keys, precision=HIGHEST_PRECISION)
    within = query_key * decays
    query_decay = jnp.exp(cumulative)[..., None] * queries
    closing_logarithm = cumulative[..., -1:]
    key_decay = jnp.exp(closing_logarithm - cumulative)[..., None] * keys
    end_decay = jnp.exp(closing_logarithm[..., 0])
    return (key_part, value_part, within, query_decay, key_decay, end_decay)


def block_apply(memory, pieces):
    key_part, value_part, within, query_decay, key_decay, end_decay = pieces
    corrected = value_part - jnp.einsum(
        "hcd,hde->hce", key_part, memory, precision=HIGHEST_PRECISION
    )
    result = jnp.einsum("hcd,hde->hce", query_decay, memory, precision=HIGHEST_PRECISION)
    result = result + jnp.einsum("hij,hje->hie", within, corrected, precision=HIGHEST_PRECISION)
    memory = end_decay[:, None, None] * memory + jnp.einsum(
        "hcd,hce->hde", key_decay, corrected, precision=HIGHEST_PRECISION
    )
    return (memory, result)


def gated_norm(outputs, gate, gain):
    meansq = jnp.mean(outputs * outputs, axis=-1, keepdims=True)
    scaled = outputs / jnp.sqrt(meansq + EPSILON) * gain * jax.nn.silu(gate)
    return scaled.astype(jnp.bfloat16).reshape(outputs.shape[0], -1)


def compose_maps(later_map, earlier_map):
    return jnp.einsum("hij,hjk->hik", later_map, earlier_map, precision=HIGHEST_PRECISION)


def on_device(
    query_rows,
    key_rows,
    value_rows,
    gate_rows,
    log_decay,
    write_strength,
    conv_query,
    conv_key,
    conv_value,
    norm_gain,
):
    parts = lax.axis_size("head")
    pieces = (query_rows, key_rows, value_rows, log_decay, write_strength)
    widths = [piece.shape[1] // parts for piece in pieces]
    packed = jnp.concatenate(
        [piece.reshape(piece.shape[0], parts, -1) for piece in pieces], axis=2
    )
    moved = lax.all_to_all(packed, "head", split_axis=1, concat_axis=0, tiled=True)
    moved = moved.reshape(moved.shape[0], -1)
    offsets = [sum(widths[:index]) for index in range(len(widths) + 1)]
    device_query, local_key, local_value, local_decay, local_strength = (
        moved[:, offsets[index] : offsets[index + 1]] for index in range(len(widths))
    )
    local_gate = lax.all_to_all(gate_rows, "head", split_axis=1, concat_axis=0, tiled=True)
    joined = jnp.concatenate([earlier_rows, inputs], axis=0)
    result = joined[kernel_width - 1 :] * weights[kernel_width - 1]
    for offset in range(1, kernel_width):
        result = (
            result
            + joined[kernel_width - 1 - offset : kernel_width - 1 - offset + count_rows]
            * weights[kernel_width - 1 - offset]
        )
    return jax.nn.silu(result)


def unit_heads(mixed, heads):
    shaped = mixed.reshape(mixed.shape[0], heads, -1)
    return shaped / jnp.sqrt(jnp.sum(shaped * shaped, axis=-1, keepdims=True) + EPSILON)


def into_blocks(array, block_len):
    count_rows, heads, inner_dim = array.shape
    return array.reshape(count_rows // block_len, block_len, heads, inner_dim).transpose(0, 2, 1, 3)


def block_scalars(array, block_len):
    count_rows, heads = array.shape
    return (
        array.astype(jnp.float32)
        .reshape(count_rows // block_len, block_len, heads)
        .transpose(0, 2, 1)
    )


def block_terms(queries, keys, values, log_gate, strength):
    block_len = queries.shape[2]
    key_dim = keys.shape[-1]
    cumulative = jnp.cumsum(log_gate, axis=-1)
    rows_index = jnp.arange(block_len)[:, None]
    cols_index = jnp.arange(block_len)[None, :]
    causal = rows_index >= cols_index
    strictly = rows_index > cols_index
    spread = jnp.where(causal, cumulative[..., :, None] - cumulative[..., None, :], 0.0)
    decays = jnp.where(causal, jnp.exp(spread), 0.0)
    key_key = jnp.einsum("nhid,nhjd->nhij", keys, keys, precision=HIGHEST_PRECISION)
    coupling = jnp.where(strictly, strength[..., None] * decays * key_key, 0.0)
    targets = jnp.concatenate(
        [(strength * jnp.exp(cumulative))[..., None] * keys, strength[..., None] * values], axis=-1
    )
    solved = forward_substitution(coupling, targets)
    key_part = solved[..., :key_dim]
    value_part = solved[..., key_dim:]
    query_key = jnp.einsum("nhid,nhjd->nhij", queries, keys, precision=HIGHEST_PRECISION)
    within = query_key * decays
    query_decay = jnp.exp(cumulative)[..., None] * queries
    closing_logarithm = cumulative[..., -1:]
    key_decay = jnp.exp(closing_logarithm - cumulative)[..., None] * keys
    end_decay = jnp.exp(closing_logarithm[..., 0])
    return (key_part, value_part, within, query_decay, key_decay, end_decay)


def block_apply(memory, pieces):
    key_part, value_part, within, query_decay, key_decay, end_decay = pieces
    corrected = value_part - jnp.einsum(
        "hcd,hde->hce", key_part, memory, precision=HIGHEST_PRECISION
    )
    result = jnp.einsum("hcd,hde->hce", query_decay, memory, precision=HIGHEST_PRECISION)
    result = result + jnp.einsum("hij,hje->hie", within, corrected, precision=HIGHEST_PRECISION)
    memory = end_decay[:, None, None] * memory + jnp.einsum(
        "hcd,hce->hde", key_decay, corrected, precision=HIGHEST_PRECISION
    )
    return (memory, result)


def gated_norm(outputs, gate, gain):
    meansq = jnp.mean(outputs * outputs, axis=-1, keepdims=True)
    scaled = outputs / jnp.sqrt(meansq + EPSILON) * gain * jax.nn.silu(gate)
    return scaled.astype(jnp.bfloat16).reshape(outputs.shape[0], -1)


def compose_maps(later_map, earlier_map):
    return jnp.einsum("hij,hjk->hik", later_map, earlier_map, precision=HIGHEST_PRECISION)


def on_device(
    query_rows,
    key_rows,
    value_rows,
    gate_rows,
    log_decay,
    write_strength,
    conv_query,
    conv_key,
    conv_value,
    norm_gain,
):
    device_query, local_key, local_value, local_gate, local_decay, local_strength = (
        lax.all_to_all(query_rows, "head", split_axis=1, concat_axis=0, tiled=True),
        lax.all_to_all(key_rows, "head", split_axis=1, concat_axis=0, tiled=True),
        lax.all_to_all(value_rows, "head", split_axis=1, concat_axis=0, tiled=True),
        lax.all_to_all(gate_rows, "head", split_axis=1, concat_axis=0, tiled=True),
        lax.all_to_all(log_decay, "head", split_axis=1, concat_axis=0, tiled=True),
        lax.all_to_all(write_strength, "head", split_axis=1, concat_axis=0, tiled=True),
    )
    joined = jnp.concatenate([device_query, local_key, local_value], axis=1)
    kernel_width = conv_query.shape[0]
    count_rows = joined.shape[0]
    tail_rows = passed_along(joined[count_rows - (kernel_width - 1) :], "ctx", 1)
    weights_all = jnp.concatenate([conv_query, conv_key, conv_value], axis=1).astype(jnp.float32)
    mixed = causal_conv(joined.astype(jnp.float32), tail_rows.astype(jnp.float32), weights_all)
    key_width = device_query.shape[1]
    head_keys = key_width // DK
    per_key = HV // HK
    query_heads = jnp.repeat(
        unit_heads(mixed[:, :key_width], head_keys) * DK ** (-0.5), per_key, axis=1
    )
    key_heads = jnp.repeat(
        unit_heads(mixed[:, key_width : 2 * key_width], head_keys), per_key, axis=1
    )
    value_heads = mixed[:, 2 * key_width :].reshape(count_rows, -1, DV)
    terms = block_terms(
        into_blocks(query_heads, BLOCK),
        into_blocks(key_heads, BLOCK),
        into_blocks(value_heads, BLOCK),
        block_scalars(local_decay, BLOCK),
        block_scalars(local_strength, BLOCK),
    )
    key_part, value_part, within, query_decay, key_decay, end_decay = terms
    heads_here = key_part.shape[1]
    identity_mat = jnp.broadcast_to(jnp.eye(DK, dtype=jnp.float32), (heads_here, DK, DK))
    trans = end_decay[..., None, None] * identity_mat - matmul(
        "nhcd,nhce->nhde", key_decay, key_part
    )
    bias = matmul("nhcd,nhce->nhde", key_decay, value_part)
    blocks_here = trans.shape[0]
    span = 1
    while span < blocks_here:
        earlier_trans = jnp.concatenate(
            [jnp.broadcast_to(identity_mat, (span,) + identity_mat.shape), trans[:-span]], axis=0
        )
        earlier_bias = jnp.concatenate([jnp.zeros_like(bias[:span]), bias[:-span]], axis=0)
        trans, bias = (
            matmul("nhij,nhjk->nhik", trans, earlier_trans),
            matmul("nhij,nhjk->nhik", trans, earlier_bias) + bias,
        )
        span *= 2
    earlier_trans = jnp.concatenate([identity_mat[None], trans[:-1]], axis=0)
    earlier_bias = jnp.concatenate([jnp.zeros_like(bias[:1]), bias[:-1]], axis=0)
    corrected = value_part - matmul("nhcd,nhde->nhce", key_part, earlier_bias)
    local_result = matmul("nhcd,nhde->nhce", query_decay, earlier_bias) + matmul(
        "nhij,nhje->nhie", within, corrected
    )
    reach = query_decay - matmul("nhij,nhjd->nhid", within, key_part)
    carry_map = matmul("nhcd,nhde->nhce", reach, earlier_trans)
    total_trans, total_bias = trans[-1], bias[-1]
    place = lax.axis_index("ctx")
    count = lax.axis_size("ctx")
    span = 1
    while 2 * span < count:
        arrived = passed_along(jnp.stack([total_trans, total_bias]), "ctx", span)
        total_trans, total_bias = (
            jnp.where(place >= span, compose_maps(total_trans, arrived[0]), total_trans),
            compose_maps(total_trans, arrived[1]) + total_bias,
        )
        span *= 2
    initial = jnp.zeros_like(total_bias)
    if count > 1:
        near = passed_along(jnp.stack([total_trans, total_bias]), "ctx", 1)
        initial = near[1]
        if span + 1 < count:
            initial = compose_maps(near[0], passed_along(total_bias, "ctx", span + 1)) + initial
    produced = local_result + matmul("nhcd,hde->nhce", carry_map, initial)
    outputs = produced.transpose(0, 2, 1, 3).reshape(count_rows, heads_here, DV)
    gate = local_gate.astype(jnp.float32).reshape(count_rows, heads_here, DV)
    normed = gated_norm(outputs, gate, norm_gain)
    return lax.all_to_all(normed, "head", split_axis=0, concat_axis=1, tiled=True)


def solution(mesh):
    in_specs = (
        P(("ctx", "head"), None),
        P(("ctx", "head"), None),
        P(("ctx", "head"), None),
        P(("ctx", "head"), None),
        P(("ctx", "head"), None),
        P(("ctx", "head"), None),
        P(None, "head"),
        P(None, "head"),
        P(None, "head"),
        P(),
    )
    out_specs = P(("ctx", "head"), None)
    return jax.shard_map(
        on_device, mesh=mesh, in_specs=in_specs, out_specs=out_specs, check_vma=False
    )
```

```python
import functools

import jax
import jax.numpy as jnp
from jax import lax
from jax.experimental import pallas as pl
from jax.experimental.pallas import tpu as pltpu
from jax.sharding import PartitionSpec as P

DK = 128
DV = 128
HK = 8
HV = 16
BLOCK = 64


HIGHEST_PRECISION = lax.Precision.HIGHEST
EPSILON = 1e-06


def passed_along(value, axis, steps):
    count = lax.axis_size(axis)
    leading, last = (max(0, -steps), min(count, count - steps))
    return lax.ppermute(value, axis, [(source, source + steps) for source in range(leading, last)])


def matmul(spec, left, right):
    return jnp.einsum(spec, left, right, precision=HIGHEST_PRECISION)


def unit_lower_inverse(strict):
    size = strict.shape[-1]
    rows_index = jnp.arange(size)[:, None]
    cols_index = jnp.arange(size)[None, :]
    inverse = jnp.broadcast_to(jnp.eye(size, dtype=strict.dtype), strict.shape)
    width = 1
    while width < size:
        pick = (
            (rows_index // (2 * width) == cols_index // (2 * width))
            & ((rows_index // width) % 2 == 1)
            & ((cols_index // width) % 2 == 0)
        )
        lower = jnp.where(pick, strict, 0.0)
        step = matmul("...ij,...jk->...ik", inverse, matmul("...ij,...jk->...ik", lower, inverse))
        inverse = inverse - lax.optimization_barrier(step)
        width *= 2
    return inverse


def forward_substitution(coupling, targets):
    return matmul("...ij,...jf->...if", unit_lower_inverse(coupling), targets)


def causal_conv(inputs, earlier_rows, weights):
    kernel_width = weights.shape[0]
    count_rows = inputs.shape[0]
    joined = jnp.concatenate([earlier_rows, inputs], axis=0)
    result = joined[kernel_width - 1 :] * weights[kernel_width - 1]
    for offset in range(1, kernel_width):
        result = (
            result
            + joined[kernel_width - 1 - offset : kernel_width - 1 - offset + count_rows]
            * weights[kernel_width - 1 - offset]
        )
    return jax.nn.silu(result)


def unit_heads(mixed, heads):
    shaped = mixed.reshape(mixed.shape[0], heads, -1)
    return shaped / jnp.sqrt(jnp.sum(shaped * shaped, axis=-1, keepdims=True) + EPSILON)


def into_blocks(array, block_len):
    count_rows, heads, inner_dim = array.shape
    return array.reshape(count_rows // block_len, block_len, heads, inner_dim).transpose(0, 2, 1, 3)


def block_scalars(array, block_len):
    count_rows, heads = array.shape
    return (
        array.astype(jnp.float32)
        .reshape(count_rows // block_len, block_len, heads)
        .transpose(0, 2, 1)
    )


def block_terms(queries, keys, values, log_gate, strength):
    block_len = queries.shape[2]
    key_dim = keys.shape[-1]
    cumulative = jnp.cumsum(log_gate, axis=-1)
    rows_index = jnp.arange(block_len)[:, None]
    cols_index = jnp.arange(block_len)[None, :]
    causal = rows_index >= cols_index
    strictly = rows_index > cols_index
    spread = jnp.where(causal, cumulative[..., :, None] - cumulative[..., None, :], 0.0)
    decays = jnp.where(causal, jnp.exp(spread), 0.0)
    key_key = jnp.einsum("nhid,nhjd->nhij", keys, keys, precision=HIGHEST_PRECISION)
    coupling = jnp.where(strictly, strength[..., None] * decays * key_key, 0.0)
    targets = jnp.concatenate(
        [(strength * jnp.exp(cumulative))[..., None] * keys, strength[..., None] * values], axis=-1
    )
    solved = forward_substitution(coupling, targets)
    key_part = solved[..., :key_dim]
    value_part = solved[..., key_dim:]
    query_key = jnp.einsum("nhid,nhjd->nhij", queries, keys, precision=HIGHEST_PRECISION)
    within = query_key * decays
    query_decay = jnp.exp(cumulative)[..., None] * queries
    closing_logarithm = cumulative[..., -1:]
    key_decay = jnp.exp(closing_logarithm - cumulative)[..., None] * keys
    end_decay = jnp.exp(closing_logarithm[..., 0])
    return (key_part, value_part, within, query_decay, key_decay, end_decay)


def block_apply(memory, pieces):
    key_part, value_part, within, query_decay, key_decay, end_decay = pieces
    corrected = value_part - jnp.einsum(
        "hcd,hde->hce", key_part, memory, precision=HIGHEST_PRECISION
    )
    result = jnp.einsum("hcd,hde->hce", query_decay, memory, precision=HIGHEST_PRECISION)
    result = result + jnp.einsum("hij,hje->hie", within, corrected, precision=HIGHEST_PRECISION)
    memory = end_decay[:, None, None] * memory + jnp.einsum(
        "hcd,hce->hde", key_decay, corrected, precision=HIGHEST_PRECISION
    )
    return (memory, result)


def gated_norm(outputs, gate, gain):
    meansq = jnp.mean(outputs * outputs, axis=-1, keepdims=True)
    scaled = outputs / jnp.sqrt(meansq + EPSILON) * gain * jax.nn.silu(gate)
    return scaled.astype(jnp.bfloat16).reshape(outputs.shape[0], -1)


def compose_maps(later_map, earlier_map):
    return jnp.einsum("hij,hjk->hik", later_map, earlier_map, precision=HIGHEST_PRECISION)


MESH_IDS = pl.DeviceIdType.MESH


def scan_spans(count):
    spans = []
    span = 1
    while 2 * span < count:
        spans.append(span)
        span *= 2
    return spans, span + 1


def kernel_dot(left, right):
    return jnp.dot(left, right, preferred_element_type=jnp.float32, precision=HIGHEST_PRECISION)


def ctx_scan_kernel(count, maps_ref, out_ref, current, slots, near_slot, far_slot, send_sems, recv_sems):
    place = lax.axis_index("ctx")
    group = lax.axis_index("head")
    heads = maps_ref.shape[1]
    spans, far = scan_spans(count)
    offsets = sorted(set(spans + [1] + ([far] if far < count else [])))
    barrier = pltpu.get_barrier_semaphore()
    partners = jnp.int32(0)
    for offset in offsets:
        for target in (place + offset, place - offset):
            valid = jnp.logical_and(target >= 0, target < count)

            @pl.when(valid)
            def _():
                pl.semaphore_signal(barrier, inc=1, device_id=(target, group), device_id_type=MESH_IDS)

            partners = partners + valid.astype(jnp.int32)
    pl.semaphore_wait(barrier, partners)

    source = maps_ref
    for index, span in enumerate(spans):
        sending = place + span < count
        receiving = place >= span
        copy_out = pltpu.make_async_remote_copy(
            src_ref=source,
            dst_ref=slots.at[index],
            send_sem=send_sems.at[index],
            recv_sem=recv_sems.at[index],
            device_id=(place + span, group),
            device_id_type=MESH_IDS,
        )
        pl.when(sending)(copy_out.start)
        pl.when(receiving)(copy_out.wait_recv)
        dest = current.at[index % 2]

        def composed(source=source, dest=dest, index=index):
            for head in range(heads):
                trans_here = source[0, head]
                dest[0, head] = kernel_dot(trans_here, slots[index, 0, head])
                dest[1, head] = kernel_dot(trans_here, slots[index, 1, head]) + source[1, head]

        def kept(source=source, dest=dest):
            dest[...] = source[...]

        pl.when(receiving)(composed)
        pl.when(jnp.logical_not(receiving))(kept)
        pl.when(sending)(copy_out.wait_send)
        source = dest

    last = len(spans)
    near_copy = pltpu.make_async_remote_copy(
        src_ref=source,
        dst_ref=near_slot,
        send_sem=send_sems.at[last],
        recv_sem=recv_sems.at[last],
        device_id=(place + 1, group),
        device_id_type=MESH_IDS,
    )
    pl.when(place + 1 < count)(near_copy.start)
    if far < count:
        far_copy = pltpu.make_async_remote_copy(
            src_ref=source.at[1],
            dst_ref=far_slot,
            send_sem=send_sems.at[last + 1],
            recv_sem=recv_sems.at[last + 1],
            device_id=(place + far, group),
            device_id_type=MESH_IDS,
        )
        pl.when(place + far < count)(far_copy.start)
    pl.when(place >= 1)(near_copy.wait_recv)
    out_ref[...] = jnp.zeros_like(out_ref)

    def from_near():
        out_ref[...] = near_slot[1]

    pl.when(place >= 1)(from_near)
    if far < count:
        pl.when(place >= far)(far_copy.wait_recv)

        def from_far():
            for head in range(heads):
                out_ref[head] = out_ref[head] + kernel_dot(near_slot[0, head], far_slot[head])

        pl.when(place >= far)(from_far)
        pl.when(place + far < count)(far_copy.wait_send)
    pl.when(place + 1 < count)(near_copy.wait_send)


def ctx_scan(maps):
    count = lax.axis_size("ctx")
    if count == 1:
        return jnp.zeros_like(maps[1])
    spans, far = scan_spans(count)
    side = maps.shape[1:]
    return pl.pallas_call(
        functools.partial(ctx_scan_kernel, count),
        out_shape=jax.ShapeDtypeStruct(side, jnp.float32),
        in_specs=[pl.BlockSpec(memory_space=pltpu.VMEM)],
        out_specs=pl.BlockSpec(memory_space=pltpu.VMEM),
        scratch_shapes=[
            pltpu.VMEM((2,) + maps.shape, jnp.float32),
            pltpu.VMEM((max(len(spans), 1),) + maps.shape, jnp.float32),
            pltpu.VMEM(maps.shape, jnp.float32),
            pltpu.VMEM(side, jnp.float32),
            pltpu.SemaphoreType.DMA((len(spans) + 2,)),
            pltpu.SemaphoreType.DMA((len(spans) + 2,)),
        ],
        compiler_params=pltpu.CompilerParams(collective_id=0, has_side_effects=True),
    )(maps)


def on_device(
    query_rows,
    key_rows,
    value_rows,
    gate_rows,
    log_decay,
    write_strength,
    conv_query,
    conv_key,
    conv_value,
    norm_gain,
):
    parts = lax.axis_size("head")
    pieces = (query_rows, key_rows, value_rows, log_decay, write_strength)
    widths = [piece.shape[1] // parts for piece in pieces]
    packed = jnp.concatenate(
        [piece.reshape(piece.shape[0], parts, -1) for piece in pieces], axis=2
    )
    moved = lax.all_to_all(packed, "head", split_axis=1, concat_axis=0, tiled=True)
    moved = moved.reshape(moved.shape[0], -1)
    offsets = [sum(widths[:index]) for index in range(len(widths) + 1)]
    device_query, local_key, local_value, local_decay, local_strength = (
        moved[:, offsets[index] : offsets[index + 1]] for index in range(len(widths))
    )
    local_gate = lax.all_to_all(gate_rows, "head", split_axis=1, concat_axis=0, tiled=True)
    joined = jnp.concatenate([earlier_rows, inputs], axis=0)
    result = joined[kernel_width - 1 :] * weights[kernel_width - 1]
    for offset in range(1, kernel_width):
        result = (
            result
            + joined[kernel_width - 1 - offset : kernel_width - 1 - offset + count_rows]
            * weights[kernel_width - 1 - offset]
        )
    return jax.nn.silu(result)


def unit_heads(mixed, heads):
    shaped = mixed.reshape(mixed.shape[0], heads, -1)
    return shaped / jnp.sqrt(jnp.sum(shaped * shaped, axis=-1, keepdims=True) + EPSILON)


def into_blocks(array, block_len):
    count_rows, heads, inner_dim = array.shape
    return array.reshape(count_rows // block_len, block_len, heads, inner_dim).transpose(0, 2, 1, 3)


def block_scalars(array, block_len):
    count_rows, heads = array.shape
    return (
        array.astype(jnp.float32)
        .reshape(count_rows // block_len, block_len, heads)
        .transpose(0, 2, 1)
    )


def block_terms(queries, keys, values, log_gate, strength):
    block_len = queries.shape[2]
    key_dim = keys.shape[-1]
    cumulative = jnp.cumsum(log_gate, axis=-1)
    rows_index = jnp.arange(block_len)[:, None]
    cols_index = jnp.arange(block_len)[None, :]
    causal = rows_index >= cols_index
    strictly = rows_index > cols_index
    spread = jnp.where(causal, cumulative[..., :, None] - cumulative[..., None, :], 0.0)
    decays = jnp.where(causal, jnp.exp(spread), 0.0)
    key_key = jnp.einsum("nhid,nhjd->nhij", keys, keys, precision=HIGHEST_PRECISION)
    coupling = jnp.where(strictly, strength[..., None] * decays * key_key, 0.0)
    targets = jnp.concatenate(
        [(strength * jnp.exp(cumulative))[..., None] * keys, strength[..., None] * values], axis=-1
    )
    solved = forward_substitution(coupling, targets)
    key_part = solved[..., :key_dim]
    value_part = solved[..., key_dim:]
    query_key = jnp.einsum("nhid,nhjd->nhij", queries, keys, precision=HIGHEST_PRECISION)
    within = query_key * decays
    query_decay = jnp.exp(cumulative)[..., None] * queries
    closing_logarithm = cumulative[..., -1:]
    key_decay = jnp.exp(closing_logarithm - cumulative)[..., None] * keys
    end_decay = jnp.exp(closing_logarithm[..., 0])
    return (key_part, value_part, within, query_decay, key_decay, end_decay)


def block_apply(memory, pieces):
    key_part, value_part, within, query_decay, key_decay, end_decay = pieces
    corrected = value_part - jnp.einsum(
        "hcd,hde->hce", key_part, memory, precision=HIGHEST_PRECISION
    )
    result = jnp.einsum("hcd,hde->hce", query_decay, memory, precision=HIGHEST_PRECISION)
    result = result + jnp.einsum("hij,hje->hie", within, corrected, precision=HIGHEST_PRECISION)
    memory = end_decay[:, None, None] * memory + jnp.einsum(
        "hcd,hce->hde", key_decay, corrected, precision=HIGHEST_PRECISION
    )
    return (memory, result)


def gated_norm(outputs, gate, gain):
    meansq = jnp.mean(outputs * outputs, axis=-1, keepdims=True)
    scaled = outputs / jnp.sqrt(meansq + EPSILON) * gain * jax.nn.silu(gate)
    return scaled.astype(jnp.bfloat16).reshape(outputs.shape[0], -1)


def compose_maps(later_map, earlier_map):
    return jnp.einsum("hij,hjk->hik", later_map, earlier_map, precision=HIGHEST_PRECISION)


MESH_IDS = pl.DeviceIdType.MESH


def scan_spans(count):
    spans = []
    span = 1
    while 2 * span < count:
        spans.append(span)
        span *= 2
    return spans, span + 1


def kernel_dot(left, right):
    return jnp.dot(left, right, preferred_element_type=jnp.float32, precision=HIGHEST_PRECISION)


def ctx_scan_kernel(count, maps_ref, out_ref, current, slots, near_slot, far_slot, send_sems, recv_sems):
    place = lax.axis_index("ctx")
    group = lax.axis_index("head")
    heads = maps_ref.shape[1]
    spans, far = scan_spans(count)
    offsets = sorted(set(spans + [1] + ([far] if far < count else [])))
    barrier = pltpu.get_barrier_semaphore()
    partners = jnp.int32(0)
    for offset in offsets:
        for target in (place + offset, place - offset):
            valid = jnp.logical_and(target >= 0, target < count)

            @pl.when(valid)
            def _():
                pl.semaphore_signal(barrier, inc=1, device_id=(target, group), device_id_type=MESH_IDS)

            partners = partners + valid.astype(jnp.int32)
    pl.semaphore_wait(barrier, partners)

    source = maps_ref
    for index, span in enumerate(spans):
        sending = place + span < count
        receiving = place >= span
        copy_out = pltpu.make_async_remote_copy(
            src_ref=source,
            dst_ref=slots.at[index],
            send_sem=send_sems.at[index],
            recv_sem=recv_sems.at[index],
            device_id=(place + span, group),
            device_id_type=MESH_IDS,
        )
        pl.when(sending)(copy_out.start)
        pl.when(receiving)(copy_out.wait_recv)
        dest = current.at[index % 2]

        def composed(source=source, dest=dest, index=index):
            for head in range(heads):
                trans_here = source[0, head]
                dest[0, head] = kernel_dot(trans_here, slots[index, 0, head])
                dest[1, head] = kernel_dot(trans_here, slots[index, 1, head]) + source[1, head]

        def kept(source=source, dest=dest):
            dest[...] = source[...]

        pl.when(receiving)(composed)
        pl.when(jnp.logical_not(receiving))(kept)
        pl.when(sending)(copy_out.wait_send)
        source = dest

    last = len(spans)
    near_copy = pltpu.make_async_remote_copy(
        src_ref=source,
        dst_ref=near_slot,
        send_sem=send_sems.at[last],
        recv_sem=recv_sems.at[last],
        device_id=(place + 1, group),
        device_id_type=MESH_IDS,
    )
    pl.when(place + 1 < count)(near_copy.start)
    if far < count:
        far_copy = pltpu.make_async_remote_copy(
            src_ref=source.at[1],
            dst_ref=far_slot,
            send_sem=send_sems.at[last + 1],
            recv_sem=recv_sems.at[last + 1],
            device_id=(place + far, group),
            device_id_type=MESH_IDS,
        )
        pl.when(place + far < count)(far_copy.start)
    pl.when(place >= 1)(near_copy.wait_recv)
    out_ref[...] = jnp.zeros_like(out_ref)

    def from_near():
        out_ref[...] = near_slot[1]

    pl.when(place >= 1)(from_near)
    if far < count:
        pl.when(place >= far)(far_copy.wait_recv)

        def from_far():
            for head in range(heads):
                out_ref[head] = out_ref[head] + kernel_dot(near_slot[0, head], far_slot[head])

        pl.when(place >= far)(from_far)
        pl.when(place + far < count)(far_copy.wait_send)
    pl.when(place + 1 < count)(near_copy.wait_send)


def ctx_scan(maps):
    count = lax.axis_size("ctx")
    if count == 1:
        return jnp.zeros_like(maps[1])
    spans, far = scan_spans(count)
    side = maps.shape[1:]
    return pl.pallas_call(
        functools.partial(ctx_scan_kernel, count),
        out_shape=jax.ShapeDtypeStruct(side, jnp.float32),
        in_specs=[pl.BlockSpec(memory_space=pltpu.VMEM)],
        out_specs=pl.BlockSpec(memory_space=pltpu.VMEM),
        scratch_shapes=[
            pltpu.VMEM((2,) + maps.shape, jnp.float32),
            pltpu.VMEM((max(len(spans), 1),) + maps.shape, jnp.float32),
            pltpu.VMEM(maps.shape, jnp.float32),
            pltpu.VMEM(side, jnp.float32),
            pltpu.SemaphoreType.DMA((len(spans) + 2,)),
            pltpu.SemaphoreType.DMA((len(spans) + 2,)),
        ],
        compiler_params=pltpu.CompilerParams(collective_id=0, has_side_effects=True),
    )(maps)


def on_device(
    query_rows,
    key_rows,
    value_rows,
    gate_rows,
    log_decay,
    write_strength,
    conv_query,
    conv_key,
    conv_value,
    norm_gain,
):
    device_query, local_key, local_value, local_gate, local_decay, local_strength = (
        lax.all_to_all(query_rows, "head", split_axis=1, concat_axis=0, tiled=True),
        lax.all_to_all(key_rows, "head", split_axis=1, concat_axis=0, tiled=True),
        lax.all_to_all(value_rows, "head", split_axis=1, concat_axis=0, tiled=True),
        lax.all_to_all(gate_rows, "head", split_axis=1, concat_axis=0, tiled=True),
        lax.all_to_all(log_decay, "head", split_axis=1, concat_axis=0, tiled=True),
        lax.all_to_all(write_strength, "head", split_axis=1, concat_axis=0, tiled=True),
    )
    joined = jnp.concatenate([device_query, local_key, local_value], axis=1)
    kernel_width = conv_query.shape[0]
    count_rows = joined.shape[0]
    tail_rows = passed_along(joined[count_rows - (kernel_width - 1) :], "ctx", 1)
    weights_all = jnp.concatenate([conv_query, conv_key, conv_value], axis=1).astype(jnp.float32)
    mixed = causal_conv(joined.astype(jnp.float32), tail_rows.astype(jnp.float32), weights_all)
    key_width = device_query.shape[1]
    head_keys = key_width // DK
    per_key = HV // HK
    query_heads = jnp.repeat(
        unit_heads(mixed[:, :key_width], head_keys) * DK ** (-0.5), per_key, axis=1
    )
    key_heads = jnp.repeat(
        unit_heads(mixed[:, key_width : 2 * key_width], head_keys), per_key, axis=1
    )
    value_heads = mixed[:, 2 * key_width :].reshape(count_rows, -1, DV)
    terms = block_terms(
        into_blocks(query_heads, BLOCK),
        into_blocks(key_heads, BLOCK),
        into_blocks(value_heads, BLOCK),
        block_scalars(local_decay, BLOCK),
        block_scalars(local_strength, BLOCK),
    )
    key_part, value_part, within, query_decay, key_decay, end_decay = terms
    heads_here = key_part.shape[1]
    identity_mat = jnp.broadcast_to(jnp.eye(DK, dtype=jnp.float32), (heads_here, DK, DK))
    trans = end_decay[..., None, None] * identity_mat - matmul(
        "nhcd,nhce->nhde", key_decay, key_part
    )
    bias = matmul("nhcd,nhce->nhde", key_decay, value_part)
    blocks_here = trans.shape[0]
    span = 1
    while span < blocks_here:
        earlier_trans = jnp.concatenate(
            [jnp.broadcast_to(identity_mat, (span,) + identity_mat.shape), trans[:-span]], axis=0
        )
        earlier_bias = jnp.concatenate([jnp.zeros_like(bias[:span]), bias[:-span]], axis=0)
        trans, bias = (
            matmul("nhij,nhjk->nhik", trans, earlier_trans),
            matmul("nhij,nhjk->nhik", trans, earlier_bias) + bias,
        )
        span *= 2
    earlier_trans = jnp.concatenate([identity_mat[None], trans[:-1]], axis=0)
    earlier_bias = jnp.concatenate([jnp.zeros_like(bias[:1]), bias[:-1]], axis=0)
    corrected = value_part - matmul("nhcd,nhde->nhce", key_part, earlier_bias)
    local_result = matmul("nhcd,nhde->nhce", query_decay, earlier_bias) + matmul(
        "nhij,nhje->nhie", within, corrected
    )
    reach = query_decay - matmul("nhij,nhjd->nhid", within, key_part)
    carry_map = matmul("nhcd,nhde->nhce", reach, earlier_trans)
    total_trans, total_bias = trans[-1], bias[-1]
    initial = ctx_scan(jnp.stack([total_trans, total_bias]))
    produced = local_result + matmul("nhcd,hde->nhce", carry_map, initial)
    outputs = produced.transpose(0, 2, 1, 3).reshape(count_rows, heads_here, DV)
    gate = local_gate.astype(jnp.float32).reshape(count_rows, heads_here, DV)
    normed = gated_norm(outputs, gate, norm_gain)
    return lax.all_to_all(normed, "head", split_axis=0, concat_axis=1, tiled=True)


def solution(mesh):
    in_specs = (
        P(("ctx", "head"), None),
        P(("ctx", "head"), None),
        P(("ctx", "head"), None),
        P(("ctx", "head"), None),
        P(("ctx", "head"), None),
        P(("ctx", "head"), None),
        P(None, "head"),
        P(None, "head"),
        P(None, "head"),
        P(),
    )
    out_specs = P(("ctx", "head"), None)
    return jax.shard_map(
        on_device, mesh=mesh, in_specs=in_specs, out_specs=out_specs, check_vma=False
    )
```

```python
import functools

import jax
import jax.numpy as jnp
from jax import lax
from jax.experimental import pallas as pl
from jax.experimental.pallas import tpu as pltpu
from jax.sharding import PartitionSpec as P

DK = 128
DV = 128
HK = 8
HV = 16
BLOCK = 64


HIGHEST_PRECISION = lax.Precision.HIGHEST
EPSILON = 1e-06


def passed_along(value, axis, steps):
    count = lax.axis_size(axis)
    leading, last = (max(0, -steps), min(count, count - steps))
    return lax.ppermute(value, axis, [(source, source + steps) for source in range(leading, last)])


def matmul(spec, left, right):
    return jnp.einsum(spec, left, right, precision=HIGHEST_PRECISION)


def unit_lower_inverse(strict):
    size = strict.shape[-1]
    rows_index = jnp.arange(size)[:, None]
    cols_index = jnp.arange(size)[None, :]
    inverse = jnp.broadcast_to(jnp.eye(size, dtype=strict.dtype), strict.shape)
    width = 1
    while width < size:
        pick = (
            (rows_index // (2 * width) == cols_index // (2 * width))
            & ((rows_index // width) % 2 == 1)
            & ((cols_index // width) % 2 == 0)
        )
        lower = jnp.where(pick, strict, 0.0)
        step = matmul("...ij,...jk->...ik", inverse, matmul("...ij,...jk->...ik", lower, inverse))
        inverse = inverse - lax.optimization_barrier(step)
        width *= 2
    return inverse


def forward_substitution(coupling, targets):
    return matmul("...ij,...jf->...if", unit_lower_inverse(coupling), targets)


def causal_conv(inputs, earlier_rows, weights):
    kernel_width = weights.shape[0]
    count_rows = inputs.shape[0]
    joined = jnp.concatenate([earlier_rows, inputs], axis=0)
    result = joined[kernel_width - 1 :] * weights[kernel_width - 1]
    for offset in range(1, kernel_width):
        result = (
            result
            + joined[kernel_width - 1 - offset : kernel_width - 1 - offset + count_rows]
            * weights[kernel_width - 1 - offset]
        )
    return jax.nn.silu(result)


def unit_heads(mixed, heads):
    shaped = mixed.reshape(mixed.shape[0], heads, -1)
    return shaped / jnp.sqrt(jnp.sum(shaped * shaped, axis=-1, keepdims=True) + EPSILON)


def into_blocks(array, block_len):
    count_rows, heads, inner_dim = array.shape
    return array.reshape(count_rows // block_len, block_len, heads, inner_dim).transpose(0, 2, 1, 3)


def block_scalars(array, block_len):
    count_rows, heads = array.shape
    return (
        array.astype(jnp.float32)
        .reshape(count_rows // block_len, block_len, heads)
        .transpose(0, 2, 1)
    )


def block_terms(queries, keys, values, log_gate, strength):
    block_len = queries.shape[2]
    key_dim = keys.shape[-1]
    cumulative = jnp.cumsum(log_gate, axis=-1)
    rows_index = jnp.arange(block_len)[:, None]
    cols_index = jnp.arange(block_len)[None, :]
    causal = rows_index >= cols_index
    strictly = rows_index > cols_index
    spread = jnp.where(causal, cumulative[..., :, None] - cumulative[..., None, :], 0.0)
    decays = jnp.where(causal, jnp.exp(spread), 0.0)
    key_key = jnp.einsum("nhid,nhjd->nhij", keys, keys, precision=HIGHEST_PRECISION)
    coupling = jnp.where(strictly, strength[..., None] * decays * key_key, 0.0)
    targets = jnp.concatenate(
        [(strength * jnp.exp(cumulative))[..., None] * keys, strength[..., None] * values], axis=-1
    )
    solved = forward_substitution(coupling, targets)
    key_part = solved[..., :key_dim]
    value_part = solved[..., key_dim:]
    query_key = jnp.einsum("nhid,nhjd->nhij", queries, keys, precision=HIGHEST_PRECISION)
    within = query_key * decays
    query_decay = jnp.exp(cumulative)[..., None] * queries
    closing_logarithm = cumulative[..., -1:]
    key_decay = jnp.exp(closing_logarithm - cumulative)[..., None] * keys
    end_decay = jnp.exp(closing_logarithm[..., 0])
    return (key_part, value_part, within, query_decay, key_decay, end_decay)


def block_apply(memory, pieces):
    key_part, value_part, within, query_decay, key_decay, end_decay = pieces
    corrected = value_part - jnp.einsum(
        "hcd,hde->hce", key_part, memory, precision=HIGHEST_PRECISION
    )
    result = jnp.einsum("hcd,hde->hce", query_decay, memory, precision=HIGHEST_PRECISION)
    result = result + jnp.einsum("hij,hje->hie", within, corrected, precision=HIGHEST_PRECISION)
    memory = end_decay[:, None, None] * memory + jnp.einsum(
        "hcd,hce->hde", key_decay, corrected, precision=HIGHEST_PRECISION
    )
    return (memory, result)


def gated_norm(outputs, gate, gain):
    meansq = jnp.mean(outputs * outputs, axis=-1, keepdims=True)
    scaled = outputs / jnp.sqrt(meansq + EPSILON) * gain * jax.nn.silu(gate)
    return scaled.astype(jnp.bfloat16).reshape(outputs.shape[0], -1)


def compose_maps(later_map, earlier_map):
    return jnp.einsum("hij,hjk->hik", later_map, earlier_map, precision=HIGHEST_PRECISION)


MESH_IDS = pl.DeviceIdType.MESH


def scan_spans(count):
    spans = []
    span = 1
    while 2 * span < count:
        spans.append(span)
        span *= 2
    return spans, span + 1


def kernel_dot(left, right):
    return jnp.dot(left, right, preferred_element_type=jnp.float32, precision=HIGHEST_PRECISION)


def ctx_scan_kernel(count, maps_ref, out_ref, current, slots, near_slot, far_slot, send_sems, recv_sems):
    place = lax.axis_index("ctx")
    group = lax.axis_index("head")
    heads = maps_ref.shape[1]
    spans, far = scan_spans(count)
    offsets = sorted(set(spans + [1] + ([far] if far < count else [])))
    barrier = pltpu.get_barrier_semaphore()
    partners = jnp.int32(0)
    for offset in offsets:
        for target in (place + offset, place - offset):
            valid = jnp.logical_and(target >= 0, target < count)

            @pl.when(valid)
            def _():
                pl.semaphore_signal(barrier, inc=1, device_id=(target, group), device_id_type=MESH_IDS)

            partners = partners + valid.astype(jnp.int32)
    pl.semaphore_wait(barrier, partners)

    source = maps_ref
    for index, span in enumerate(spans):
        sending = place + span < count
        receiving = place >= span
        copy_out = pltpu.make_async_remote_copy(
            src_ref=source,
            dst_ref=slots.at[index],
            send_sem=send_sems.at[index],
            recv_sem=recv_sems.at[index],
            device_id=(place + span, group),
            device_id_type=MESH_IDS,
        )
        pl.when(sending)(copy_out.start)
        pl.when(receiving)(copy_out.wait_recv)
        dest = current.at[index % 2]

        def composed(source=source, dest=dest, index=index):
            for head in range(heads):
                trans_here = source[0, head]
                dest[0, head] = kernel_dot(trans_here, slots[index, 0, head])
                dest[1, head] = kernel_dot(trans_here, slots[index, 1, head]) + source[1, head]

        def kept(source=source, dest=dest):
            dest[...] = source[...]

        pl.when(receiving)(composed)
        pl.when(jnp.logical_not(receiving))(kept)
        pl.when(sending)(copy_out.wait_send)
        source = dest

    last = len(spans)
    near_copy = pltpu.make_async_remote_copy(
        src_ref=source,
        dst_ref=near_slot,
        send_sem=send_sems.at[last],
        recv_sem=recv_sems.at[last],
        device_id=(place + 1, group),
        device_id_type=MESH_IDS,
    )
    pl.when(place + 1 < count)(near_copy.start)
    if far < count:
        far_copy = pltpu.make_async_remote_copy(
            src_ref=source.at[1],
            dst_ref=far_slot,
            send_sem=send_sems.at[last + 1],
            recv_sem=recv_sems.at[last + 1],
            device_id=(place + far, group),
            device_id_type=MESH_IDS,
        )
        pl.when(place + far < count)(far_copy.start)
    pl.when(place >= 1)(near_copy.wait_recv)
    out_ref[...] = jnp.zeros_like(out_ref)

    def from_near():
        out_ref[...] = near_slot[1]

    pl.when(place >= 1)(from_near)
    if far < count:
        pl.when(place >= far)(far_copy.wait_recv)

        def from_far():
            for head in range(heads):
                out_ref[head] = out_ref[head] + kernel_dot(near_slot[0, head], far_slot[head])

        pl.when(place >= far)(from_far)
        pl.when(place + far < count)(far_copy.wait_send)
    pl.when(place + 1 < count)(near_copy.wait_send)


def ctx_scan(maps):
    count = lax.axis_size("ctx")
    if count == 1:
        return jnp.zeros_like(maps[1])
    spans, far = scan_spans(count)
    side = maps.shape[1:]
    return pl.pallas_call(
        functools.partial(ctx_scan_kernel, count),
        out_shape=jax.ShapeDtypeStruct(side, jnp.float32),
        in_specs=[pl.BlockSpec(memory_space=pltpu.VMEM)],
        out_specs=pl.BlockSpec(memory_space=pltpu.VMEM),
        scratch_shapes=[
            pltpu.VMEM((2,) + maps.shape, jnp.float32),
            pltpu.VMEM((max(len(spans), 1),) + maps.shape, jnp.float32),
            pltpu.VMEM(maps.shape, jnp.float32),
            pltpu.VMEM(side, jnp.float32),
            pltpu.SemaphoreType.DMA((len(spans) + 2,)),
            pltpu.SemaphoreType.DMA((len(spans) + 2,)),
        ],
        compiler_params=pltpu.CompilerParams(collective_id=0, has_side_effects=True),
    )(maps)


def head_exchange_kernel(parts, count, source_view, target_view, *refs):
    sources, targets = refs[:count], refs[count : 2 * count]
    send_sems, recv_sems = refs[2 * count], refs[2 * count + 1]
    me = lax.axis_index("head")
    line = lax.axis_index("ctx")
    barrier = pltpu.get_barrier_semaphore()
    for peer in range(parts):

        @pl.when(me != peer)
        def _():
            pl.semaphore_signal(barrier, inc=1, device_id=(line, peer), device_id_type=MESH_IDS)

    pl.semaphore_wait(barrier, parts - 1)
    outgoing, incoming, local = [], [], []
    for index in range(count):
        for peer in range(parts):
            away = peer != me
            sending = pltpu.make_async_remote_copy(
                src_ref=source_view(sources[index], peer),
                dst_ref=target_view(targets[index], me),
                send_sem=send_sems.at[index, peer],
                recv_sem=recv_sems.at[index, me],
                device_id=(line, peer),
                device_id_type=MESH_IDS,
            )
            pl.when(away)(sending.start)
            staying = pltpu.make_async_copy(
                source_view(sources[index], peer),
                target_view(targets[index], peer),
                send_sems.at[index, peer],
            )
            pl.when(jnp.logical_not(away))(staying.start)
            arriving = pltpu.make_async_remote_copy(
                src_ref=source_view(sources[index], peer),
                dst_ref=target_view(targets[index], peer),
                send_sem=send_sems.at[index, peer],
                recv_sem=recv_sems.at[index, peer],
                device_id=(line, peer),
                device_id_type=MESH_IDS,
            )
            outgoing.append((away, sending))
            incoming.append((away, arriving))
            local.append((away, staying))
    for (away, sending), (_, arriving), (_, staying) in zip(outgoing, incoming, local):
        pl.when(away)(sending.wait_send)
        pl.when(away)(arriving.wait_recv)
        pl.when(jnp.logical_not(away))(staying.wait)


def head_exchange(arrays, target_shapes, source_view, target_view, collective):
    parts = lax.axis_size("head")
    count = len(arrays)
    return pl.pallas_call(
        functools.partial(head_exchange_kernel, parts, count, source_view, target_view),
        out_shape=[jax.ShapeDtypeStruct(shape, array.dtype) for shape, array in zip(target_shapes, arrays)],
        in_specs=[pl.BlockSpec(memory_space=pl.ANY)] * count,
        out_specs=[pl.BlockSpec(memory_space=pl.ANY)] * count,
        scratch_shapes=[
            pltpu.SemaphoreType.DMA((count, parts)),
            pltpu.SemaphoreType.DMA((count, parts)),
        ],
        compiler_params=pltpu.CompilerParams(collective_id=collective, has_side_effects=True),
    )(*arrays)


def columns_of(ref, peer):
    if len(ref.shape) == 3:
        return ref.at[peer]
    width = ref.shape[1] // lax.axis_size("head")
    return ref.at[:, pl.ds(peer * width, width)]


def rows_of(ref, peer):
    if len(ref.shape) == 3:
        return ref.at[peer]
    height = ref.shape[0] // lax.axis_size("head")
    return ref.at[pl.ds(peer * height, height), :]


def spread_heads(arrays):
    parts = lax.axis_size("head")
    shapes = [
        array.shape if array.ndim == 3 else (parts * array.shape[0], array.shape[1] // parts)
        for array in arrays
    ]
    return head_exchange(arrays, shapes, columns_of, rows_of, 1)


def gather_heads(array):
    parts = lax.axis_size("head")
    shape = (array.shape[0] // parts, array.shape[1] * parts)
    return head_exchange([array], [shape], rows_of, columns_of, 2)[0]


def on_device(
    query_rows,
    key_rows,
    value_rows,
    gate_rows,
    log_decay,
    write_strength,
    conv_query,
    conv_key,
    conv_value,
    norm_gain,
):
    parts = lax.axis_size("head")
    scalars = jnp.concatenate(
        [
            log_decay.reshape(log_decay.shape[0], parts, -1),
            write_strength.reshape(write_strength.shape[0], parts, -1),
        ],
        axis=2,
    ).transpose(1, 0, 2)
    device_query, local_key, local_value, moved_scalars = spread_heads(
        [query_rows, key_rows, value_rows, scalars]
    )
    moved_scalars = moved_scalars.reshape(-1, moved_scalars.shape[-1])
    split_at = log_decay.shape[1] // parts
    local_decay, local_strength = moved_scalars[:, :split_at], moved_scalars[:, split_at:]
    local_gate = lax.all_to_all(gate_rows, "head", split_axis=1, concat_axis=0, tiled=True)
    joined = jnp.concatenate([device_query, local_key, local_value], axis=1)
    kernel_width = conv_query.shape[0]
    count_rows = joined.shape[0]
    tail_rows = passed_along(joined[count_rows - (kernel_width - 1) :], "ctx", 1)
    weights_all = jnp.concatenate([conv_query, conv_key, conv_value], axis=1).astype(jnp.float32)
    mixed = causal_conv(joined.astype(jnp.float32), tail_rows.astype(jnp.float32), weights_all)
    key_width = device_query.shape[1]
    head_keys = key_width // DK
    per_key = HV // HK
    query_heads = jnp.repeat(
        unit_heads(mixed[:, :key_width], head_keys) * DK ** (-0.5), per_key, axis=1
    )
    key_heads = jnp.repeat(
        unit_heads(mixed[:, key_width : 2 * key_width], head_keys), per_key, axis=1
    )
    value_heads = mixed[:, 2 * key_width :].reshape(count_rows, -1, DV)
    terms = block_terms(
        into_blocks(query_heads, BLOCK),
        into_blocks(key_heads, BLOCK),
        into_blocks(value_heads, BLOCK),
        block_scalars(local_decay, BLOCK),
        block_scalars(local_strength, BLOCK),
    )
    key_part, value_part, within, query_decay, key_decay, end_decay = terms
    heads_here = key_part.shape[1]
    identity_mat = jnp.broadcast_to(jnp.eye(DK, dtype=jnp.float32), (heads_here, DK, DK))
    trans = end_decay[..., None, None] * identity_mat - matmul(
        "nhcd,nhce->nhde", key_decay, key_part
    )
    bias = matmul("nhcd,nhce->nhde", key_decay, value_part)
    blocks_here = trans.shape[0]
    span = 1
    while span < blocks_here:
        earlier_trans = jnp.concatenate(
            [jnp.broadcast_to(identity_mat, (span,) + identity_mat.shape), trans[:-span]], axis=0
        )
        earlier_bias = jnp.concatenate([jnp.zeros_like(bias[:span]), bias[:-span]], axis=0)
        trans, bias = (
            matmul("nhij,nhjk->nhik", trans, earlier_trans),
            matmul("nhij,nhjk->nhik", trans, earlier_bias) + bias,
        )
        span *= 2
    earlier_trans = jnp.concatenate([identity_mat[None], trans[:-1]], axis=0)
    earlier_bias = jnp.concatenate([jnp.zeros_like(bias[:1]), bias[:-1]], axis=0)
    corrected = value_part - matmul("nhcd,nhde->nhce", key_part, earlier_bias)
    local_result = matmul("nhcd,nhde->nhce", query_decay, earlier_bias) + matmul(
        "nhij,nhje->nhie", within, corrected
    )
    reach = query_decay - matmul("nhij,nhjd->nhid", within, key_part)
    carry_map = matmul("nhcd,nhde->nhce", reach, earlier_trans)
    total_trans, total_bias = trans[-1], bias[-1]
    initial = ctx_scan(jnp.stack([total_trans, total_bias]))
    produced = local_result + matmul("nhcd,hde->nhce", carry_map, initial)
    outputs = produced.transpose(0, 2, 1, 3).reshape(count_rows, heads_here, DV)
    gate = local_gate.astype(jnp.float32).reshape(count_rows, heads_here, DV)
    normed = gated_norm(outputs, gate, norm_gain)
    return gather_heads(normed)


def solution(mesh):
    in_specs = (
        P(("ctx", "head"), None),
        P(("ctx", "head"), None),
        P(("ctx", "head"), None),
        P(("ctx", "head"), None),
        P(("ctx", "head"), None),
        P(("ctx", "head"), None),
        P(None, "head"),
        P(None, "head"),
        P(None, "head"),
        P(),
    )
    out_specs = P(("ctx", "head"), None)
    return jax.shard_map(
        on_device, mesh=mesh, in_specs=in_specs, out_specs=out_specs, check_vma=False
    )
```

```python
import functools

import jax
import jax.numpy as jnp
from jax import lax
from jax.experimental import pallas as pl
from jax.experimental.pallas import tpu as pltpu
from jax.sharding import PartitionSpec as P

DK = 128
DV = 128
HK = 8
HV = 16
BLOCK = 64


HIGHEST_PRECISION = lax.Precision.HIGHEST
EPSILON = 1e-06
MATMUL_PRECISION = lax.Precision.HIGH


def passed_along(value, axis, steps):
    count = lax.axis_size(axis)
    leading, last = (max(0, -steps), min(count, count - steps))
    return lax.ppermute(value, axis, [(source, source + steps) for source in range(leading, last)])


def matmul(spec, left, right):
    return jnp.einsum(spec, left, right, precision=MATMUL_PRECISION)


def unit_lower_inverse(strict):
    size = strict.shape[-1]
    rows_index = jnp.arange(size)[:, None]
    cols_index = jnp.arange(size)[None, :]
    inverse = jnp.broadcast_to(jnp.eye(size, dtype=strict.dtype), strict.shape)
    width = 1
    while width < size:
        pick = (
            (rows_index // (2 * width) == cols_index // (2 * width))
            & ((rows_index // width) % 2 == 1)
            & ((cols_index // width) % 2 == 0)
        )
        lower = jnp.where(pick, strict, 0.0)
        step = matmul("...ij,...jk->...ik", inverse, matmul("...ij,...jk->...ik", lower, inverse))
        inverse = inverse - lax.optimization_barrier(step)
        width *= 2
    return inverse


def forward_substitution(coupling, targets):
    return matmul("...ij,...jf->...if", unit_lower_inverse(coupling), targets)


def causal_conv(inputs, earlier_rows, weights):
    kernel_width = weights.shape[0]
    count_rows = inputs.shape[0]
    joined = jnp.concatenate([earlier_rows, inputs], axis=0)
    result = joined[kernel_width - 1 :] * weights[kernel_width - 1]
    for offset in range(1, kernel_width):
        result = (
            result
            + joined[kernel_width - 1 - offset : kernel_width - 1 - offset + count_rows]
            * weights[kernel_width - 1 - offset]
        )
    return jax.nn.silu(result)


def unit_heads(mixed, heads):
    shaped = mixed.reshape(mixed.shape[0], heads, -1)
    return shaped / jnp.sqrt(jnp.sum(shaped * shaped, axis=-1, keepdims=True) + EPSILON)


def into_blocks(array, block_len):
    count_rows, heads, inner_dim = array.shape
    return array.reshape(count_rows // block_len, block_len, heads, inner_dim).transpose(0, 2, 1, 3)


def block_scalars(array, block_len):
    count_rows, heads = array.shape
    return (
        array.astype(jnp.float32)
        .reshape(count_rows // block_len, block_len, heads)
        .transpose(0, 2, 1)
    )


def block_terms(queries, keys, values, log_gate, strength):
    block_len = queries.shape[2]
    key_dim = keys.shape[-1]
    cumulative = jnp.cumsum(log_gate, axis=-1)
    rows_index = jnp.arange(block_len)[:, None]
    cols_index = jnp.arange(block_len)[None, :]
    causal = rows_index >= cols_index
    strictly = rows_index > cols_index
    spread = jnp.where(causal, cumulative[..., :, None] - cumulative[..., None, :], 0.0)
    decays = jnp.where(causal, jnp.exp(spread), 0.0)
    key_key = jnp.einsum("nhid,nhjd->nhij", keys, keys, precision=MATMUL_PRECISION)
    coupling = jnp.where(strictly, strength[..., None] * decays * key_key, 0.0)
    targets = jnp.concatenate(
        [(strength * jnp.exp(cumulative))[..., None] * keys, strength[..., None] * values], axis=-1
    )
    solved = forward_substitution(coupling, targets)
    key_part = solved[..., :key_dim]
    value_part = solved[..., key_dim:]
    query_key = jnp.einsum("nhid,nhjd->nhij", queries, keys, precision=MATMUL_PRECISION)
    within = query_key * decays
    query_decay = jnp.exp(cumulative)[..., None] * queries
    closing_logarithm = cumulative[..., -1:]
    key_decay = jnp.exp(closing_logarithm - cumulative)[..., None] * keys
    end_decay = jnp.exp(closing_logarithm[..., 0])
    return (key_part, value_part, within, query_decay, key_decay, end_decay)


def block_apply(memory, pieces):
    key_part, value_part, within, query_decay, key_decay, end_decay = pieces
    corrected = value_part - jnp.einsum(
        "hcd,hde->hce", key_part, memory, precision=HIGHEST_PRECISION
    )
    result = jnp.einsum("hcd,hde->hce", query_decay, memory, precision=HIGHEST_PRECISION)
    result = result + jnp.einsum("hij,hje->hie", within, corrected, precision=HIGHEST_PRECISION)
    memory = end_decay[:, None, None] * memory + jnp.einsum(
        "hcd,hce->hde", key_decay, corrected, precision=HIGHEST_PRECISION
    )
    return (memory, result)


def gated_norm(outputs, gate, gain):
    meansq = jnp.mean(outputs * outputs, axis=-1, keepdims=True)
    scaled = outputs / jnp.sqrt(meansq + EPSILON) * gain * jax.nn.silu(gate)
    return scaled.astype(jnp.bfloat16).reshape(outputs.shape[0], -1)


def compose_maps(later_map, earlier_map):
    return jnp.einsum("hij,hjk->hik", later_map, earlier_map, precision=HIGHEST_PRECISION)


MESH_IDS = pl.DeviceIdType.MESH


def scan_spans(count):
    spans = []
    span = 1
    while 2 * span < count:
        spans.append(span)
        span *= 2
    return spans, span + 1


def kernel_dot(left, right):
    return jnp.dot(left, right, preferred_element_type=jnp.float32, precision=HIGHEST_PRECISION)


def ctx_scan_kernel(count, maps_ref, out_ref, current, slots, near_slot, far_slot, send_sems, recv_sems):
    place = lax.axis_index("ctx")
    group = lax.axis_index("head")
    heads = maps_ref.shape[1]
    spans, far = scan_spans(count)
    offsets = sorted(set(spans + [1] + ([far] if far < count else [])))
    barrier = pltpu.get_barrier_semaphore()
    partners = jnp.int32(0)
    for offset in offsets:
        for target in (place + offset, place - offset):
            valid = jnp.logical_and(target >= 0, target < count)

            @pl.when(valid)
            def _():
                pl.semaphore_signal(barrier, inc=1, device_id=(target, group), device_id_type=MESH_IDS)

            partners = partners + valid.astype(jnp.int32)
    pl.semaphore_wait(barrier, partners)

    source = maps_ref
    for index, span in enumerate(spans):
        sending = place + span < count
        receiving = place >= span
        copy_out = pltpu.make_async_remote_copy(
            src_ref=source,
            dst_ref=slots.at[index],
            send_sem=send_sems.at[index],
            recv_sem=recv_sems.at[index],
            device_id=(place + span, group),
            device_id_type=MESH_IDS,
        )
        pl.when(sending)(copy_out.start)
        pl.when(receiving)(copy_out.wait_recv)
        dest = current.at[index % 2]

        def composed(source=source, dest=dest, index=index):
            for head in range(heads):
                trans_here = source[0, head]
                dest[0, head] = kernel_dot(trans_here, slots[index, 0, head])
                dest[1, head] = kernel_dot(trans_here, slots[index, 1, head]) + source[1, head]

        def kept(source=source, dest=dest):
            dest[...] = source[...]

        pl.when(receiving)(composed)
        pl.when(jnp.logical_not(receiving))(kept)
        pl.when(sending)(copy_out.wait_send)
        source = dest

    last = len(spans)
    near_copy = pltpu.make_async_remote_copy(
        src_ref=source,
        dst_ref=near_slot,
        send_sem=send_sems.at[last],
        recv_sem=recv_sems.at[last],
        device_id=(place + 1, group),
        device_id_type=MESH_IDS,
    )
    pl.when(place + 1 < count)(near_copy.start)
    if far < count:
        far_copy = pltpu.make_async_remote_copy(
            src_ref=source.at[1],
            dst_ref=far_slot,
            send_sem=send_sems.at[last + 1],
            recv_sem=recv_sems.at[last + 1],
            device_id=(place + far, group),
            device_id_type=MESH_IDS,
        )
        pl.when(place + far < count)(far_copy.start)
    pl.when(place >= 1)(near_copy.wait_recv)
    out_ref[...] = jnp.zeros_like(out_ref)

    def from_near():
        out_ref[...] = near_slot[1]

    pl.when(place >= 1)(from_near)
    if far < count:
        pl.when(place >= far)(far_copy.wait_recv)

        def from_far():
            for head in range(heads):
                out_ref[head] = out_ref[head] + kernel_dot(near_slot[0, head], far_slot[head])

        pl.when(place >= far)(from_far)
        pl.when(place + far < count)(far_copy.wait_send)
    pl.when(place + 1 < count)(near_copy.wait_send)


def ctx_scan(maps):
    count = lax.axis_size("ctx")
    if count == 1:
        return jnp.zeros_like(maps[1])
    spans, far = scan_spans(count)
    side = maps.shape[1:]
    return pl.pallas_call(
        functools.partial(ctx_scan_kernel, count),
        out_shape=jax.ShapeDtypeStruct(side, jnp.float32),
        in_specs=[pl.BlockSpec(memory_space=pltpu.VMEM)],
        out_specs=pl.BlockSpec(memory_space=pltpu.VMEM),
        scratch_shapes=[
            pltpu.VMEM((2,) + maps.shape, jnp.float32),
            pltpu.VMEM((max(len(spans), 1),) + maps.shape, jnp.float32),
            pltpu.VMEM(maps.shape, jnp.float32),
            pltpu.VMEM(side, jnp.float32),
            pltpu.SemaphoreType.DMA((len(spans) + 2,)),
            pltpu.SemaphoreType.DMA((len(spans) + 2,)),
        ],
        compiler_params=pltpu.CompilerParams(collective_id=0, has_side_effects=True),
    )(maps)


def head_exchange_kernel(parts, count, source_view, target_view, *refs):
    sources, targets = refs[:count], refs[count : 2 * count]
    send_sems, recv_sems = refs[2 * count], refs[2 * count + 1]
    me = lax.axis_index("head")
    line = lax.axis_index("ctx")
    barrier = pltpu.get_barrier_semaphore()
    for peer in range(parts):

        @pl.when(me != peer)
        def _():
            pl.semaphore_signal(barrier, inc=1, device_id=(line, peer), device_id_type=MESH_IDS)

    pl.semaphore_wait(barrier, parts - 1)
    outgoing, incoming, local = [], [], []
    for index in range(count):
        for peer in range(parts):
            away = peer != me
            sending = pltpu.make_async_remote_copy(
                src_ref=source_view(sources[index], peer),
                dst_ref=target_view(targets[index], me),
                send_sem=send_sems.at[index, peer],
                recv_sem=recv_sems.at[index, me],
                device_id=(line, peer),
                device_id_type=MESH_IDS,
            )
            pl.when(away)(sending.start)
            staying = pltpu.make_async_copy(
                source_view(sources[index], peer),
                target_view(targets[index], peer),
                send_sems.at[index, peer],
            )
            pl.when(jnp.logical_not(away))(staying.start)
            arriving = pltpu.make_async_remote_copy(
                src_ref=source_view(sources[index], peer),
                dst_ref=target_view(targets[index], peer),
                send_sem=send_sems.at[index, peer],
                recv_sem=recv_sems.at[index, peer],
                device_id=(line, peer),
                device_id_type=MESH_IDS,
            )
            outgoing.append((away, sending))
            incoming.append((away, arriving))
            local.append((away, staying))
    for (away, sending), (_, arriving), (_, staying) in zip(outgoing, incoming, local):
        pl.when(away)(sending.wait_send)
        pl.when(away)(arriving.wait_recv)
        pl.when(jnp.logical_not(away))(staying.wait)


def head_exchange(arrays, target_shapes, source_view, target_view, collective):
    parts = lax.axis_size("head")
    count = len(arrays)
    return pl.pallas_call(
        functools.partial(head_exchange_kernel, parts, count, source_view, target_view),
        out_shape=[jax.ShapeDtypeStruct(shape, array.dtype) for shape, array in zip(target_shapes, arrays)],
        in_specs=[pl.BlockSpec(memory_space=pl.ANY)] * count,
        out_specs=[pl.BlockSpec(memory_space=pl.ANY)] * count,
        scratch_shapes=[
            pltpu.SemaphoreType.DMA((count, parts)),
            pltpu.SemaphoreType.DMA((count, parts)),
        ],
        compiler_params=pltpu.CompilerParams(collective_id=collective, has_side_effects=True),
    )(*arrays)


def columns_of(ref, peer):
    if len(ref.shape) == 3:
        return ref.at[peer]
    width = ref.shape[1] // lax.axis_size("head")
    return ref.at[:, pl.ds(peer * width, width)]


def rows_of(ref, peer):
    if len(ref.shape) == 3:
        return ref.at[peer]
    height = ref.shape[0] // lax.axis_size("head")
    return ref.at[pl.ds(peer * height, height), :]


def spread_heads(arrays):
    parts = lax.axis_size("head")
    shapes = [
        array.shape if array.ndim == 3 else (parts * array.shape[0], array.shape[1] // parts)
        for array in arrays
    ]
    return head_exchange(arrays, shapes, columns_of, rows_of, 1)


def gather_heads(array):
    parts = lax.axis_size("head")
    shape = (array.shape[0] // parts, array.shape[1] * parts)
    return head_exchange([array], [shape], rows_of, columns_of, 2)[0]


def on_device(
    query_rows,
    key_rows,
    value_rows,
    gate_rows,
    log_decay,
    write_strength,
    conv_query,
    conv_key,
    conv_value,
    norm_gain,
):
    parts = lax.axis_size("head")
    scalars = jnp.concatenate(
        [
            log_decay.reshape(log_decay.shape[0], parts, -1),
            write_strength.reshape(write_strength.shape[0], parts, -1),
        ],
        axis=2,
    ).transpose(1, 0, 2)
    device_query, local_key, local_value, moved_scalars = spread_heads(
        [query_rows, key_rows, value_rows, scalars]
    )
    moved_scalars = moved_scalars.reshape(-1, moved_scalars.shape[-1])
    split_at = log_decay.shape[1] // parts
    local_decay, local_strength = moved_scalars[:, :split_at], moved_scalars[:, split_at:]
    local_gate = lax.all_to_all(gate_rows, "head", split_axis=1, concat_axis=0, tiled=True)
    joined = jnp.concatenate([device_query, local_key, local_value], axis=1)
    kernel_width = conv_query.shape[0]
    count_rows = joined.shape[0]
    tail_rows = passed_along(joined[count_rows - (kernel_width - 1) :], "ctx", 1)
    weights_all = jnp.concatenate([conv_query, conv_key, conv_value], axis=1).astype(jnp.float32)
    mixed = causal_conv(joined.astype(jnp.float32), tail_rows.astype(jnp.float32), weights_all)
    key_width = device_query.shape[1]
    head_keys = key_width // DK
    per_key = HV // HK
    query_heads = jnp.repeat(
        unit_heads(mixed[:, :key_width], head_keys) * DK ** (-0.5), per_key, axis=1
    )
    key_heads = jnp.repeat(
        unit_heads(mixed[:, key_width : 2 * key_width], head_keys), per_key, axis=1
    )
    value_heads = mixed[:, 2 * key_width :].reshape(count_rows, -1, DV)
    terms = block_terms(
        into_blocks(query_heads, BLOCK),
        into_blocks(key_heads, BLOCK),
        into_blocks(value_heads, BLOCK),
        block_scalars(local_decay, BLOCK),
        block_scalars(local_strength, BLOCK),
    )
    key_part, value_part, within, query_decay, key_decay, end_decay = terms
    heads_here = key_part.shape[1]
    identity_mat = jnp.broadcast_to(jnp.eye(DK, dtype=jnp.float32), (heads_here, DK, DK))
    trans = end_decay[..., None, None] * identity_mat - matmul(
        "nhcd,nhce->nhde", key_decay, key_part
    )
    bias = matmul("nhcd,nhce->nhde", key_decay, value_part)
    blocks_here = trans.shape[0]
    span = 1
    while span < blocks_here:
        earlier_trans = jnp.concatenate(
            [jnp.broadcast_to(identity_mat, (span,) + identity_mat.shape), trans[:-span]], axis=0
        )
        earlier_bias = jnp.concatenate([jnp.zeros_like(bias[:span]), bias[:-span]], axis=0)
        trans, bias = (
            matmul("nhij,nhjk->nhik", trans, earlier_trans),
            matmul("nhij,nhjk->nhik", trans, earlier_bias) + bias,
        )
        span *= 2
    earlier_trans = jnp.concatenate([identity_mat[None], trans[:-1]], axis=0)
    earlier_bias = jnp.concatenate([jnp.zeros_like(bias[:1]), bias[:-1]], axis=0)
    corrected = value_part - matmul("nhcd,nhde->nhce", key_part, earlier_bias)
    local_result = matmul("nhcd,nhde->nhce", query_decay, earlier_bias) + matmul(
        "nhij,nhje->nhie", within, corrected
    )
    reach = query_decay - matmul("nhij,nhjd->nhid", within, key_part)
    carry_map = matmul("nhcd,nhde->nhce", reach, earlier_trans)
    total_trans, total_bias = trans[-1], bias[-1]
    initial = ctx_scan(jnp.stack([total_trans, total_bias]))
    produced = local_result + matmul("nhcd,hde->nhce", carry_map, initial)
    outputs = produced.transpose(0, 2, 1, 3).reshape(count_rows, heads_here, DV)
    gate = local_gate.astype(jnp.float32).reshape(count_rows, heads_here, DV)
    normed = gated_norm(outputs, gate, norm_gain)
    return gather_heads(normed)


def solution(mesh):
    in_specs = (
        P(("ctx", "head"), None),
        P(("ctx", "head"), None),
        P(("ctx", "head"), None),
        P(("ctx", "head"), None),
        P(("ctx", "head"), None),
        P(("ctx", "head"), None),
        P(None, "head"),
        P(None, "head"),
        P(None, "head"),
        P(),
    )
    out_specs = P(("ctx", "head"), None)
    return jax.shard_map(
        on_device, mesh=mesh, in_specs=in_specs, out_specs=out_specs, check_vma=False
    )
```

```python
import functools

import jax
import jax.numpy as jnp
from jax import lax
from jax.experimental import pallas as pl
from jax.experimental.pallas import tpu as pltpu
from jax.sharding import PartitionSpec as P

DK = 128
DV = 128
HK = 8
HV = 16
BLOCK = 64


HIGHEST_PRECISION = lax.Precision.HIGHEST
EPSILON = 1e-06
MATMUL_PRECISION = lax.Precision.HIGH


def passed_along(value, axis, steps):
    count = lax.axis_size(axis)
    leading, last = (max(0, -steps), min(count, count - steps))
    return lax.ppermute(value, axis, [(source, source + steps) for source in range(leading, last)])


def matmul(spec, left, right):
    return jnp.einsum(spec, left, right, precision=MATMUL_PRECISION)


def unit_lower_inverse(strict):
    size = strict.shape[-1]
    rows_index = jnp.arange(size)[:, None]
    cols_index = jnp.arange(size)[None, :]
    inverse = jnp.broadcast_to(jnp.eye(size, dtype=strict.dtype), strict.shape)
    width = 1
    while width < size:
        pick = (
            (rows_index // (2 * width) == cols_index // (2 * width))
            & ((rows_index // width) % 2 == 1)
            & ((cols_index // width) % 2 == 0)
        )
        lower = jnp.where(pick, strict, 0.0)
        step = matmul("...ij,...jk->...ik", inverse, matmul("...ij,...jk->...ik", lower, inverse))
        inverse = inverse - lax.optimization_barrier(step)
        width *= 2
    return inverse


def forward_substitution(coupling, targets):
    return matmul("...ij,...jf->...if", unit_lower_inverse(coupling), targets)


def causal_conv(inputs, earlier_rows, weights):
    kernel_width = weights.shape[0]
    count_rows = inputs.shape[0]
    joined = jnp.concatenate([earlier_rows, inputs], axis=0)
    result = joined[kernel_width - 1 :] * weights[kernel_width - 1]
    for offset in range(1, kernel_width):
        result = (
            result
            + joined[kernel_width - 1 - offset : kernel_width - 1 - offset + count_rows]
            * weights[kernel_width - 1 - offset]
        )
    return jax.nn.silu(result)


def unit_heads(mixed, heads):
    shaped = mixed.reshape(mixed.shape[0], heads, -1)
    return shaped / jnp.sqrt(jnp.sum(shaped * shaped, axis=-1, keepdims=True) + EPSILON)


def into_blocks(array, block_len):
    count_rows, heads, inner_dim = array.shape
    return array.reshape(count_rows // block_len, block_len, heads, inner_dim).transpose(0, 2, 1, 3)


def block_scalars(array, block_len):
    count_rows, heads = array.shape
    return (
        array.astype(jnp.float32)
        .reshape(count_rows // block_len, block_len, heads)
        .transpose(0, 2, 1)
    )


def block_terms(queries, keys, values, log_gate, strength):
    block_len = queries.shape[2]
    key_dim = keys.shape[-1]
    cumulative = jnp.cumsum(log_gate, axis=-1)
    rows_index = jnp.arange(block_len)[:, None]
    cols_index = jnp.arange(block_len)[None, :]
    causal = rows_index >= cols_index
    strictly = rows_index > cols_index
    spread = jnp.where(causal, cumulative[..., :, None] - cumulative[..., None, :], 0.0)
    decays = jnp.where(causal, jnp.exp(spread), 0.0)
    key_key = jnp.einsum("nhid,nhjd->nhij", keys, keys, precision=MATMUL_PRECISION)
    coupling = jnp.where(strictly, strength[..., None] * decays * key_key, 0.0)
    targets = jnp.concatenate(
        [(strength * jnp.exp(cumulative))[..., None] * keys, strength[..., None] * values], axis=-1
    )
    solved = forward_substitution(coupling, targets)
    key_part = solved[..., :key_dim]
    value_part = solved[..., key_dim:]
    query_key = jnp.einsum("nhid,nhjd->nhij", queries, keys, precision=MATMUL_PRECISION)
    within = query_key * decays
    query_decay = jnp.exp(cumulative)[..., None] * queries
    closing_logarithm = cumulative[..., -1:]
    key_decay = jnp.exp(closing_logarithm - cumulative)[..., None] * keys
    end_decay = jnp.exp(closing_logarithm[..., 0])
    return (key_part, value_part, within, query_decay, key_decay, end_decay)


def block_apply(memory, pieces):
    key_part, value_part, within, query_decay, key_decay, end_decay = pieces
    corrected = value_part - jnp.einsum(
        "hcd,hde->hce", key_part, memory, precision=HIGHEST_PRECISION
    )
    result = jnp.einsum("hcd,hde->hce", query_decay, memory, precision=HIGHEST_PRECISION)
    result = result + jnp.einsum("hij,hje->hie", within, corrected, precision=HIGHEST_PRECISION)
    memory = end_decay[:, None, None] * memory + jnp.einsum(
        "hcd,hce->hde", key_decay, corrected, precision=HIGHEST_PRECISION
    )
    return (memory, result)


def gated_norm(outputs, gate, gain):
    meansq = jnp.mean(outputs * outputs, axis=-1, keepdims=True)
    scaled = outputs / jnp.sqrt(meansq + EPSILON) * gain * jax.nn.silu(gate)
    return scaled.astype(jnp.bfloat16).reshape(outputs.shape[0], -1)


def compose_maps(later_map, earlier_map):
    return jnp.einsum("hij,hjk->hik", later_map, earlier_map, precision=HIGHEST_PRECISION)


MESH_IDS = pl.DeviceIdType.MESH


def scan_spans(count):
    spans = []
    span = 1
    while 2 * span < count:
        spans.append(span)
        span *= 2
    return spans, span + 1


def kernel_dot(left, right):
    return jnp.dot(left, right, preferred_element_type=jnp.float32, precision=HIGHEST_PRECISION)


def ctx_scan_kernel(count, maps_ref, out_ref, current, slots, near_slot, far_slot, send_sems, recv_sems):
    place = lax.axis_index("ctx")
    group = lax.axis_index("head")
    heads = maps_ref.shape[1]
    spans, far = scan_spans(count)
    rounds = len(spans)
    has_far = far < count
    offsets = sorted(set(spans + [1] + ([far] if has_far else [])))
    barrier = pltpu.get_barrier_semaphore()
    partners = jnp.int32(0)
    for offset in offsets:
        for target in (place + offset, place - offset):
            valid = jnp.logical_and(target >= 0, target < count)

            @pl.when(valid)
            def _():
                pl.semaphore_signal(barrier, inc=1, device_id=(target, group), device_id_type=MESH_IDS)

            partners = partners + valid.astype(jnp.int32)
    pl.semaphore_wait(barrier, partners)

    def result_of(index):
        return maps_ref if index < 0 else current.at[index % 2]

    def round_copy(index, kind, head):
        return pltpu.make_async_remote_copy(
            src_ref=result_of(index - 1).at[kind, head],
            dst_ref=slots.at[index, kind, head],
            send_sem=send_sems.at[index, kind * heads + head],
            recv_sem=recv_sems.at[index, kind * heads + head],
            device_id=(place + spans[index], group),
            device_id_type=MESH_IDS,
        )

    def near_copy(kind, head):
        return pltpu.make_async_remote_copy(
            src_ref=result_of(rounds - 1).at[kind, head],
            dst_ref=near_slot.at[kind, head],
            send_sem=send_sems.at[rounds, kind * heads + head],
            recv_sem=recv_sems.at[rounds, kind * heads + head],
            device_id=(place + 1, group),
            device_id_type=MESH_IDS,
        )

    def far_copy(head):
        return pltpu.make_async_remote_copy(
            src_ref=result_of(rounds - 1).at[1, head],
            dst_ref=far_slot.at[head],
            send_sem=send_sems.at[rounds + 1, head],
            recv_sem=recv_sems.at[rounds + 1, head],
            device_id=(place + far, group),
            device_id_type=MESH_IDS,
        )

    def launch_after(index, kind, head):
        following = index + 1
        if following < rounds:
            pl.when(place + spans[following] < count)(round_copy(following, kind, head).start)
        else:
            pl.when(place + 1 < count)(near_copy(kind, head).start)
            if has_far and kind == 1:
                pl.when(place + far < count)(far_copy(head).start)

    for kind in range(2):
        for head in range(heads):
            launch_after(-1, kind, head)

    for index, span in enumerate(spans):
        source = result_of(index - 1)
        dest = result_of(index)
        receiving = place >= span

        def composed(index=index, source=source, dest=dest):
            for head in range(heads):
                round_copy(index, 0, head).wait_recv()
                dest[0, head] = kernel_dot(source[0, head], slots[index, 0, head])
                launch_after(index, 0, head)
                round_copy(index, 1, head).wait_recv()
                dest[1, head] = kernel_dot(source[0, head], slots[index, 1, head]) + source[1, head]
                launch_after(index, 1, head)

        def kept(index=index, source=source, dest=dest):
            dest[...] = source[...]
            for kind in range(2):
                for head in range(heads):
                    launch_after(index, kind, head)

        pl.when(receiving)(composed)
        pl.when(jnp.logical_not(receiving))(kept)

        def sent(index=index):
            for kind in range(2):
                for head in range(heads):
                    round_copy(index, kind, head).wait_send()

        pl.when(place + span < count)(sent)

    def near_arrived():
        for kind in range(2):
            for head in range(heads):
                near_copy(kind, head).wait_recv()
        out_ref[...] = near_slot[1]

    out_ref[...] = jnp.zeros_like(out_ref)
    pl.when(place >= 1)(near_arrived)
    if has_far:

        def far_arrived():
            for head in range(heads):
                far_copy(head).wait_recv()
                out_ref[head] = out_ref[head] + kernel_dot(near_slot[0, head], far_slot[head])

        pl.when(place >= far)(far_arrived)

        def far_sent():
            for head in range(heads):
                far_copy(head).wait_send()

        pl.when(place + far < count)(far_sent)

    def near_sent():
        for kind in range(2):
            for head in range(heads):
                near_copy(kind, head).wait_send()

    pl.when(place + 1 < count)(near_sent)


def ctx_scan(maps):
    count = lax.axis_size("ctx")
    if count == 1:
        return jnp.zeros_like(maps[1])
    spans, far = scan_spans(count)
    side = maps.shape[1:]
    return pl.pallas_call(
        functools.partial(ctx_scan_kernel, count),
        out_shape=jax.ShapeDtypeStruct(side, jnp.float32),
        in_specs=[pl.BlockSpec(memory_space=pltpu.VMEM)],
        out_specs=pl.BlockSpec(memory_space=pltpu.VMEM),
        scratch_shapes=[
            pltpu.VMEM((2,) + maps.shape, jnp.float32),
            pltpu.VMEM((max(len(spans), 1),) + maps.shape, jnp.float32),
            pltpu.VMEM(maps.shape, jnp.float32),
            pltpu.VMEM(side, jnp.float32),
            pltpu.SemaphoreType.DMA((len(spans) + 2, 2 * maps.shape[1])),
            pltpu.SemaphoreType.DMA((len(spans) + 2, 2 * maps.shape[1])),
        ],
        compiler_params=pltpu.CompilerParams(collective_id=0, has_side_effects=True),
    )(maps)


def head_exchange_kernel(parts, count, source_view, target_view, *refs):
    sources, targets = refs[:count], refs[count : 2 * count]
    send_sems, recv_sems = refs[2 * count], refs[2 * count + 1]
    me = lax.axis_index("head")
    line = lax.axis_index("ctx")
    barrier = pltpu.get_barrier_semaphore()
    for peer in range(parts):

        @pl.when(me != peer)
        def _():
            pl.semaphore_signal(barrier, inc=1, device_id=(line, peer), device_id_type=MESH_IDS)

    pl.semaphore_wait(barrier, parts - 1)
    outgoing, incoming, local = [], [], []
    for index in range(count):
        for peer in range(parts):
            away = peer != me
            sending = pltpu.make_async_remote_copy(
                src_ref=source_view(sources[index], peer),
                dst_ref=target_view(targets[index], me),
                send_sem=send_sems.at[index, peer],
                recv_sem=recv_sems.at[index, me],
                device_id=(line, peer),
                device_id_type=MESH_IDS,
            )
            pl.when(away)(sending.start)
            staying = pltpu.make_async_copy(
                source_view(sources[index], peer),
                target_view(targets[index], peer),
                send_sems.at[index, peer],
            )
            pl.when(jnp.logical_not(away))(staying.start)
            arriving = pltpu.make_async_remote_copy(
                src_ref=source_view(sources[index], peer),
                dst_ref=target_view(targets[index], peer),
                send_sem=send_sems.at[index, peer],
                recv_sem=recv_sems.at[index, peer],
                device_id=(line, peer),
                device_id_type=MESH_IDS,
            )
            outgoing.append((away, sending))
            incoming.append((away, arriving))
            local.append((away, staying))
    for (away, sending), (_, arriving), (_, staying) in zip(outgoing, incoming, local):
        pl.when(away)(sending.wait_send)
        pl.when(away)(arriving.wait_recv)
        pl.when(jnp.logical_not(away))(staying.wait)


def head_exchange(arrays, target_shapes, source_view, target_view, collective):
    parts = lax.axis_size("head")
    count = len(arrays)
    return pl.pallas_call(
        functools.partial(head_exchange_kernel, parts, count, source_view, target_view),
        out_shape=[jax.ShapeDtypeStruct(shape, array.dtype) for shape, array in zip(target_shapes, arrays)],
        in_specs=[pl.BlockSpec(memory_space=pl.ANY)] * count,
        out_specs=[pl.BlockSpec(memory_space=pl.ANY)] * count,
        scratch_shapes=[
            pltpu.SemaphoreType.DMA((count, parts)),
            pltpu.SemaphoreType.DMA((count, parts)),
        ],
        compiler_params=pltpu.CompilerParams(collective_id=collective, has_side_effects=True),
    )(*arrays)


def columns_of(ref, peer):
    if len(ref.shape) == 3:
        return ref.at[peer]
    width = ref.shape[1] // lax.axis_size("head")
    return ref.at[:, pl.ds(peer * width, width)]


def rows_of(ref, peer):
    if len(ref.shape) == 3:
        return ref.at[peer]
    height = ref.shape[0] // lax.axis_size("head")
    return ref.at[pl.ds(peer * height, height), :]


def spread_heads(arrays):
    parts = lax.axis_size("head")
    shapes = [
        array.shape if array.ndim == 3 else (parts * array.shape[0], array.shape[1] // parts)
        for array in arrays
    ]
    return head_exchange(arrays, shapes, columns_of, rows_of, 1)


def gather_heads(array):
    parts = lax.axis_size("head")
    shape = (array.shape[0] // parts, array.shape[1] * parts)
    return head_exchange([array], [shape], rows_of, columns_of, 2)[0]


def on_device(
    query_rows,
    key_rows,
    value_rows,
    gate_rows,
    log_decay,
    write_strength,
    conv_query,
    conv_key,
    conv_value,
    norm_gain,
):
    parts = lax.axis_size("head")
    scalars = jnp.concatenate(
        [
            log_decay.reshape(log_decay.shape[0], parts, -1),
            write_strength.reshape(write_strength.shape[0], parts, -1),
        ],
        axis=2,
    ).transpose(1, 0, 2)
    device_query, local_key, local_value, moved_scalars = spread_heads(
        [query_rows, key_rows, value_rows, scalars]
    )
    moved_scalars = moved_scalars.reshape(-1, moved_scalars.shape[-1])
    split_at = log_decay.shape[1] // parts
    local_decay, local_strength = moved_scalars[:, :split_at], moved_scalars[:, split_at:]
    local_gate = lax.all_to_all(gate_rows, "head", split_axis=1, concat_axis=0, tiled=True)
    joined = jnp.concatenate([device_query, local_key, local_value], axis=1)
    kernel_width = conv_query.shape[0]
    count_rows = joined.shape[0]
    tail_rows = passed_along(joined[count_rows - (kernel_width - 1) :], "ctx", 1)
    weights_all = jnp.concatenate([conv_query, conv_key, conv_value], axis=1).astype(jnp.float32)
    mixed = causal_conv(joined.astype(jnp.float32), tail_rows.astype(jnp.float32), weights_all)
    key_width = device_query.shape[1]
    head_keys = key_width // DK
    per_key = HV // HK
    query_heads = jnp.repeat(
        unit_heads(mixed[:, :key_width], head_keys) * DK ** (-0.5), per_key, axis=1
    )
    key_heads = jnp.repeat(
        unit_heads(mixed[:, key_width : 2 * key_width], head_keys), per_key, axis=1
    )
    value_heads = mixed[:, 2 * key_width :].reshape(count_rows, -1, DV)
    terms = block_terms(
        into_blocks(query_heads, BLOCK),
        into_blocks(key_heads, BLOCK),
        into_blocks(value_heads, BLOCK),
        block_scalars(local_decay, BLOCK),
        block_scalars(local_strength, BLOCK),
    )
    key_part, value_part, within, query_decay, key_decay, end_decay = terms
    heads_here = key_part.shape[1]
    identity_mat = jnp.broadcast_to(jnp.eye(DK, dtype=jnp.float32), (heads_here, DK, DK))
    trans = end_decay[..., None, None] * identity_mat - matmul(
        "nhcd,nhce->nhde", key_decay, key_part
    )
    bias = matmul("nhcd,nhce->nhde", key_decay, value_part)
    blocks_here = trans.shape[0]
    span = 1
    while span < blocks_here:
        earlier_trans = jnp.concatenate(
            [jnp.broadcast_to(identity_mat, (span,) + identity_mat.shape), trans[:-span]], axis=0
        )
        earlier_bias = jnp.concatenate([jnp.zeros_like(bias[:span]), bias[:-span]], axis=0)
        trans, bias = (
            matmul("nhij,nhjk->nhik", trans, earlier_trans),
            matmul("nhij,nhjk->nhik", trans, earlier_bias) + bias,
        )
        span *= 2
    earlier_trans = jnp.concatenate([identity_mat[None], trans[:-1]], axis=0)
    earlier_bias = jnp.concatenate([jnp.zeros_like(bias[:1]), bias[:-1]], axis=0)
    corrected = value_part - matmul("nhcd,nhde->nhce", key_part, earlier_bias)
    local_result = matmul("nhcd,nhde->nhce", query_decay, earlier_bias) + matmul(
        "nhij,nhje->nhie", within, corrected
    )
    reach = query_decay - matmul("nhij,nhjd->nhid", within, key_part)
    carry_map = matmul("nhcd,nhde->nhce", reach, earlier_trans)
    total_trans, total_bias = trans[-1], bias[-1]
    initial = ctx_scan(jnp.stack([total_trans, total_bias]))
    produced = local_result + matmul("nhcd,hde->nhce", carry_map, initial)
    outputs = produced.transpose(0, 2, 1, 3).reshape(count_rows, heads_here, DV)
    gate = local_gate.astype(jnp.float32).reshape(count_rows, heads_here, DV)
    normed = gated_norm(outputs, gate, norm_gain)
    return gather_heads(normed)


def solution(mesh):
    in_specs = (
        P(("ctx", "head"), None),
        P(("ctx", "head"), None),
        P(("ctx", "head"), None),
        P(("ctx", "head"), None),
        P(("ctx", "head"), None),
        P(("ctx", "head"), None),
        P(None, "head"),
        P(None, "head"),
        P(None, "head"),
        P(),
    )
    out_specs = P(("ctx", "head"), None)
    return jax.shard_map(
        on_device, mesh=mesh, in_specs=in_specs, out_specs=out_specs, check_vma=False
    )
```

```python
import functools

import jax
import jax.numpy as jnp
from jax import lax
from jax.experimental import pallas as pl
from jax.experimental.pallas import tpu as pltpu
from jax.sharding import PartitionSpec as P

DK = 128
DV = 128
HK = 8
HV = 16
BLOCK = 64


HIGHEST_PRECISION = lax.Precision.HIGHEST
EPSILON = 1e-06
MATMUL_PRECISION = lax.Precision.HIGH


def passed_along(value, axis, steps):
    count = lax.axis_size(axis)
    leading, last = (max(0, -steps), min(count, count - steps))
    return lax.ppermute(value, axis, [(source, source + steps) for source in range(leading, last)])


def matmul(spec, left, right):
    return jnp.einsum(spec, left, right, precision=MATMUL_PRECISION)


def unit_lower_inverse(strict):
    size = strict.shape[-1]
    rows_index = jnp.arange(size)[:, None]
    cols_index = jnp.arange(size)[None, :]
    inverse = jnp.broadcast_to(jnp.eye(size, dtype=strict.dtype), strict.shape)
    width = 1
    while width < size:
        pick = (
            (rows_index // (2 * width) == cols_index // (2 * width))
            & ((rows_index // width) % 2 == 1)
            & ((cols_index // width) % 2 == 0)
        )
        lower = jnp.where(pick, strict, 0.0)
        step = jnp.einsum(
            "...ij,...jk->...ik",
            inverse,
            jnp.einsum("...ij,...jk->...ik", lower, inverse, precision=HIGHEST_PRECISION),
            precision=HIGHEST_PRECISION,
        )
        inverse = inverse - lax.optimization_barrier(step)
        width *= 2
    return inverse


def forward_substitution(coupling, targets):
    return jnp.einsum(
        "...ij,...jf->...if", unit_lower_inverse(coupling), targets, precision=HIGHEST_PRECISION
    )


def causal_conv(inputs, earlier_rows, weights):
    kernel_width = weights.shape[0]
    count_rows = inputs.shape[0]
    joined = jnp.concatenate([earlier_rows, inputs], axis=0)
    result = joined[kernel_width - 1 :] * weights[kernel_width - 1]
    for offset in range(1, kernel_width):
        result = (
            result
            + joined[kernel_width - 1 - offset : kernel_width - 1 - offset + count_rows]
            * weights[kernel_width - 1 - offset]
        )
    return jax.nn.silu(result)


def unit_heads(mixed, heads):
    shaped = mixed.reshape(mixed.shape[0], heads, -1)
    return shaped / jnp.sqrt(jnp.sum(shaped * shaped, axis=-1, keepdims=True) + EPSILON)


def into_blocks(array, block_len):
    count_rows, heads, inner_dim = array.shape
    return array.reshape(count_rows // block_len, block_len, heads, inner_dim).transpose(0, 2, 1, 3)


def block_scalars(array, block_len):
    count_rows, heads = array.shape
    return (
        array.astype(jnp.float32)
        .reshape(count_rows // block_len, block_len, heads)
        .transpose(0, 2, 1)
    )


def block_terms(queries, keys, values, log_gate, strength):
    block_len = queries.shape[2]
    key_dim = keys.shape[-1]
    cumulative = jnp.cumsum(log_gate, axis=-1)
    rows_index = jnp.arange(block_len)[:, None]
    cols_index = jnp.arange(block_len)[None, :]
    causal = rows_index >= cols_index
    strictly = rows_index > cols_index
    spread = jnp.where(causal, cumulative[..., :, None] - cumulative[..., None, :], 0.0)
    decays = jnp.where(causal, jnp.exp(spread), 0.0)
    key_key = jnp.einsum("nhid,nhjd->nhij", keys, keys, precision=HIGHEST_PRECISION)
    coupling = jnp.where(strictly, strength[..., None] * decays * key_key, 0.0)
    targets = jnp.concatenate(
        [(strength * jnp.exp(cumulative))[..., None] * keys, strength[..., None] * values], axis=-1
    )
    solved = forward_substitution(coupling, targets)
    key_part = solved[..., :key_dim]
    value_part = solved[..., key_dim:]
    query_key = jnp.einsum("nhid,nhjd->nhij", queries, keys, precision=MATMUL_PRECISION)
    within = query_key * decays
    query_decay = jnp.exp(cumulative)[..., None] * queries
    closing_logarithm = cumulative[..., -1:]
    key_decay = jnp.exp(closing_logarithm - cumulative)[..., None] * keys
    end_decay = jnp.exp(closing_logarithm[..., 0])
    return (key_part, value_part, within, query_decay, key_decay, end_decay)


def block_apply(memory, pieces):
    key_part, value_part, within, query_decay, key_decay, end_decay = pieces
    corrected = value_part - jnp.einsum(
        "hcd,hde->hce", key_part, memory, precision=HIGHEST_PRECISION
    )
    result = jnp.einsum("hcd,hde->hce", query_decay, memory, precision=HIGHEST_PRECISION)
    result = result + jnp.einsum("hij,hje->hie", within, corrected, precision=HIGHEST_PRECISION)
    memory = end_decay[:, None, None] * memory + jnp.einsum(
        "hcd,hce->hde", key_decay, corrected, precision=HIGHEST_PRECISION
    )
    return (memory, result)


def gated_norm(outputs, gate, gain):
    meansq = jnp.mean(outputs * outputs, axis=-1, keepdims=True)
    scaled = outputs / jnp.sqrt(meansq + EPSILON) * gain * jax.nn.silu(gate)
    return scaled.astype(jnp.bfloat16).reshape(outputs.shape[0], -1)


def compose_maps(later_map, earlier_map):
    return jnp.einsum("hij,hjk->hik", later_map, earlier_map, precision=HIGHEST_PRECISION)


MESH_IDS = pl.DeviceIdType.MESH


def scan_spans(count):
    spans = []
    span = 1
    while 2 * span < count:
        spans.append(span)
        span *= 2
    return spans, span + 1


def kernel_dot(left, right):
    return jnp.dot(left, right, preferred_element_type=jnp.float32, precision=HIGHEST_PRECISION)


def ctx_scan_kernel(count, maps_ref, out_ref, current, slots, near_slot, far_slot, send_sems, recv_sems):
    place = lax.axis_index("ctx")
    group = lax.axis_index("head")
    heads = maps_ref.shape[1]
    spans, far = scan_spans(count)
    rounds = len(spans)
    has_far = far < count
    offsets = sorted(set(spans + [1] + ([far] if has_far else [])))
    barrier = pltpu.get_barrier_semaphore()
    partners = jnp.int32(0)
    for offset in offsets:
        for target in (place + offset, place - offset):
            valid = jnp.logical_and(target >= 0, target < count)

            @pl.when(valid)
            def _():
                pl.semaphore_signal(barrier, inc=1, device_id=(target, group), device_id_type=MESH_IDS)

            partners = partners + valid.astype(jnp.int32)
    pl.semaphore_wait(barrier, partners)

    def result_of(index):
        return maps_ref if index < 0 else current.at[index % 2]

    def round_copy(index, kind, head):
        return pltpu.make_async_remote_copy(
            src_ref=result_of(index - 1).at[kind, head],
            dst_ref=slots.at[index, kind, head],
            send_sem=send_sems.at[index, kind * heads + head],
            recv_sem=recv_sems.at[index, kind * heads + head],
            device_id=(place + spans[index], group),
            device_id_type=MESH_IDS,
        )

    def near_copy(kind, head):
        return pltpu.make_async_remote_copy(
            src_ref=result_of(rounds - 1).at[kind, head],
            dst_ref=near_slot.at[kind, head],
            send_sem=send_sems.at[rounds, kind * heads + head],
            recv_sem=recv_sems.at[rounds, kind * heads + head],
            device_id=(place + 1, group),
            device_id_type=MESH_IDS,
        )

    def far_copy(head):
        return pltpu.make_async_remote_copy(
            src_ref=result_of(rounds - 1).at[1, head],
            dst_ref=far_slot.at[head],
            send_sem=send_sems.at[rounds + 1, head],
            recv_sem=recv_sems.at[rounds + 1, head],
            device_id=(place + far, group),
            device_id_type=MESH_IDS,
        )

    def launch_after(index, kind, head):
        following = index + 1
        if following < rounds:
            pl.when(place + spans[following] < count)(round_copy(following, kind, head).start)
        else:
            pl.when(place + 1 < count)(near_copy(kind, head).start)
            if has_far and kind == 1:
                pl.when(place + far < count)(far_copy(head).start)

    for kind in range(2):
        for head in range(heads):
            launch_after(-1, kind, head)

    for index, span in enumerate(spans):
        source = result_of(index - 1)
        dest = result_of(index)
        receiving = place >= span

        def composed(index=index, source=source, dest=dest):
            for head in range(heads):
                round_copy(index, 0, head).wait_recv()
                dest[0, head] = kernel_dot(source[0, head], slots[index, 0, head])
                launch_after(index, 0, head)
                round_copy(index, 1, head).wait_recv()
                dest[1, head] = kernel_dot(source[0, head], slots[index, 1, head]) + source[1, head]
                launch_after(index, 1, head)

        def kept(index=index, source=source, dest=dest):
            dest[...] = source[...]
            for kind in range(2):
                for head in range(heads):
                    launch_after(index, kind, head)

        pl.when(receiving)(composed)
        pl.when(jnp.logical_not(receiving))(kept)

        def sent(index=index):
            for kind in range(2):
                for head in range(heads):
                    round_copy(index, kind, head).wait_send()

        pl.when(place + span < count)(sent)

    def near_arrived():
        for kind in range(2):
            for head in range(heads):
                near_copy(kind, head).wait_recv()
        out_ref[...] = near_slot[1]

    out_ref[...] = jnp.zeros_like(out_ref)
    pl.when(place >= 1)(near_arrived)
    if has_far:

        def far_arrived():
            for head in range(heads):
                far_copy(head).wait_recv()
                out_ref[head] = out_ref[head] + kernel_dot(near_slot[0, head], far_slot[head])

        pl.when(place >= far)(far_arrived)

        def far_sent():
            for head in range(heads):
                far_copy(head).wait_send()

        pl.when(place + far < count)(far_sent)

    def near_sent():
        for kind in range(2):
            for head in range(heads):
                near_copy(kind, head).wait_send()

    pl.when(place + 1 < count)(near_sent)


def ctx_scan(maps):
    count = lax.axis_size("ctx")
    if count == 1:
        return jnp.zeros_like(maps[1])
    spans, far = scan_spans(count)
    side = maps.shape[1:]
    return pl.pallas_call(
        functools.partial(ctx_scan_kernel, count),
        out_shape=jax.ShapeDtypeStruct(side, jnp.float32),
        in_specs=[pl.BlockSpec(memory_space=pltpu.VMEM)],
        out_specs=pl.BlockSpec(memory_space=pltpu.VMEM),
        scratch_shapes=[
            pltpu.VMEM((2,) + maps.shape, jnp.float32),
            pltpu.VMEM((max(len(spans), 1),) + maps.shape, jnp.float32),
            pltpu.VMEM(maps.shape, jnp.float32),
            pltpu.VMEM(side, jnp.float32),
            pltpu.SemaphoreType.DMA((len(spans) + 2, 2 * maps.shape[1])),
            pltpu.SemaphoreType.DMA((len(spans) + 2, 2 * maps.shape[1])),
        ],
        compiler_params=pltpu.CompilerParams(collective_id=0, has_side_effects=True),
    )(maps)


def head_exchange_kernel(parts, count, source_view, target_view, *refs):
    sources, targets = refs[:count], refs[count : 2 * count]
    send_sems, recv_sems = refs[2 * count], refs[2 * count + 1]
    me = lax.axis_index("head")
    line = lax.axis_index("ctx")
    barrier = pltpu.get_barrier_semaphore()
    for peer in range(parts):

        @pl.when(me != peer)
        def _():
            pl.semaphore_signal(barrier, inc=1, device_id=(line, peer), device_id_type=MESH_IDS)

    pl.semaphore_wait(barrier, parts - 1)
    outgoing, incoming, local = [], [], []
    for index in range(count):
        for peer in range(parts):
            away = peer != me
            sending = pltpu.make_async_remote_copy(
                src_ref=source_view(sources[index], peer),
                dst_ref=target_view(targets[index], me),
                send_sem=send_sems.at[index, peer],
                recv_sem=recv_sems.at[index, me],
                device_id=(line, peer),
                device_id_type=MESH_IDS,
            )
            pl.when(away)(sending.start)
            staying = pltpu.make_async_copy(
                source_view(sources[index], peer),
                target_view(targets[index], peer),
                send_sems.at[index, peer],
            )
            pl.when(jnp.logical_not(away))(staying.start)
            arriving = pltpu.make_async_remote_copy(
                src_ref=source_view(sources[index], peer),
                dst_ref=target_view(targets[index], peer),
                send_sem=send_sems.at[index, peer],
                recv_sem=recv_sems.at[index, peer],
                device_id=(line, peer),
                device_id_type=MESH_IDS,
            )
            outgoing.append((away, sending))
            incoming.append((away, arriving))
            local.append((away, staying))
    for (away, sending), (_, arriving), (_, staying) in zip(outgoing, incoming, local):
        pl.when(away)(sending.wait_send)
        pl.when(away)(arriving.wait_recv)
        pl.when(jnp.logical_not(away))(staying.wait)


def head_exchange(arrays, target_shapes, source_view, target_view, collective):
    parts = lax.axis_size("head")
    count = len(arrays)
    return pl.pallas_call(
        functools.partial(head_exchange_kernel, parts, count, source_view, target_view),
        out_shape=[jax.ShapeDtypeStruct(shape, array.dtype) for shape, array in zip(target_shapes, arrays)],
        in_specs=[pl.BlockSpec(memory_space=pl.ANY)] * count,
        out_specs=[pl.BlockSpec(memory_space=pl.ANY)] * count,
        scratch_shapes=[
            pltpu.SemaphoreType.DMA((count, parts)),
            pltpu.SemaphoreType.DMA((count, parts)),
        ],
        compiler_params=pltpu.CompilerParams(collective_id=collective, has_side_effects=True),
    )(*arrays)


def columns_of(ref, peer):
    if len(ref.shape) == 3:
        return ref.at[peer]
    width = ref.shape[1] // lax.axis_size("head")
    return ref.at[:, pl.ds(peer * width, width)]


def rows_of(ref, peer):
    if len(ref.shape) == 3:
        return ref.at[peer]
    height = ref.shape[0] // lax.axis_size("head")
    return ref.at[pl.ds(peer * height, height), :]


def spread_heads(arrays):
    parts = lax.axis_size("head")
    shapes = [
        array.shape if array.ndim == 3 else (parts * array.shape[0], array.shape[1] // parts)
        for array in arrays
    ]
    return head_exchange(arrays, shapes, columns_of, rows_of, 1)


def gather_heads(array):
    parts = lax.axis_size("head")
    shape = (array.shape[0] // parts, array.shape[1] * parts)
    return head_exchange([array], [shape], rows_of, columns_of, 2)[0]


def on_device(
    query_rows,
    key_rows,
    value_rows,
    gate_rows,
    log_decay,
    write_strength,
    conv_query,
    conv_key,
    conv_value,
    norm_gain,
):
    parts = lax.axis_size("head")
    scalars = jnp.concatenate(
        [
            log_decay.reshape(log_decay.shape[0], parts, -1),
            write_strength.reshape(write_strength.shape[0], parts, -1),
        ],
        axis=2,
    ).transpose(1, 0, 2)
    device_query, local_key, local_value, moved_scalars = spread_heads(
        [query_rows, key_rows, value_rows, scalars]
    )
    moved_scalars = moved_scalars.reshape(-1, moved_scalars.shape[-1])
    split_at = log_decay.shape[1] // parts
    local_decay, local_strength = moved_scalars[:, :split_at], moved_scalars[:, split_at:]
    local_gate = lax.all_to_all(gate_rows, "head", split_axis=1, concat_axis=0, tiled=True)
    joined = jnp.concatenate([device_query, local_key, local_value], axis=1)
    kernel_width = conv_query.shape[0]
    count_rows = joined.shape[0]
    tail_rows = passed_along(joined[count_rows - (kernel_width - 1) :], "ctx", 1)
    weights_all = jnp.concatenate([conv_query, conv_key, conv_value], axis=1).astype(jnp.float32)
    mixed = causal_conv(joined.astype(jnp.float32), tail_rows.astype(jnp.float32), weights_all)
    key_width = device_query.shape[1]
    head_keys = key_width // DK
    per_key = HV // HK
    query_heads = jnp.repeat(
        unit_heads(mixed[:, :key_width], head_keys) * DK ** (-0.5), per_key, axis=1
    )
    key_heads = jnp.repeat(
        unit_heads(mixed[:, key_width : 2 * key_width], head_keys), per_key, axis=1
    )
    value_heads = mixed[:, 2 * key_width :].reshape(count_rows, -1, DV)
    terms = block_terms(
        into_blocks(query_heads, BLOCK),
        into_blocks(key_heads, BLOCK),
        into_blocks(value_heads, BLOCK),
        block_scalars(local_decay, BLOCK),
        block_scalars(local_strength, BLOCK),
    )
    key_part, value_part, within, query_decay, key_decay, end_decay = terms
    heads_here = key_part.shape[1]
    identity_mat = jnp.broadcast_to(jnp.eye(DK, dtype=jnp.float32), (heads_here, DK, DK))
    trans = end_decay[..., None, None] * identity_mat - matmul(
        "nhcd,nhce->nhde", key_decay, key_part
    )
    bias = matmul("nhcd,nhce->nhde", key_decay, value_part)
    blocks_here = trans.shape[0]
    span = 1
    while span < blocks_here:
        earlier_trans = jnp.concatenate(
            [jnp.broadcast_to(identity_mat, (span,) + identity_mat.shape), trans[:-span]], axis=0
        )
        earlier_bias = jnp.concatenate([jnp.zeros_like(bias[:span]), bias[:-span]], axis=0)
        trans, bias = (
            matmul("nhij,nhjk->nhik", trans, earlier_trans),
            matmul("nhij,nhjk->nhik", trans, earlier_bias) + bias,
        )
        span *= 2
    earlier_trans = jnp.concatenate([identity_mat[None], trans[:-1]], axis=0)
    earlier_bias = jnp.concatenate([jnp.zeros_like(bias[:1]), bias[:-1]], axis=0)
    corrected = value_part - matmul("nhcd,nhde->nhce", key_part, earlier_bias)
    local_result = matmul("nhcd,nhde->nhce", query_decay, earlier_bias) + matmul(
        "nhij,nhje->nhie", within, corrected
    )
    reach = query_decay - matmul("nhij,nhjd->nhid", within, key_part)
    carry_map = matmul("nhcd,nhde->nhce", reach, earlier_trans)
    total_trans, total_bias = trans[-1], bias[-1]
    initial = ctx_scan(jnp.stack([total_trans, total_bias]))
    produced = local_result + matmul("nhcd,hde->nhce", carry_map, initial)
    outputs = produced.transpose(0, 2, 1, 3).reshape(count_rows, heads_here, DV)
    gate = local_gate.astype(jnp.float32).reshape(count_rows, heads_here, DV)
    normed = gated_norm(outputs, gate, norm_gain)
    return gather_heads(normed)


def solution(mesh):
    in_specs = (
        P(("ctx", "head"), None),
        P(("ctx", "head"), None),
        P(("ctx", "head"), None),
        P(("ctx", "head"), None),
        P(("ctx", "head"), None),
        P(("ctx", "head"), None),
        P(None, "head"),
        P(None, "head"),
        P(None, "head"),
        P(),
    )
    out_specs = P(("ctx", "head"), None)
    return jax.shard_map(
        on_device, mesh=mesh, in_specs=in_specs, out_specs=out_specs, check_vma=False
    )
```

```python
import functools

import jax
import jax.numpy as jnp
from jax import lax
from jax.experimental import pallas as pl
from jax.experimental.pallas import tpu as pltpu
from jax.sharding import PartitionSpec as P

DK = 128
DV = 128
HK = 8
HV = 16
BLOCK = 64


HIGHEST_PRECISION = lax.Precision.HIGHEST
EPSILON = 1e-06
MATMUL_PRECISION = lax.Precision.HIGH


def passed_along(value, axis, steps):
    count = lax.axis_size(axis)
    leading, last = (max(0, -steps), min(count, count - steps))
    return lax.ppermute(value, axis, [(source, source + steps) for source in range(leading, last)])


def matmul(spec, left, right):
    return jnp.einsum(spec, left, right, precision=MATMUL_PRECISION)


def unit_lower_inverse(strict):
    size = strict.shape[-1]
    rows_index = jnp.arange(size)[:, None]
    cols_index = jnp.arange(size)[None, :]
    inverse = jnp.broadcast_to(jnp.eye(size, dtype=strict.dtype), strict.shape)
    width = 1
    while width < size:
        pick = (
            (rows_index // (2 * width) == cols_index // (2 * width))
            & ((rows_index // width) % 2 == 1)
            & ((cols_index // width) % 2 == 0)
        )
        lower = jnp.where(pick, strict, 0.0)
        step = matmul("...ij,...jk->...ik", inverse, matmul("...ij,...jk->...ik", lower, inverse))
        inverse = inverse - lax.optimization_barrier(step)
        width *= 2
    return inverse


def forward_substitution(coupling, targets):
    return matmul("...ij,...jf->...if", unit_lower_inverse(coupling), targets)


def causal_conv(inputs, earlier_rows, weights):
    kernel_width = weights.shape[0]
    count_rows = inputs.shape[0]
    joined = jnp.concatenate([earlier_rows, inputs], axis=0)
    result = joined[kernel_width - 1 :] * weights[kernel_width - 1]
    for offset in range(1, kernel_width):
        result = (
            result
            + joined[kernel_width - 1 - offset : kernel_width - 1 - offset + count_rows]
            * weights[kernel_width - 1 - offset]
        )
    return jax.nn.silu(result)


def unit_heads(mixed, heads):
    shaped = mixed.reshape(mixed.shape[0], heads, -1)
    return shaped / jnp.sqrt(jnp.sum(shaped * shaped, axis=-1, keepdims=True) + EPSILON)


def into_blocks(array, block_len):
    count_rows, heads, inner_dim = array.shape
    return array.reshape(count_rows // block_len, block_len, heads, inner_dim).transpose(0, 2, 1, 3)


def block_scalars(array, block_len):
    count_rows, heads = array.shape
    return (
        array.astype(jnp.float32)
        .reshape(count_rows // block_len, block_len, heads)
        .transpose(0, 2, 1)
    )


def block_terms(queries, keys, values, log_gate, strength):
    block_len = queries.shape[2]
    key_dim = keys.shape[-1]
    cumulative = jnp.cumsum(log_gate, axis=-1)
    rows_index = jnp.arange(block_len)[:, None]
    cols_index = jnp.arange(block_len)[None, :]
    causal = rows_index >= cols_index
    strictly = rows_index > cols_index
    spread = jnp.where(causal, cumulative[..., :, None] - cumulative[..., None, :], 0.0)
    decays = jnp.where(causal, jnp.exp(spread), 0.0)
    key_key = jnp.einsum("nhid,nhjd->nhij", keys, keys, precision=MATMUL_PRECISION)
    coupling = jnp.where(strictly, strength[..., None] * decays * key_key, 0.0)
    targets = jnp.concatenate(
        [(strength * jnp.exp(cumulative))[..., None] * keys, strength[..., None] * values], axis=-1
    )
    solved = forward_substitution(coupling, targets)
    key_part = solved[..., :key_dim]
    value_part = solved[..., key_dim:]
    query_key = jnp.einsum("nhid,nhjd->nhij", queries, keys, precision=MATMUL_PRECISION)
    within = query_key * decays
    query_decay = jnp.exp(cumulative)[..., None] * queries
    closing_logarithm = cumulative[..., -1:]
    key_decay = jnp.exp(closing_logarithm - cumulative)[..., None] * keys
    end_decay = jnp.exp(closing_logarithm[..., 0])
    return (key_part, value_part, within, query_decay, key_decay, end_decay)


def block_apply(memory, pieces):
    key_part, value_part, within, query_decay, key_decay, end_decay = pieces
    corrected = value_part - jnp.einsum(
        "hcd,hde->hce", key_part, memory, precision=HIGHEST_PRECISION
    )
    result = jnp.einsum("hcd,hde->hce", query_decay, memory, precision=HIGHEST_PRECISION)
    result = result + jnp.einsum("hij,hje->hie", within, corrected, precision=HIGHEST_PRECISION)
    memory = end_decay[:, None, None] * memory + jnp.einsum(
        "hcd,hce->hde", key_decay, corrected, precision=HIGHEST_PRECISION
    )
    return (memory, result)


def gated_norm(outputs, gate, gain):
    meansq = jnp.mean(outputs * outputs, axis=-1, keepdims=True)
    scaled = outputs / jnp.sqrt(meansq + EPSILON) * gain * jax.nn.silu(gate)
    return scaled.astype(jnp.bfloat16).reshape(outputs.shape[0], -1)


def compose_maps(later_map, earlier_map):
    return jnp.einsum("hij,hjk->hik", later_map, earlier_map, precision=HIGHEST_PRECISION)


MESH_IDS = pl.DeviceIdType.MESH


def scan_spans(count):
    spans = []
    span = 1
    while 2 * span < count:
        spans.append(span)
        span *= 2
    return spans, span + 1


def kernel_dot(left, right):
    return jnp.dot(left, right, preferred_element_type=jnp.float32, precision=HIGHEST_PRECISION)


def ctx_scan_kernel(count, maps_ref, out_ref, current, slots, near_slot, far_slot, send_sems, recv_sems):
    place = lax.axis_index("ctx")
    group = lax.axis_index("head")
    heads = maps_ref.shape[1]
    spans, far = scan_spans(count)
    rounds = len(spans)
    has_far = far < count
    offsets = sorted(set(spans + [1] + ([far] if has_far else [])))
    barrier = pltpu.get_barrier_semaphore()
    partners = jnp.int32(0)
    for offset in offsets:
        for target in (place + offset, place - offset):
            valid = jnp.logical_and(target >= 0, target < count)

            @pl.when(valid)
            def _():
                pl.semaphore_signal(barrier, inc=1, device_id=(target, group), device_id_type=MESH_IDS)

            partners = partners + valid.astype(jnp.int32)
    pl.semaphore_wait(barrier, partners)

    def result_of(index):
        return maps_ref if index < 0 else current.at[index % 2]

    def round_copy(index, kind, head):
        return pltpu.make_async_remote_copy(
            src_ref=result_of(index - 1).at[kind, head],
            dst_ref=slots.at[index, kind, head],
            send_sem=send_sems.at[index, kind * heads + head],
            recv_sem=recv_sems.at[index, kind * heads + head],
            device_id=(place + spans[index], group),
            device_id_type=MESH_IDS,
        )

    def near_copy(kind, head):
        return pltpu.make_async_remote_copy(
            src_ref=result_of(rounds - 1).at[kind, head],
            dst_ref=near_slot.at[kind, head],
            send_sem=send_sems.at[rounds, kind * heads + head],
            recv_sem=recv_sems.at[rounds, kind * heads + head],
            device_id=(place + 1, group),
            device_id_type=MESH_IDS,
        )

    def far_copy(head):
        return pltpu.make_async_remote_copy(
            src_ref=result_of(rounds - 1).at[1, head],
            dst_ref=far_slot.at[head],
            send_sem=send_sems.at[rounds + 1, head],
            recv_sem=recv_sems.at[rounds + 1, head],
            device_id=(place + far, group),
            device_id_type=MESH_IDS,
        )

    def launch_after(index, kind, head):
        following = index + 1
        if following < rounds:
            pl.when(place + spans[following] < count)(round_copy(following, kind, head).start)
        else:
            pl.when(place + 1 < count)(near_copy(kind, head).start)
            if has_far and kind == 1:
                pl.when(place + far < count)(far_copy(head).start)

    for kind in range(2):
        for head in range(heads):
            launch_after(-1, kind, head)

    for index, span in enumerate(spans):
        source = result_of(index - 1)
        dest = result_of(index)
        receiving = place >= span

        def composed(index=index, source=source, dest=dest):
            for head in range(heads):
                round_copy(index, 0, head).wait_recv()
                dest[0, head] = kernel_dot(source[0, head], slots[index, 0, head])
                launch_after(index, 0, head)
                round_copy(index, 1, head).wait_recv()
                dest[1, head] = kernel_dot(source[0, head], slots[index, 1, head]) + source[1, head]
                launch_after(index, 1, head)

        def kept(index=index, source=source, dest=dest):
            dest[...] = source[...]
            for kind in range(2):
                for head in range(heads):
                    launch_after(index, kind, head)

        pl.when(receiving)(composed)
        pl.when(jnp.logical_not(receiving))(kept)

        def sent(index=index):
            for kind in range(2):
                for head in range(heads):
                    round_copy(index, kind, head).wait_send()

        pl.when(place + span < count)(sent)

    def near_arrived():
        for kind in range(2):
            for head in range(heads):
                near_copy(kind, head).wait_recv()
        out_ref[...] = near_slot[1]

    out_ref[...] = jnp.zeros_like(out_ref)
    pl.when(place >= 1)(near_arrived)
    if has_far:

        def far_arrived():
            for head in range(heads):
                far_copy(head).wait_recv()
                out_ref[head] = out_ref[head] + kernel_dot(near_slot[0, head], far_slot[head])

        pl.when(place >= far)(far_arrived)

        def far_sent():
            for head in range(heads):
                far_copy(head).wait_send()

        pl.when(place + far < count)(far_sent)

    def near_sent():
        for kind in range(2):
            for head in range(heads):
                near_copy(kind, head).wait_send()

    pl.when(place + 1 < count)(near_sent)


def ctx_scan(maps):
    count = lax.axis_size("ctx")
    if count == 1:
        return jnp.zeros_like(maps[1])
    spans, far = scan_spans(count)
    side = maps.shape[1:]
    return pl.pallas_call(
        functools.partial(ctx_scan_kernel, count),
        out_shape=jax.ShapeDtypeStruct(side, jnp.float32),
        in_specs=[pl.BlockSpec(memory_space=pltpu.VMEM)],
        out_specs=pl.BlockSpec(memory_space=pltpu.VMEM),
        scratch_shapes=[
            pltpu.VMEM((2,) + maps.shape, jnp.float32),
            pltpu.VMEM((max(len(spans), 1),) + maps.shape, jnp.float32),
            pltpu.VMEM(maps.shape, jnp.float32),
            pltpu.VMEM(side, jnp.float32),
            pltpu.SemaphoreType.DMA((len(spans) + 2, 2 * maps.shape[1])),
            pltpu.SemaphoreType.DMA((len(spans) + 2, 2 * maps.shape[1])),
        ],
        compiler_params=pltpu.CompilerParams(collective_id=0, has_side_effects=True),
    )(maps)


def head_exchange_kernel(parts, plan, count, *refs):
    sources, targets = refs[:count], refs[count:-2]
    send_sems, recv_sems = refs[-2], refs[-1]
    me = lax.axis_index("head")
    line = lax.axis_index("ctx")
    barrier = pltpu.get_barrier_semaphore()
    for peer in range(parts):

        @pl.when(me != peer)
        def _():
            pl.semaphore_signal(barrier, inc=1, device_id=(line, peer), device_id_type=MESH_IDS)

    pl.semaphore_wait(barrier, parts - 1)
    pending = []
    for index, (source_at, target_at, source_view, target_view) in enumerate(plan):
        for peer in range(parts):
            away = peer != me
            sending = pltpu.make_async_remote_copy(
                src_ref=source_view(sources[source_at], peer),
                dst_ref=target_view(targets[target_at], me),
                send_sem=send_sems.at[index, peer],
                recv_sem=recv_sems.at[index, me],
                device_id=(line, peer),
                device_id_type=MESH_IDS,
            )
            pl.when(away)(sending.start)
            staying = pltpu.make_async_copy(
                source_view(sources[source_at], peer),
                target_view(targets[target_at], peer),
                send_sems.at[index, peer],
            )
            pl.when(jnp.logical_not(away))(staying.start)
            arriving = pltpu.make_async_remote_copy(
                src_ref=source_view(sources[source_at], peer),
                dst_ref=target_view(targets[target_at], peer),
                send_sem=send_sems.at[index, peer],
                recv_sem=recv_sems.at[index, peer],
                device_id=(line, peer),
                device_id_type=MESH_IDS,
            )
            pending.append((away, sending, arriving, staying))
    for away, sending, arriving, staying in pending:
        pl.when(away)(sending.wait_send)
        pl.when(away)(arriving.wait_recv)
        pl.when(jnp.logical_not(away))(staying.wait)


def head_exchange(arrays, target_specs, plan, collective):
    parts = lax.axis_size("head")
    count = len(arrays)
    return pl.pallas_call(
        functools.partial(head_exchange_kernel, parts, plan, count),
        out_shape=[jax.ShapeDtypeStruct(shape, dtype) for shape, dtype in target_specs],
        in_specs=[pl.BlockSpec(memory_space=pl.ANY)] * count,
        out_specs=[pl.BlockSpec(memory_space=pl.ANY)] * len(target_specs),
        scratch_shapes=[
            pltpu.SemaphoreType.DMA((len(plan), parts)),
            pltpu.SemaphoreType.DMA((len(plan), parts)),
        ],
        compiler_params=pltpu.CompilerParams(collective_id=collective, has_side_effects=True),
    )(*arrays)


def columns_of(ref, peer):
    if len(ref.shape) == 3:
        return ref.at[peer]
    width = ref.shape[1] // lax.axis_size("head")
    return ref.at[:, pl.ds(peer * width, width)]


def rows_of(ref, peer):
    if len(ref.shape) == 3:
        return ref.at[peer]
    height = ref.shape[0] // lax.axis_size("head")
    return ref.at[pl.ds(peer * height, height), :]


def block_of(ref, peer):
    return ref.at[peer]


def spread_heads(joined_parts, scalars):
    parts = lax.axis_size("head")
    rows = joined_parts[0].shape[0]
    widths = [array.shape[1] // parts for array in joined_parts]
    plan = []
    for index, width in enumerate(widths):
        offset = sum(widths[:index])

        def placed(ref, peer, offset=offset, width=width):
            return ref.at[pl.ds(peer * rows, rows), pl.ds(offset, width)]

        plan.append((index, 0, columns_of, placed))
    plan.append((len(joined_parts), 1, block_of, block_of))
    specs = [((parts * rows, sum(widths)), joined_parts[0].dtype), (scalars.shape, scalars.dtype)]
    return head_exchange(list(joined_parts) + [scalars], specs, plan, 1)


def gather_heads(array):
    parts = lax.axis_size("head")
    shape = (array.shape[0] // parts, array.shape[1] * parts)
    return head_exchange([array], [(shape, array.dtype)], [(0, 0, rows_of, columns_of)], 2)[0]


def on_device(
    query_rows,
    key_rows,
    value_rows,
    gate_rows,
    log_decay,
    write_strength,
    conv_query,
    conv_key,
    conv_value,
    norm_gain,
):
    parts = lax.axis_size("head")
    scalars = jnp.concatenate(
        [
            log_decay.reshape(log_decay.shape[0], parts, -1),
            write_strength.reshape(write_strength.shape[0], parts, -1),
        ],
        axis=2,
    ).transpose(1, 0, 2)
    joined, moved_scalars = spread_heads([query_rows, key_rows, value_rows], scalars)
    moved_scalars = moved_scalars.reshape(-1, moved_scalars.shape[-1])
    split_at = log_decay.shape[1] // parts
    local_decay, local_strength = moved_scalars[:, :split_at], moved_scalars[:, split_at:]
    local_gate = lax.all_to_all(gate_rows, "head", split_axis=1, concat_axis=0, tiled=True)
    kernel_width = conv_query.shape[0]
    count_rows = joined.shape[0]
    tail_rows = passed_along(joined[count_rows - (kernel_width - 1) :], "ctx", 1)
    weights_all = jnp.concatenate([conv_query, conv_key, conv_value], axis=1).astype(jnp.float32)
    mixed = causal_conv(joined.astype(jnp.float32), tail_rows.astype(jnp.float32), weights_all)
    key_width = query_rows.shape[1] // parts
    head_keys = key_width // DK
    per_key = HV // HK
    query_heads = jnp.repeat(
        unit_heads(mixed[:, :key_width], head_keys) * DK ** (-0.5), per_key, axis=1
    )
    key_heads = jnp.repeat(
        unit_heads(mixed[:, key_width : 2 * key_width], head_keys), per_key, axis=1
    )
    value_heads = mixed[:, 2 * key_width :].reshape(count_rows, -1, DV)
    terms = block_terms(
        into_blocks(query_heads, BLOCK),
        into_blocks(key_heads, BLOCK),
        into_blocks(value_heads, BLOCK),
        block_scalars(local_decay, BLOCK),
        block_scalars(local_strength, BLOCK),
    )
    key_part, value_part, within, query_decay, key_decay, end_decay = terms
    heads_here = key_part.shape[1]
    identity_mat = jnp.broadcast_to(jnp.eye(DK, dtype=jnp.float32), (heads_here, DK, DK))
    trans = end_decay[..., None, None] * identity_mat - matmul(
        "nhcd,nhce->nhde", key_decay, key_part
    )
    bias = matmul("nhcd,nhce->nhde", key_decay, value_part)
    blocks_here = trans.shape[0]
    span = 1
    while span < blocks_here:
        earlier_trans = jnp.concatenate(
            [jnp.broadcast_to(identity_mat, (span,) + identity_mat.shape), trans[:-span]], axis=0
        )
        earlier_bias = jnp.concatenate([jnp.zeros_like(bias[:span]), bias[:-span]], axis=0)
        trans, bias = (
            matmul("nhij,nhjk->nhik", trans, earlier_trans),
            matmul("nhij,nhjk->nhik", trans, earlier_bias) + bias,
        )
        span *= 2
    earlier_trans = jnp.concatenate([identity_mat[None], trans[:-1]], axis=0)
    earlier_bias = jnp.concatenate([jnp.zeros_like(bias[:1]), bias[:-1]], axis=0)
    corrected = value_part - matmul("nhcd,nhde->nhce", key_part, earlier_bias)
    local_result = matmul("nhcd,nhde->nhce", query_decay, earlier_bias) + matmul(
        "nhij,nhje->nhie", within, corrected
    )
    reach = query_decay - matmul("nhij,nhjd->nhid", within, key_part)
    carry_map = matmul("nhcd,nhde->nhce", reach, earlier_trans)
    total_trans, total_bias = trans[-1], bias[-1]
    initial = ctx_scan(jnp.stack([total_trans, total_bias]))
    produced = local_result + matmul("nhcd,hde->nhce", carry_map, initial)
    outputs = produced.transpose(0, 2, 1, 3).reshape(count_rows, heads_here, DV)
    gate = local_gate.astype(jnp.float32).reshape(count_rows, heads_here, DV)
    normed = gated_norm(outputs, gate, norm_gain)
    return gather_heads(normed)


def solution(mesh):
    in_specs = (
        P(("ctx", "head"), None),
        P(("ctx", "head"), None),
        P(("ctx", "head"), None),
        P(("ctx", "head"), None),
        P(("ctx", "head"), None),
        P(("ctx", "head"), None),
        P(None, "head"),
        P(None, "head"),
        P(None, "head"),
        P(),
    )
    out_specs = P(("ctx", "head"), None)
    return jax.shard_map(
        on_device, mesh=mesh, in_specs=in_specs, out_specs=out_specs, check_vma=False
    )
```

```python
import functools

import jax
import jax.numpy as jnp
from jax import lax
from jax.experimental import pallas as pl
from jax.experimental.pallas import tpu as pltpu
from jax.sharding import PartitionSpec as P

DK = 128
DV = 128
HK = 8
HV = 16
BLOCK = 64


HIGHEST_PRECISION = lax.Precision.HIGHEST
EPSILON = 1e-06
MATMUL_PRECISION = lax.Precision.HIGH


def passed_along(value, axis, steps):
    count = lax.axis_size(axis)
    leading, last = (max(0, -steps), min(count, count - steps))
    return lax.ppermute(value, axis, [(source, source + steps) for source in range(leading, last)])


def matmul(spec, left, right):
    return jnp.einsum(spec, left, right, precision=MATMUL_PRECISION)


def unit_lower_inverse(strict):
    size = strict.shape[-1]
    rows_index = jnp.arange(size)[:, None]
    cols_index = jnp.arange(size)[None, :]
    levels = max(size - 1, 1).bit_length()

    def level(step, inverse):
        width = jnp.left_shift(jnp.int32(1), step)
        pick = (
            (rows_index // (2 * width) == cols_index // (2 * width))
            & ((rows_index // width) % 2 == 1)
            & ((cols_index // width) % 2 == 0)
        )
        lower = jnp.where(pick, strict, 0.0)
        update = matmul("...ij,...jk->...ik", inverse, matmul("...ij,...jk->...ik", lower, inverse))
        return inverse - lax.optimization_barrier(update)

    start = jnp.broadcast_to(jnp.eye(size, dtype=strict.dtype), strict.shape)
    return lax.fori_loop(0, levels, level, start)


def forward_substitution(coupling, targets):
    return matmul("...ij,...jf->...if", unit_lower_inverse(coupling), targets)


def causal_conv(inputs, earlier_rows, weights):
    kernel_width = weights.shape[0]
    count_rows = inputs.shape[0]
    joined = jnp.concatenate([earlier_rows, inputs], axis=0)
    result = joined[kernel_width - 1 :] * weights[kernel_width - 1]
    for offset in range(1, kernel_width):
        result = (
            result
            + joined[kernel_width - 1 - offset : kernel_width - 1 - offset + count_rows]
            * weights[kernel_width - 1 - offset]
        )
    return jax.nn.silu(result)


def unit_heads(mixed, heads):
    shaped = mixed.reshape(mixed.shape[0], heads, -1)
    return shaped / jnp.sqrt(jnp.sum(shaped * shaped, axis=-1, keepdims=True) + EPSILON)


def into_blocks(array, block_len):
    count_rows, heads, inner_dim = array.shape
    return array.reshape(count_rows // block_len, block_len, heads, inner_dim).transpose(0, 2, 1, 3)


def block_scalars(array, block_len):
    count_rows, heads = array.shape
    return (
        array.astype(jnp.float32)
        .reshape(count_rows // block_len, block_len, heads)
        .transpose(0, 2, 1)
    )


def block_terms(queries, keys, values, log_gate, strength):
    block_len = queries.shape[2]
    key_dim = keys.shape[-1]
    cumulative = jnp.cumsum(log_gate, axis=-1)
    rows_index = jnp.arange(block_len)[:, None]
    cols_index = jnp.arange(block_len)[None, :]
    causal = rows_index >= cols_index
    strictly = rows_index > cols_index
    spread = jnp.where(causal, cumulative[..., :, None] - cumulative[..., None, :], 0.0)
    decays = jnp.where(causal, jnp.exp(spread), 0.0)
    key_key = jnp.einsum("nhid,nhjd->nhij", keys, keys, precision=MATMUL_PRECISION)
    coupling = jnp.where(strictly, strength[..., None] * decays * key_key, 0.0)
    targets = jnp.concatenate(
        [(strength * jnp.exp(cumulative))[..., None] * keys, strength[..., None] * values], axis=-1
    )
    solved = forward_substitution(coupling, targets)
    key_part = solved[..., :key_dim]
    value_part = solved[..., key_dim:]
    query_key = jnp.einsum("nhid,nhjd->nhij", queries, keys, precision=MATMUL_PRECISION)
    within = query_key * decays
    query_decay = jnp.exp(cumulative)[..., None] * queries
    closing_logarithm = cumulative[..., -1:]
    key_decay = jnp.exp(closing_logarithm - cumulative)[..., None] * keys
    end_decay = jnp.exp(closing_logarithm[..., 0])
    return (key_part, value_part, within, query_decay, key_decay, end_decay)


def block_apply(memory, pieces):
    key_part, value_part, within, query_decay, key_decay, end_decay = pieces
    corrected = value_part - jnp.einsum(
        "hcd,hde->hce", key_part, memory, precision=HIGHEST_PRECISION
    )
    result = jnp.einsum("hcd,hde->hce", query_decay, memory, precision=HIGHEST_PRECISION)
    result = result + jnp.einsum("hij,hje->hie", within, corrected, precision=HIGHEST_PRECISION)
    memory = end_decay[:, None, None] * memory + jnp.einsum(
        "hcd,hce->hde", key_decay, corrected, precision=HIGHEST_PRECISION
    )
    return (memory, result)


def gated_norm(outputs, gate, gain):
    meansq = jnp.mean(outputs * outputs, axis=-1, keepdims=True)
    scaled = outputs / jnp.sqrt(meansq + EPSILON) * gain * jax.nn.silu(gate)
    return scaled.astype(jnp.bfloat16).reshape(outputs.shape[0], -1)


def compose_maps(later_map, earlier_map):
    return jnp.einsum("hij,hjk->hik", later_map, earlier_map, precision=HIGHEST_PRECISION)


MESH_IDS = pl.DeviceIdType.MESH


def scan_spans(count):
    spans = []
    span = 1
    while 2 * span < count:
        spans.append(span)
        span *= 2
    return spans, span + 1


def kernel_dot(left, right):
    return jnp.dot(left, right, preferred_element_type=jnp.float32, precision=HIGHEST_PRECISION)


def ctx_scan_kernel(count, maps_ref, out_ref, current, slots, near_slot, far_slot, send_sems, recv_sems):
    place = lax.axis_index("ctx")
    group = lax.axis_index("head")
    heads = maps_ref.shape[1]
    spans, far = scan_spans(count)
    rounds = len(spans)
    has_far = far < count
    offsets = sorted(set(spans + [1] + ([far] if has_far else [])))
    barrier = pltpu.get_barrier_semaphore()
    partners = jnp.int32(0)
    for offset in offsets:
        for target in (place + offset, place - offset):
            valid = jnp.logical_and(target >= 0, target < count)

            @pl.when(valid)
            def _():
                pl.semaphore_signal(barrier, inc=1, device_id=(target, group), device_id_type=MESH_IDS)

            partners = partners + valid.astype(jnp.int32)
    pl.semaphore_wait(barrier, partners)

    def result_of(index):
        return maps_ref if index < 0 else current.at[index % 2]

    def round_copy(index, kind, head):
        return pltpu.make_async_remote_copy(
            src_ref=result_of(index - 1).at[kind, head],
            dst_ref=slots.at[index, kind, head],
            send_sem=send_sems.at[index, kind * heads + head],
            recv_sem=recv_sems.at[index, kind * heads + head],
            device_id=(place + spans[index], group),
            device_id_type=MESH_IDS,
        )

    def near_copy(kind, head):
        return pltpu.make_async_remote_copy(
            src_ref=result_of(rounds - 1).at[kind, head],
            dst_ref=near_slot.at[kind, head],
            send_sem=send_sems.at[rounds, kind * heads + head],
            recv_sem=recv_sems.at[rounds, kind * heads + head],
            device_id=(place + 1, group),
            device_id_type=MESH_IDS,
        )

    def far_copy(head):
        return pltpu.make_async_remote_copy(
            src_ref=result_of(rounds - 1).at[1, head],
            dst_ref=far_slot.at[head],
            send_sem=send_sems.at[rounds + 1, head],
            recv_sem=recv_sems.at[rounds + 1, head],
            device_id=(place + far, group),
            device_id_type=MESH_IDS,
        )

    def launch_after(index, kind, head):
        following = index + 1
        if following < rounds:
            pl.when(place + spans[following] < count)(round_copy(following, kind, head).start)
        else:
            pl.when(place + 1 < count)(near_copy(kind, head).start)
            if has_far and kind == 1:
                pl.when(place + far < count)(far_copy(head).start)

    for kind in range(2):
        for head in range(heads):
            launch_after(-1, kind, head)

    for index, span in enumerate(spans):
        source = result_of(index - 1)
        dest = result_of(index)
        receiving = place >= span

        def composed(index=index, source=source, dest=dest):
            for head in range(heads):
                round_copy(index, 0, head).wait_recv()
                dest[0, head] = kernel_dot(source[0, head], slots[index, 0, head])
                launch_after(index, 0, head)
                round_copy(index, 1, head).wait_recv()
                dest[1, head] = kernel_dot(source[0, head], slots[index, 1, head]) + source[1, head]
                launch_after(index, 1, head)

        def kept(index=index, source=source, dest=dest):
            dest[...] = source[...]
            for kind in range(2):
                for head in range(heads):
                    launch_after(index, kind, head)

        pl.when(receiving)(composed)
        pl.when(jnp.logical_not(receiving))(kept)

        def sent(index=index):
            for kind in range(2):
                for head in range(heads):
                    round_copy(index, kind, head).wait_send()

        pl.when(place + span < count)(sent)

    def near_arrived():
        for kind in range(2):
            for head in range(heads):
                near_copy(kind, head).wait_recv()
        out_ref[...] = near_slot[1]

    out_ref[...] = jnp.zeros_like(out_ref)
    pl.when(place >= 1)(near_arrived)
    if has_far:

        def far_arrived():
            for head in range(heads):
                far_copy(head).wait_recv()
                out_ref[head] = out_ref[head] + kernel_dot(near_slot[0, head], far_slot[head])

        pl.when(place >= far)(far_arrived)

        def far_sent():
            for head in range(heads):
                far_copy(head).wait_send()

        pl.when(place + far < count)(far_sent)

    def near_sent():
        for kind in range(2):
            for head in range(heads):
                near_copy(kind, head).wait_send()

    pl.when(place + 1 < count)(near_sent)


def ctx_scan(maps):
    count = lax.axis_size("ctx")
    if count == 1:
        return jnp.zeros_like(maps[1])
    spans, far = scan_spans(count)
    side = maps.shape[1:]
    return pl.pallas_call(
        functools.partial(ctx_scan_kernel, count),
        out_shape=jax.ShapeDtypeStruct(side, jnp.float32),
        in_specs=[pl.BlockSpec(memory_space=pltpu.VMEM)],
        out_specs=pl.BlockSpec(memory_space=pltpu.VMEM),
        scratch_shapes=[
            pltpu.VMEM((2,) + maps.shape, jnp.float32),
            pltpu.VMEM((max(len(spans), 1),) + maps.shape, jnp.float32),
            pltpu.VMEM(maps.shape, jnp.float32),
            pltpu.VMEM(side, jnp.float32),
            pltpu.SemaphoreType.DMA((len(spans) + 2, 2 * maps.shape[1])),
            pltpu.SemaphoreType.DMA((len(spans) + 2, 2 * maps.shape[1])),
        ],
        compiler_params=pltpu.CompilerParams(collective_id=0, has_side_effects=True),
    )(maps)


def head_exchange_kernel(parts, plan, count, *refs):
    sources, targets = refs[:count], refs[count:-2]
    send_sems, recv_sems = refs[-2], refs[-1]
    me = lax.axis_index("head")
    line = lax.axis_index("ctx")
    barrier = pltpu.get_barrier_semaphore()
    for peer in range(parts):

        @pl.when(me != peer)
        def _():
            pl.semaphore_signal(barrier, inc=1, device_id=(line, peer), device_id_type=MESH_IDS)

    pl.semaphore_wait(barrier, parts - 1)
    pending = []
    for index, (source_at, target_at, source_view, target_view) in enumerate(plan):
        for peer in range(parts):
            away = peer != me
            sending = pltpu.make_async_remote_copy(
                src_ref=source_view(sources[source_at], peer),
                dst_ref=target_view(targets[target_at], me),
                send_sem=send_sems.at[index, peer],
                recv_sem=recv_sems.at[index, me],
                device_id=(line, peer),
                device_id_type=MESH_IDS,
            )
            pl.when(away)(sending.start)
            staying = pltpu.make_async_copy(
                source_view(sources[source_at], peer),
                target_view(targets[target_at], peer),
                send_sems.at[index, peer],
            )
            pl.when(jnp.logical_not(away))(staying.start)
            arriving = pltpu.make_async_remote_copy(
                src_ref=source_view(sources[source_at], peer),
                dst_ref=target_view(targets[target_at], peer),
                send_sem=send_sems.at[index, peer],
                recv_sem=recv_sems.at[index, peer],
                device_id=(line, peer),
                device_id_type=MESH_IDS,
            )
            pending.append((away, sending, arriving, staying))
    for away, sending, arriving, staying in pending:
        pl.when(away)(sending.wait_send)
        pl.when(away)(arriving.wait_recv)
        pl.when(jnp.logical_not(away))(staying.wait)


def head_exchange(arrays, target_specs, plan, collective):
    parts = lax.axis_size("head")
    count = len(arrays)
    return pl.pallas_call(
        functools.partial(head_exchange_kernel, parts, plan, count),
        out_shape=[jax.ShapeDtypeStruct(shape, dtype) for shape, dtype in target_specs],
        in_specs=[pl.BlockSpec(memory_space=pl.ANY)] * count,
        out_specs=[pl.BlockSpec(memory_space=pl.ANY)] * len(target_specs),
        scratch_shapes=[
            pltpu.SemaphoreType.DMA((len(plan), parts)),
            pltpu.SemaphoreType.DMA((len(plan), parts)),
        ],
        compiler_params=pltpu.CompilerParams(collective_id=collective, has_side_effects=True),
    )(*arrays)


def columns_of(ref, peer):
    if len(ref.shape) == 3:
        return ref.at[peer]
    width = ref.shape[1] // lax.axis_size("head")
    return ref.at[:, pl.ds(peer * width, width)]


def rows_of(ref, peer):
    if len(ref.shape) == 3:
        return ref.at[peer]
    height = ref.shape[0] // lax.axis_size("head")
    return ref.at[pl.ds(peer * height, height), :]


def block_of(ref, peer):
    return ref.at[peer]


def spread_heads(joined_parts, scalars):
    parts = lax.axis_size("head")
    rows = joined_parts[0].shape[0]
    widths = [array.shape[1] // parts for array in joined_parts]
    plan = []
    for index, width in enumerate(widths):
        offset = sum(widths[:index])

        def placed(ref, peer, offset=offset, width=width):
            return ref.at[pl.ds(peer * rows, rows), pl.ds(offset, width)]

        plan.append((index, 0, columns_of, placed))
    plan.append((len(joined_parts), 1, block_of, block_of))
    specs = [((parts * rows, sum(widths)), joined_parts[0].dtype), (scalars.shape, scalars.dtype)]
    return head_exchange(list(joined_parts) + [scalars], specs, plan, 1)


def gather_heads(array):
    parts = lax.axis_size("head")
    shape = (array.shape[0] // parts, array.shape[1] * parts)
    return head_exchange([array], [(shape, array.dtype)], [(0, 0, rows_of, columns_of)], 2)[0]


def on_device(
    query_rows,
    key_rows,
    value_rows,
    gate_rows,
    log_decay,
    write_strength,
    conv_query,
    conv_key,
    conv_value,
    norm_gain,
):
    parts = lax.axis_size("head")
    scalars = jnp.concatenate(
        [
            log_decay.reshape(log_decay.shape[0], parts, -1),
            write_strength.reshape(write_strength.shape[0], parts, -1),
        ],
        axis=2,
    ).transpose(1, 0, 2)
    joined, moved_scalars = spread_heads([query_rows, key_rows, value_rows], scalars)
    moved_scalars = moved_scalars.reshape(-1, moved_scalars.shape[-1])
    split_at = log_decay.shape[1] // parts
    local_decay, local_strength = moved_scalars[:, :split_at], moved_scalars[:, split_at:]
    local_gate = lax.all_to_all(gate_rows, "head", split_axis=1, concat_axis=0, tiled=True)
    kernel_width = conv_query.shape[0]
    count_rows = joined.shape[0]
    tail_rows = passed_along(joined[count_rows - (kernel_width - 1) :], "ctx", 1)
    weights_all = jnp.concatenate([conv_query, conv_key, conv_value], axis=1).astype(jnp.float32)
    mixed = causal_conv(joined.astype(jnp.float32), tail_rows.astype(jnp.float32), weights_all)
    key_width = query_rows.shape[1] // parts
    head_keys = key_width // DK
    per_key = HV // HK
    query_heads = jnp.repeat(
        unit_heads(mixed[:, :key_width], head_keys) * DK ** (-0.5), per_key, axis=1
    )
    key_heads = jnp.repeat(
        unit_heads(mixed[:, key_width : 2 * key_width], head_keys), per_key, axis=1
    )
    value_heads = mixed[:, 2 * key_width :].reshape(count_rows, -1, DV)
    terms = block_terms(
        into_blocks(query_heads, BLOCK),
        into_blocks(key_heads, BLOCK),
        into_blocks(value_heads, BLOCK),
        block_scalars(local_decay, BLOCK),
        block_scalars(local_strength, BLOCK),
    )
    key_part, value_part, within, query_decay, key_decay, end_decay = terms
    heads_here = key_part.shape[1]
    identity_mat = jnp.broadcast_to(jnp.eye(DK, dtype=jnp.float32), (heads_here, DK, DK))
    trans = end_decay[..., None, None] * identity_mat - matmul(
        "nhcd,nhce->nhde", key_decay, key_part
    )
    bias = matmul("nhcd,nhce->nhde", key_decay, value_part)
    blocks_here = trans.shape[0]
    span = 1
    while span < blocks_here:
        earlier_trans = jnp.concatenate(
            [jnp.broadcast_to(identity_mat, (span,) + identity_mat.shape), trans[:-span]], axis=0
        )
        earlier_bias = jnp.concatenate([jnp.zeros_like(bias[:span]), bias[:-span]], axis=0)
        trans, bias = (
            matmul("nhij,nhjk->nhik", trans, earlier_trans),
            matmul("nhij,nhjk->nhik", trans, earlier_bias) + bias,
        )
        span *= 2
    earlier_trans = jnp.concatenate([identity_mat[None], trans[:-1]], axis=0)
    earlier_bias = jnp.concatenate([jnp.zeros_like(bias[:1]), bias[:-1]], axis=0)
    corrected = value_part - matmul("nhcd,nhde->nhce", key_part, earlier_bias)
    local_result = matmul("nhcd,nhde->nhce", query_decay, earlier_bias) + matmul(
        "nhij,nhje->nhie", within, corrected
    )
    reach = query_decay - matmul("nhij,nhjd->nhid", within, key_part)
    carry_map = matmul("nhcd,nhde->nhce", reach, earlier_trans)
    total_trans, total_bias = trans[-1], bias[-1]
    initial = ctx_scan(jnp.stack([total_trans, total_bias]))
    produced = local_result + matmul("nhcd,hde->nhce", carry_map, initial)
    outputs = produced.transpose(0, 2, 1, 3).reshape(count_rows, heads_here, DV)
    gate = local_gate.astype(jnp.float32).reshape(count_rows, heads_here, DV)
    normed = gated_norm(outputs, gate, norm_gain)
    return gather_heads(normed)


def solution(mesh):
    in_specs = (
        P(("ctx", "head"), None),
        P(("ctx", "head"), None),
        P(("ctx", "head"), None),
        P(("ctx", "head"), None),
        P(("ctx", "head"), None),
        P(("ctx", "head"), None),
        P(None, "head"),
        P(None, "head"),
        P(None, "head"),
        P(),
    )
    out_specs = P(("ctx", "head"), None)
    return jax.shard_map(
        on_device, mesh=mesh, in_specs=in_specs, out_specs=out_specs, check_vma=False
    )
```

```python
import functools

import jax
import jax.numpy as jnp
from jax import lax
from jax.experimental import pallas as pl
from jax.experimental.pallas import tpu as pltpu
from jax.sharding import PartitionSpec as P

DK = 128
DV = 128
HK = 8
HV = 16
BLOCK = 64


HIGHEST_PRECISION = lax.Precision.HIGHEST
EPSILON = 1e-06
MATMUL_PRECISION = lax.Precision.HIGH


def passed_along(value, axis, steps):
    count = lax.axis_size(axis)
    leading, last = (max(0, -steps), min(count, count - steps))
    return lax.ppermute(value, axis, [(source, source + steps) for source in range(leading, last)])


def matmul(spec, left, right):
    return jnp.einsum(spec, left, right, precision=MATMUL_PRECISION)


def unit_lower_inverse(strict):
    size = strict.shape[-1]
    rows_index = jnp.arange(size)[:, None]
    cols_index = jnp.arange(size)[None, :]
    levels = max(size - 1, 1).bit_length()

    def level(step, inverse):
        width = jnp.left_shift(jnp.int32(1), step)
        pick = (
            (rows_index // (2 * width) == cols_index // (2 * width))
            & ((rows_index // width) % 2 == 1)
            & ((cols_index // width) % 2 == 0)
        )
        lower = jnp.where(pick, strict, 0.0)
        update = matmul("...ij,...jk->...ik", inverse, matmul("...ij,...jk->...ik", lower, inverse))
        return inverse - lax.optimization_barrier(update)

    start = jnp.broadcast_to(jnp.eye(size, dtype=strict.dtype), strict.shape)
    return lax.fori_loop(0, levels, level, start)


def forward_substitution(coupling, targets):
    return matmul("...ij,...jf->...if", unit_lower_inverse(coupling), targets)


def causal_conv(inputs, earlier_rows, weights):
    kernel_width = weights.shape[0]
    count_rows = inputs.shape[0]
    joined = jnp.concatenate([earlier_rows, inputs], axis=0)
    result = joined[kernel_width - 1 :] * weights[kernel_width - 1]
    for offset in range(1, kernel_width):
        result = (
            result
            + joined[kernel_width - 1 - offset : kernel_width - 1 - offset + count_rows]
            * weights[kernel_width - 1 - offset]
        )
    return jax.nn.silu(result)


def unit_heads(mixed, heads):
    shaped = mixed.reshape(mixed.shape[0], heads, -1)
    return shaped / jnp.sqrt(jnp.sum(shaped * shaped, axis=-1, keepdims=True) + EPSILON)


def into_blocks(array, block_len):
    count_rows, heads, inner_dim = array.shape
    return array.reshape(count_rows // block_len, block_len, heads, inner_dim).transpose(0, 2, 1, 3)


def block_scalars(array, block_len):
    count_rows, heads = array.shape
    return (
        array.astype(jnp.float32)
        .reshape(count_rows // block_len, block_len, heads)
        .transpose(0, 2, 1)
    )


def block_terms(queries, keys, values, log_gate, strength):
    block_len = queries.shape[2]
    key_dim = keys.shape[-1]
    cumulative = jnp.cumsum(log_gate, axis=-1)
    rows_index = jnp.arange(block_len)[:, None]
    cols_index = jnp.arange(block_len)[None, :]
    causal = rows_index >= cols_index
    strictly = rows_index > cols_index
    spread = jnp.where(causal, cumulative[..., :, None] - cumulative[..., None, :], 0.0)
    decays = jnp.where(causal, jnp.exp(spread), 0.0)
    key_key = jnp.einsum("nhid,nhjd->nhij", keys, keys, precision=MATMUL_PRECISION)
    coupling = jnp.where(strictly, strength[..., None] * decays * key_key, 0.0)
    targets = jnp.concatenate(
        [(strength * jnp.exp(cumulative))[..., None] * keys, strength[..., None] * values], axis=-1
    )
    solved = forward_substitution(coupling, targets)
    key_part = solved[..., :key_dim]
    value_part = solved[..., key_dim:]
    query_key = jnp.einsum("nhid,nhjd->nhij", queries, keys, precision=MATMUL_PRECISION)
    within = query_key * decays
    query_decay = jnp.exp(cumulative)[..., None] * queries
    closing_logarithm = cumulative[..., -1:]
    key_decay = jnp.exp(closing_logarithm - cumulative)[..., None] * keys
    end_decay = jnp.exp(closing_logarithm[..., 0])
    return (key_part, value_part, within, query_decay, key_decay, end_decay)


def block_apply(memory, pieces):
    key_part, value_part, within, query_decay, key_decay, end_decay = pieces
    corrected = value_part - jnp.einsum(
        "hcd,hde->hce", key_part, memory, precision=HIGHEST_PRECISION
    )
    result = jnp.einsum("hcd,hde->hce", query_decay, memory, precision=HIGHEST_PRECISION)
    result = result + jnp.einsum("hij,hje->hie", within, corrected, precision=HIGHEST_PRECISION)
    memory = end_decay[:, None, None] * memory + jnp.einsum(
        "hcd,hce->hde", key_decay, corrected, precision=HIGHEST_PRECISION
    )
    return (memory, result)


def gated_norm(outputs, gate, gain):
    meansq = jnp.mean(outputs * outputs, axis=-1, keepdims=True)
    scaled = outputs / jnp.sqrt(meansq + EPSILON) * gain * jax.nn.silu(gate)
    return scaled.astype(jnp.bfloat16).reshape(outputs.shape[0], -1)


def compose_maps(later_map, earlier_map):
    return jnp.einsum("hij,hjk->hik", later_map, earlier_map, precision=HIGHEST_PRECISION)


MESH_IDS = pl.DeviceIdType.MESH


def scan_spans(count):
    spans = []
    span = 1
    while 2 * span < count:
        spans.append(span)
        span *= 2
    return spans, span + 1


def kernel_dot(left, right):
    return jnp.dot(left, right, preferred_element_type=jnp.float32, precision=HIGHEST_PRECISION)


def ctx_scan_kernel(count, maps_ref, out_ref, current, slots, near_slot, far_slot, send_sems, recv_sems):
    place = lax.axis_index("ctx")
    group = lax.axis_index("head")
    heads = maps_ref.shape[1]
    spans, far = scan_spans(count)
    rounds = len(spans)
    has_far = far < count
    offsets = sorted(set(spans + [1] + ([far] if has_far else [])))
    barrier = pltpu.get_barrier_semaphore()
    partners = jnp.int32(0)
    for offset in offsets:
        for target in (place + offset, place - offset):
            valid = jnp.logical_and(target >= 0, target < count)

            @pl.when(valid)
            def _():
                pl.semaphore_signal(barrier, inc=1, device_id=(target, group), device_id_type=MESH_IDS)

            partners = partners + valid.astype(jnp.int32)
    pl.semaphore_wait(barrier, partners)

    def result_of(index):
        return maps_ref if index < 0 else current.at[index % 2]

    def round_copy(index, kind, head):
        return pltpu.make_async_remote_copy(
            src_ref=result_of(index - 1).at[kind, head],
            dst_ref=slots.at[index, kind, head],
            send_sem=send_sems.at[index, kind * heads + head],
            recv_sem=recv_sems.at[index, kind * heads + head],
            device_id=(place + spans[index], group),
            device_id_type=MESH_IDS,
        )

    def near_copy(kind, head):
        return pltpu.make_async_remote_copy(
            src_ref=result_of(rounds - 1).at[kind, head],
            dst_ref=near_slot.at[kind, head],
            send_sem=send_sems.at[rounds, kind * heads + head],
            recv_sem=recv_sems.at[rounds, kind * heads + head],
            device_id=(place + 1, group),
            device_id_type=MESH_IDS,
        )

    def far_copy(head):
        return pltpu.make_async_remote_copy(
            src_ref=result_of(rounds - 1).at[1, head],
            dst_ref=far_slot.at[head],
            send_sem=send_sems.at[rounds + 1, head],
            recv_sem=recv_sems.at[rounds + 1, head],
            device_id=(place + far, group),
            device_id_type=MESH_IDS,
        )

    def launch_after(index, kind, head):
        following = index + 1
        if following < rounds:
            pl.when(place + spans[following] < count)(round_copy(following, kind, head).start)
        else:
            pl.when(place + 1 < count)(near_copy(kind, head).start)
            if has_far and kind == 1:
                pl.when(place + far < count)(far_copy(head).start)

    for kind in range(2):
        for head in range(heads):
            launch_after(-1, kind, head)

    for index, span in enumerate(spans):
        source = result_of(index - 1)
        dest = result_of(index)
        receiving = place >= span

        def composed(index=index, source=source, dest=dest):
            for head in range(heads):
                round_copy(index, 0, head).wait_recv()
                dest[0, head] = kernel_dot(source[0, head], slots[index, 0, head])
                launch_after(index, 0, head)
                round_copy(index, 1, head).wait_recv()
                dest[1, head] = kernel_dot(source[0, head], slots[index, 1, head]) + source[1, head]
                launch_after(index, 1, head)

        def kept(index=index, source=source, dest=dest):
            dest[...] = source[...]
            for kind in range(2):
                for head in range(heads):
                    launch_after(index, kind, head)

        pl.when(receiving)(composed)
        pl.when(jnp.logical_not(receiving))(kept)

        def sent(index=index):
            for kind in range(2):
                for head in range(heads):
                    round_copy(index, kind, head).wait_send()

        pl.when(place + span < count)(sent)

    def near_arrived():
        for kind in range(2):
            for head in range(heads):
                near_copy(kind, head).wait_recv()
        out_ref[...] = near_slot[1]

    out_ref[...] = jnp.zeros_like(out_ref)
    pl.when(place >= 1)(near_arrived)
    if has_far:

        def far_arrived():
            for head in range(heads):
                far_copy(head).wait_recv()
                out_ref[head] = out_ref[head] + kernel_dot(near_slot[0, head], far_slot[head])

        pl.when(place >= far)(far_arrived)

        def far_sent():
            for head in range(heads):
                far_copy(head).wait_send()

        pl.when(place + far < count)(far_sent)

    def near_sent():
        for kind in range(2):
            for head in range(heads):
                near_copy(kind, head).wait_send()

    pl.when(place + 1 < count)(near_sent)


def ctx_scan(maps):
    count = lax.axis_size("ctx")
    if count == 1:
        return jnp.zeros_like(maps[1])
    spans, far = scan_spans(count)
    side = maps.shape[1:]
    return pl.pallas_call(
        functools.partial(ctx_scan_kernel, count),
        out_shape=jax.ShapeDtypeStruct(side, jnp.float32),
        in_specs=[pl.BlockSpec(memory_space=pltpu.VMEM)],
        out_specs=pl.BlockSpec(memory_space=pltpu.VMEM),
        scratch_shapes=[
            pltpu.VMEM((2,) + maps.shape, jnp.float32),
            pltpu.VMEM((max(len(spans), 1),) + maps.shape, jnp.float32),
            pltpu.VMEM(maps.shape, jnp.float32),
            pltpu.VMEM(side, jnp.float32),
            pltpu.SemaphoreType.DMA((len(spans) + 2, 2 * maps.shape[1])),
            pltpu.SemaphoreType.DMA((len(spans) + 2, 2 * maps.shape[1])),
        ],
        compiler_params=pltpu.CompilerParams(collective_id=0, has_side_effects=True),
    )(maps)


def head_exchange_kernel(parts, plan, count, *refs):
    sources, targets = refs[:count], refs[count:-2]
    send_sems, recv_sems = refs[-2], refs[-1]
    me = lax.axis_index("head")
    line = lax.axis_index("ctx")
    barrier = pltpu.get_barrier_semaphore()
    for peer in range(parts):

        @pl.when(me != peer)
        def _():
            pl.semaphore_signal(barrier, inc=1, device_id=(line, peer), device_id_type=MESH_IDS)

    pl.semaphore_wait(barrier, parts - 1)
    pending = []
    for index, (source_at, target_at, source_view, target_view) in enumerate(plan):
        for peer in range(parts):
            away = peer != me
            sending = pltpu.make_async_remote_copy(
                src_ref=source_view(sources[source_at], peer),
                dst_ref=target_view(targets[target_at], me),
                send_sem=send_sems.at[index, peer],
                recv_sem=recv_sems.at[index, me],
                device_id=(line, peer),
                device_id_type=MESH_IDS,
            )
            pl.when(away)(sending.start)
            staying = pltpu.make_async_copy(
                source_view(sources[source_at], peer),
                target_view(targets[target_at], peer),
                send_sems.at[index, peer],
            )
            pl.when(jnp.logical_not(away))(staying.start)
            arriving = pltpu.make_async_remote_copy(
                src_ref=source_view(sources[source_at], peer),
                dst_ref=target_view(targets[target_at], peer),
                send_sem=send_sems.at[index, peer],
                recv_sem=recv_sems.at[index, peer],
                device_id=(line, peer),
                device_id_type=MESH_IDS,
            )
            pending.append((away, sending, arriving, staying))
    for away, sending, arriving, staying in pending:
        pl.when(away)(sending.wait_send)
        pl.when(away)(arriving.wait_recv)
        pl.when(jnp.logical_not(away))(staying.wait)


def head_exchange(arrays, target_specs, plan, collective):
    parts = lax.axis_size("head")
    count = len(arrays)
    return pl.pallas_call(
        functools.partial(head_exchange_kernel, parts, plan, count),
        out_shape=[jax.ShapeDtypeStruct(shape, dtype) for shape, dtype in target_specs],
        in_specs=[pl.BlockSpec(memory_space=pl.ANY)] * count,
        out_specs=[pl.BlockSpec(memory_space=pl.ANY)] * len(target_specs),
        scratch_shapes=[
            pltpu.SemaphoreType.DMA((len(plan), parts)),
            pltpu.SemaphoreType.DMA((len(plan), parts)),
        ],
        compiler_params=pltpu.CompilerParams(collective_id=collective, has_side_effects=True),
    )(*arrays)


def columns_of(ref, peer):
    if len(ref.shape) == 3:
        return ref.at[peer]
    width = ref.shape[1] // lax.axis_size("head")
    return ref.at[:, pl.ds(peer * width, width)]


def rows_of(ref, peer):
    if len(ref.shape) == 3:
        return ref.at[peer]
    height = ref.shape[0] // lax.axis_size("head")
    return ref.at[pl.ds(peer * height, height), :]


def block_of(ref, peer):
    return ref.at[peer]


def spread_heads(joined_parts, scalars):
    parts = lax.axis_size("head")
    rows = joined_parts[0].shape[0]
    widths = [array.shape[1] // parts for array in joined_parts]
    plan = []
    for index, width in enumerate(widths):
        offset = sum(widths[:index])

        def placed(ref, peer, offset=offset, width=width):
            return ref.at[pl.ds(peer * rows, rows), pl.ds(offset, width)]

        plan.append((index, 0, columns_of, placed))
    plan.append((len(joined_parts), 1, block_of, block_of))
    specs = [((parts * rows, sum(widths)), joined_parts[0].dtype), (scalars.shape, scalars.dtype)]
    return head_exchange(list(joined_parts) + [scalars], specs, plan, 1)


def gather_heads(array):
    parts = lax.axis_size("head")
    shape = (array.shape[0] // parts, array.shape[1] * parts)
    return head_exchange([array], [(shape, array.dtype)], [(0, 0, rows_of, columns_of)], 2)[0]


def on_device(
    query_rows,
    key_rows,
    value_rows,
    gate_rows,
    log_decay,
    write_strength,
    conv_query,
    conv_key,
    conv_value,
    norm_gain,
):
    parts = lax.axis_size("head")
    scalars = jnp.concatenate(
        [
            log_decay.reshape(log_decay.shape[0], parts, -1),
            write_strength.reshape(write_strength.shape[0], parts, -1),
        ],
        axis=2,
    ).transpose(1, 0, 2)
    joined, moved_scalars = spread_heads([query_rows, key_rows, value_rows], scalars)
    moved_scalars = moved_scalars.reshape(-1, moved_scalars.shape[-1])
    split_at = log_decay.shape[1] // parts
    local_decay, local_strength = moved_scalars[:, :split_at], moved_scalars[:, split_at:]
    local_gate = lax.all_to_all(gate_rows, "head", split_axis=1, concat_axis=0, tiled=True)
    kernel_width = conv_query.shape[0]
    count_rows = joined.shape[0]
    tail_rows = passed_along(joined[count_rows - (kernel_width - 1) :], "ctx", 1)
    weights_all = jnp.concatenate([conv_query, conv_key, conv_value], axis=1).astype(jnp.float32)
    mixed = causal_conv(joined, tail_rows, weights_all)
    key_width = query_rows.shape[1] // parts
    head_keys = key_width // DK
    per_key = HV // HK
    query_heads = jnp.repeat(
        unit_heads(mixed[:, :key_width], head_keys) * DK ** (-0.5), per_key, axis=1
    )
    key_heads = jnp.repeat(
        unit_heads(mixed[:, key_width : 2 * key_width], head_keys), per_key, axis=1
    )
    value_heads = mixed[:, 2 * key_width :].reshape(count_rows, -1, DV)
    terms = block_terms(
        into_blocks(query_heads, BLOCK),
        into_blocks(key_heads, BLOCK),
        into_blocks(value_heads, BLOCK),
        block_scalars(local_decay, BLOCK),
        block_scalars(local_strength, BLOCK),
    )
    key_part, value_part, within, query_decay, key_decay, end_decay = terms
    heads_here = key_part.shape[1]
    identity_mat = jnp.broadcast_to(jnp.eye(DK, dtype=jnp.float32), (heads_here, DK, DK))
    trans = end_decay[..., None, None] * identity_mat - matmul(
        "nhcd,nhce->nhde", key_decay, key_part
    )
    bias = matmul("nhcd,nhce->nhde", key_decay, value_part)
    blocks_here = trans.shape[0]
    span = 1
    while span < blocks_here:
        earlier_trans = jnp.concatenate(
            [jnp.broadcast_to(identity_mat, (span,) + identity_mat.shape), trans[:-span]], axis=0
        )
        earlier_bias = jnp.concatenate([jnp.zeros_like(bias[:span]), bias[:-span]], axis=0)
        trans, bias = (
            matmul("nhij,nhjk->nhik", trans, earlier_trans),
            matmul("nhij,nhjk->nhik", trans, earlier_bias) + bias,
        )
        span *= 2
    earlier_trans = jnp.concatenate([identity_mat[None], trans[:-1]], axis=0)
    earlier_bias = jnp.concatenate([jnp.zeros_like(bias[:1]), bias[:-1]], axis=0)
    corrected = value_part - matmul("nhcd,nhde->nhce", key_part, earlier_bias)
    local_result = matmul("nhcd,nhde->nhce", query_decay, earlier_bias) + matmul(
        "nhij,nhje->nhie", within, corrected
    )
    reach = query_decay - matmul("nhij,nhjd->nhid", within, key_part)
    carry_map = matmul("nhcd,nhde->nhce", reach, earlier_trans)
    total_trans, total_bias = trans[-1], bias[-1]
    initial = ctx_scan(jnp.stack([total_trans, total_bias]))
    produced = local_result + matmul("nhcd,hde->nhce", carry_map, initial)
    outputs = produced.transpose(0, 2, 1, 3).reshape(count_rows, heads_here, DV)
    gate = local_gate.astype(jnp.float32).reshape(count_rows, heads_here, DV)
    normed = gated_norm(outputs, gate, norm_gain)
    return gather_heads(normed)


def solution(mesh):
    in_specs = (
        P(("ctx", "head"), None),
        P(("ctx", "head"), None),
        P(("ctx", "head"), None),
        P(("ctx", "head"), None),
        P(("ctx", "head"), None),
        P(("ctx", "head"), None),
        P(None, "head"),
        P(None, "head"),
        P(None, "head"),
        P(),
    )
    out_specs = P(("ctx", "head"), None)
    return jax.shard_map(
        on_device, mesh=mesh, in_specs=in_specs, out_specs=out_specs, check_vma=False
    )
```

```python
import functools

import jax
import jax.numpy as jnp
from jax import lax
from jax.experimental import pallas as pl
from jax.experimental.pallas import tpu as pltpu
from jax.sharding import PartitionSpec as P

DK = 128
DV = 128
HK = 8
HV = 16
BLOCK = 64


HIGHEST_PRECISION = lax.Precision.HIGHEST
EPSILON = 1e-06
MATMUL_PRECISION = lax.Precision.HIGH


def passed_along(value, axis, steps):
    count = lax.axis_size(axis)
    leading, last = (max(0, -steps), min(count, count - steps))
    return lax.ppermute(value, axis, [(source, source + steps) for source in range(leading, last)])


def matmul(spec, left, right):
    return jnp.einsum(spec, left, right, precision=MATMUL_PRECISION)


def unit_lower_inverse(strict):
    size = strict.shape[-1]
    rows_index = jnp.arange(size)[:, None]
    cols_index = jnp.arange(size)[None, :]
    levels = max(size - 1, 1).bit_length()

    def level(step, inverse):
        width = jnp.left_shift(jnp.int32(1), step)
        pick = (
            (rows_index // (2 * width) == cols_index // (2 * width))
            & ((rows_index // width) % 2 == 1)
            & ((cols_index // width) % 2 == 0)
        )
        lower = jnp.where(pick, strict, 0.0)
        update = matmul("...ij,...jk->...ik", inverse, matmul("...ij,...jk->...ik", lower, inverse))
        return inverse - update

    start = jnp.broadcast_to(jnp.eye(size, dtype=strict.dtype), strict.shape)
    return lax.fori_loop(0, levels, level, start)


def forward_substitution(coupling, targets):
    return matmul("...ij,...jf->...if", unit_lower_inverse(coupling), targets)


def causal_conv(inputs, earlier_rows, weights):
    kernel_width = weights.shape[0]
    count_rows = inputs.shape[0]
    joined = jnp.concatenate([earlier_rows, inputs], axis=0)
    result = joined[kernel_width - 1 :] * weights[kernel_width - 1]
    for offset in range(1, kernel_width):
        result = (
            result
            + joined[kernel_width - 1 - offset : kernel_width - 1 - offset + count_rows]
            * weights[kernel_width - 1 - offset]
        )
    return jax.nn.silu(result)


def unit_heads(mixed, heads):
    shaped = mixed.reshape(mixed.shape[0], heads, -1)
    return shaped / jnp.sqrt(jnp.sum(shaped * shaped, axis=-1, keepdims=True) + EPSILON)


def into_blocks(array, block_len):
    count_rows, heads, inner_dim = array.shape
    return array.reshape(count_rows // block_len, block_len, heads, inner_dim).transpose(0, 2, 1, 3)


def block_scalars(array, block_len):
    count_rows, heads = array.shape
    return (
        array.astype(jnp.float32)
        .reshape(count_rows // block_len, block_len, heads)
        .transpose(0, 2, 1)
    )


def block_terms(queries, keys, values, log_gate, strength):
    block_len = queries.shape[2]
    key_dim = keys.shape[-1]
    cumulative = jnp.cumsum(log_gate, axis=-1)
    rows_index = jnp.arange(block_len)[:, None]
    cols_index = jnp.arange(block_len)[None, :]
    causal = rows_index >= cols_index
    strictly = rows_index > cols_index
    spread = jnp.where(causal, cumulative[..., :, None] - cumulative[..., None, :], 0.0)
    decays = jnp.where(causal, jnp.exp(spread), 0.0)
    key_key = jnp.einsum("nhid,nhjd->nhij", keys, keys, precision=MATMUL_PRECISION)
    coupling = jnp.where(strictly, strength[..., None] * decays * key_key, 0.0)
    targets = jnp.concatenate(
        [(strength * jnp.exp(cumulative))[..., None] * keys, strength[..., None] * values], axis=-1
    )
    solved = forward_substitution(coupling, targets)
    key_part = solved[..., :key_dim]
    value_part = solved[..., key_dim:]
    query_key = jnp.einsum("nhid,nhjd->nhij", queries, keys, precision=MATMUL_PRECISION)
    within = query_key * decays
    query_decay = jnp.exp(cumulative)[..., None] * queries
    closing_logarithm = cumulative[..., -1:]
    key_decay = jnp.exp(closing_logarithm - cumulative)[..., None] * keys
    end_decay = jnp.exp(closing_logarithm[..., 0])
    return (key_part, value_part, within, query_decay, key_decay, end_decay)


def block_apply(memory, pieces):
    key_part, value_part, within, query_decay, key_decay, end_decay = pieces
    corrected = value_part - jnp.einsum(
        "hcd,hde->hce", key_part, memory, precision=HIGHEST_PRECISION
    )
    result = jnp.einsum("hcd,hde->hce", query_decay, memory, precision=HIGHEST_PRECISION)
    result = result + jnp.einsum("hij,hje->hie", within, corrected, precision=HIGHEST_PRECISION)
    memory = end_decay[:, None, None] * memory + jnp.einsum(
        "hcd,hce->hde", key_decay, corrected, precision=HIGHEST_PRECISION
    )
    return (memory, result)


def gated_norm(outputs, gate, gain):
    meansq = jnp.mean(outputs * outputs, axis=-1, keepdims=True)
    scaled = outputs / jnp.sqrt(meansq + EPSILON) * gain * jax.nn.silu(gate)
    return scaled.astype(jnp.bfloat16).reshape(outputs.shape[0], -1)


def compose_maps(later_map, earlier_map):
    return jnp.einsum("hij,hjk->hik", later_map, earlier_map, precision=HIGHEST_PRECISION)


MESH_IDS = pl.DeviceIdType.MESH


def scan_spans(count):
    spans = []
    span = 1
    while 2 * span < count:
        spans.append(span)
        span *= 2
    return spans, span + 1


def kernel_dot(left, right):
    return jnp.dot(left, right, preferred_element_type=jnp.float32, precision=HIGHEST_PRECISION)


def ctx_scan_kernel(count, maps_ref, out_ref, current, slots, near_slot, far_slot, send_sems, recv_sems):
    place = lax.axis_index("ctx")
    group = lax.axis_index("head")
    heads = maps_ref.shape[1]
    spans, far = scan_spans(count)
    rounds = len(spans)
    has_far = far < count
    offsets = sorted(set(spans + [1] + ([far] if has_far else [])))
    barrier = pltpu.get_barrier_semaphore()
    partners = jnp.int32(0)
    for offset in offsets:
        for target in (place + offset, place - offset):
            valid = jnp.logical_and(target >= 0, target < count)

            @pl.when(valid)
            def _():
                pl.semaphore_signal(barrier, inc=1, device_id=(target, group), device_id_type=MESH_IDS)

            partners = partners + valid.astype(jnp.int32)
    pl.semaphore_wait(barrier, partners)

    def result_of(index):
        return maps_ref if index < 0 else current.at[index % 2]

    def round_copy(index, kind, head):
        return pltpu.make_async_remote_copy(
            src_ref=result_of(index - 1).at[kind, head],
            dst_ref=slots.at[index, kind, head],
            send_sem=send_sems.at[index, kind * heads + head],
            recv_sem=recv_sems.at[index, kind * heads + head],
            device_id=(place + spans[index], group),
            device_id_type=MESH_IDS,
        )

    def near_copy(kind, head):
        return pltpu.make_async_remote_copy(
            src_ref=result_of(rounds - 1).at[kind, head],
            dst_ref=near_slot.at[kind, head],
            send_sem=send_sems.at[rounds, kind * heads + head],
            recv_sem=recv_sems.at[rounds, kind * heads + head],
            device_id=(place + 1, group),
            device_id_type=MESH_IDS,
        )

    def far_copy(head):
        return pltpu.make_async_remote_copy(
            src_ref=result_of(rounds - 1).at[1, head],
            dst_ref=far_slot.at[head],
            send_sem=send_sems.at[rounds + 1, head],
            recv_sem=recv_sems.at[rounds + 1, head],
            device_id=(place + far, group),
            device_id_type=MESH_IDS,
        )

    def launch_after(index, kind, head):
        following = index + 1
        if following < rounds:
            pl.when(place + spans[following] < count)(round_copy(following, kind, head).start)
        else:
            pl.when(place + 1 < count)(near_copy(kind, head).start)
            if has_far and kind == 1:
                pl.when(place + far < count)(far_copy(head).start)

    for kind in range(2):
        for head in range(heads):
            launch_after(-1, kind, head)

    for index, span in enumerate(spans):
        source = result_of(index - 1)
        dest = result_of(index)
        receiving = place >= span

        def composed(index=index, source=source, dest=dest):
            for head in range(heads):
                round_copy(index, 0, head).wait_recv()
                dest[0, head] = kernel_dot(source[0, head], slots[index, 0, head])
                launch_after(index, 0, head)
                round_copy(index, 1, head).wait_recv()
                dest[1, head] = kernel_dot(source[0, head], slots[index, 1, head]) + source[1, head]
                launch_after(index, 1, head)

        def kept(index=index, source=source, dest=dest):
            dest[...] = source[...]
            for kind in range(2):
                for head in range(heads):
                    launch_after(index, kind, head)

        pl.when(receiving)(composed)
        pl.when(jnp.logical_not(receiving))(kept)

        def sent(index=index):
            for kind in range(2):
                for head in range(heads):
                    round_copy(index, kind, head).wait_send()

        pl.when(place + span < count)(sent)

    def near_arrived():
        for kind in range(2):
            for head in range(heads):
                near_copy(kind, head).wait_recv()
        out_ref[...] = near_slot[1]

    out_ref[...] = jnp.zeros_like(out_ref)
    pl.when(place >= 1)(near_arrived)
    if has_far:

        def far_arrived():
            for head in range(heads):
                far_copy(head).wait_recv()
                out_ref[head] = out_ref[head] + kernel_dot(near_slot[0, head], far_slot[head])

        pl.when(place >= far)(far_arrived)

        def far_sent():
            for head in range(heads):
                far_copy(head).wait_send()

        pl.when(place + far < count)(far_sent)

    def near_sent():
        for kind in range(2):
            for head in range(heads):
                near_copy(kind, head).wait_send()

    pl.when(place + 1 < count)(near_sent)


def ctx_scan(maps):
    count = lax.axis_size("ctx")
    if count == 1:
        return jnp.zeros_like(maps[1])
    spans, far = scan_spans(count)
    side = maps.shape[1:]
    return pl.pallas_call(
        functools.partial(ctx_scan_kernel, count),
        out_shape=jax.ShapeDtypeStruct(side, jnp.float32),
        in_specs=[pl.BlockSpec(memory_space=pltpu.VMEM)],
        out_specs=pl.BlockSpec(memory_space=pltpu.VMEM),
        scratch_shapes=[
            pltpu.VMEM((2,) + maps.shape, jnp.float32),
            pltpu.VMEM((max(len(spans), 1),) + maps.shape, jnp.float32),
            pltpu.VMEM(maps.shape, jnp.float32),
            pltpu.VMEM(side, jnp.float32),
            pltpu.SemaphoreType.DMA((len(spans) + 2, 2 * maps.shape[1])),
            pltpu.SemaphoreType.DMA((len(spans) + 2, 2 * maps.shape[1])),
        ],
        compiler_params=pltpu.CompilerParams(collective_id=0, has_side_effects=True),
    )(maps)


def head_exchange_kernel(parts, plan, count, *refs):
    sources, targets = refs[:count], refs[count:-2]
    send_sems, recv_sems = refs[-2], refs[-1]
    me = lax.axis_index("head")
    line = lax.axis_index("ctx")
    barrier = pltpu.get_barrier_semaphore()
    for peer in range(parts):

        @pl.when(me != peer)
        def _():
            pl.semaphore_signal(barrier, inc=1, device_id=(line, peer), device_id_type=MESH_IDS)

    pl.semaphore_wait(barrier, parts - 1)
    pending = []
    for index, (source_at, target_at, source_view, target_view) in enumerate(plan):
        for peer in range(parts):
            away = peer != me
            sending = pltpu.make_async_remote_copy(
                src_ref=source_view(sources[source_at], peer),
                dst_ref=target_view(targets[target_at], me),
                send_sem=send_sems.at[index, peer],
                recv_sem=recv_sems.at[index, me],
                device_id=(line, peer),
                device_id_type=MESH_IDS,
            )
            pl.when(away)(sending.start)
            staying = pltpu.make_async_copy(
                source_view(sources[source_at], peer),
                target_view(targets[target_at], peer),
                send_sems.at[index, peer],
            )
            pl.when(jnp.logical_not(away))(staying.start)
            arriving = pltpu.make_async_remote_copy(
                src_ref=source_view(sources[source_at], peer),
                dst_ref=target_view(targets[target_at], peer),
                send_sem=send_sems.at[index, peer],
                recv_sem=recv_sems.at[index, peer],
                device_id=(line, peer),
                device_id_type=MESH_IDS,
            )
            pending.append((away, sending, arriving, staying))
    for away, sending, arriving, staying in pending:
        pl.when(away)(sending.wait_send)
        pl.when(away)(arriving.wait_recv)
        pl.when(jnp.logical_not(away))(staying.wait)


def head_exchange(arrays, target_specs, plan, collective):
    parts = lax.axis_size("head")
    count = len(arrays)
    return pl.pallas_call(
        functools.partial(head_exchange_kernel, parts, plan, count),
        out_shape=[jax.ShapeDtypeStruct(shape, dtype) for shape, dtype in target_specs],
        in_specs=[pl.BlockSpec(memory_space=pl.ANY)] * count,
        out_specs=[pl.BlockSpec(memory_space=pl.ANY)] * len(target_specs),
        scratch_shapes=[
            pltpu.SemaphoreType.DMA((len(plan), parts)),
            pltpu.SemaphoreType.DMA((len(plan), parts)),
        ],
        compiler_params=pltpu.CompilerParams(collective_id=collective, has_side_effects=True),
    )(*arrays)


def columns_of(ref, peer):
    if len(ref.shape) == 3:
        return ref.at[peer]
    width = ref.shape[1] // lax.axis_size("head")
    return ref.at[:, pl.ds(peer * width, width)]


def rows_of(ref, peer):
    if len(ref.shape) == 3:
        return ref.at[peer]
    height = ref.shape[0] // lax.axis_size("head")
    return ref.at[pl.ds(peer * height, height), :]


def block_of(ref, peer):
    return ref.at[peer]


def spread_heads(joined_parts, scalars):
    parts = lax.axis_size("head")
    rows = joined_parts[0].shape[0]
    widths = [array.shape[1] // parts for array in joined_parts]
    plan = []
    for index, width in enumerate(widths):
        offset = sum(widths[:index])

        def placed(ref, peer, offset=offset, width=width):
            return ref.at[pl.ds(peer * rows, rows), pl.ds(offset, width)]

        plan.append((index, 0, columns_of, placed))
    plan.append((len(joined_parts), 1, block_of, block_of))
    specs = [((parts * rows, sum(widths)), joined_parts[0].dtype), (scalars.shape, scalars.dtype)]
    return head_exchange(list(joined_parts) + [scalars], specs, plan, 1)


def gather_heads(array):
    parts = lax.axis_size("head")
    shape = (array.shape[0] // parts, array.shape[1] * parts)
    return head_exchange([array], [(shape, array.dtype)], [(0, 0, rows_of, columns_of)], 2)[0]


def on_device(
    query_rows,
    key_rows,
    value_rows,
    gate_rows,
    log_decay,
    write_strength,
    conv_query,
    conv_key,
    conv_value,
    norm_gain,
):
    parts = lax.axis_size("head")
    scalars = jnp.concatenate(
        [
            log_decay.reshape(log_decay.shape[0], parts, -1),
            write_strength.reshape(write_strength.shape[0], parts, -1),
        ],
        axis=2,
    ).transpose(1, 0, 2)
    joined, moved_scalars = spread_heads([query_rows, key_rows, value_rows], scalars)
    moved_scalars = moved_scalars.reshape(-1, moved_scalars.shape[-1])
    split_at = log_decay.shape[1] // parts
    local_decay, local_strength = moved_scalars[:, :split_at], moved_scalars[:, split_at:]
    local_gate = lax.all_to_all(gate_rows, "head", split_axis=1, concat_axis=0, tiled=True)
    kernel_width = conv_query.shape[0]
    count_rows = joined.shape[0]
    tail_rows = passed_along(joined[count_rows - (kernel_width - 1) :], "ctx", 1)
    weights_all = jnp.concatenate([conv_query, conv_key, conv_value], axis=1).astype(jnp.float32)
    mixed = causal_conv(joined, tail_rows, weights_all)
    key_width = query_rows.shape[1] // parts
    head_keys = key_width // DK
    per_key = HV // HK
    query_heads = jnp.repeat(
        unit_heads(mixed[:, :key_width], head_keys) * DK ** (-0.5), per_key, axis=1
    )
    key_heads = jnp.repeat(
        unit_heads(mixed[:, key_width : 2 * key_width], head_keys), per_key, axis=1
    )
    value_heads = mixed[:, 2 * key_width :].reshape(count_rows, -1, DV)
    terms = block_terms(
        into_blocks(query_heads, BLOCK),
        into_blocks(key_heads, BLOCK),
        into_blocks(value_heads, BLOCK),
        block_scalars(local_decay, BLOCK),
        block_scalars(local_strength, BLOCK),
    )
    key_part, value_part, within, query_decay, key_decay, end_decay = terms
    heads_here = key_part.shape[1]
    identity_mat = jnp.broadcast_to(jnp.eye(DK, dtype=jnp.float32), (heads_here, DK, DK))
    trans = end_decay[..., None, None] * identity_mat - matmul(
        "nhcd,nhce->nhde", key_decay, key_part
    )
    bias = matmul("nhcd,nhce->nhde", key_decay, value_part)
    blocks_here = trans.shape[0]
    span = 1
    while span < blocks_here:
        earlier_trans = jnp.concatenate(
            [jnp.broadcast_to(identity_mat, (span,) + identity_mat.shape), trans[:-span]], axis=0
        )
        earlier_bias = jnp.concatenate([jnp.zeros_like(bias[:span]), bias[:-span]], axis=0)
        trans, bias = (
            matmul("nhij,nhjk->nhik", trans, earlier_trans),
            matmul("nhij,nhjk->nhik", trans, earlier_bias) + bias,
        )
        span *= 2
    earlier_trans = jnp.concatenate([identity_mat[None], trans[:-1]], axis=0)
    earlier_bias = jnp.concatenate([jnp.zeros_like(bias[:1]), bias[:-1]], axis=0)
    corrected = value_part - matmul("nhcd,nhde->nhce", key_part, earlier_bias)
    local_result = matmul("nhcd,nhde->nhce", query_decay, earlier_bias) + matmul(
        "nhij,nhje->nhie", within, corrected
    )
    reach = query_decay - matmul("nhij,nhjd->nhid", within, key_part)
    carry_map = matmul("nhcd,nhde->nhce", reach, earlier_trans)
    total_trans, total_bias = trans[-1], bias[-1]
    initial = ctx_scan(jnp.stack([total_trans, total_bias]))
    produced = local_result + matmul("nhcd,hde->nhce", carry_map, initial)
    outputs = produced.transpose(0, 2, 1, 3).reshape(count_rows, heads_here, DV)
    gate = local_gate.astype(jnp.float32).reshape(count_rows, heads_here, DV)
    normed = gated_norm(outputs, gate, norm_gain)
    return gather_heads(normed)


def solution(mesh):
    in_specs = (
        P(("ctx", "head"), None),
        P(("ctx", "head"), None),
        P(("ctx", "head"), None),
        P(("ctx", "head"), None),
        P(("ctx", "head"), None),
        P(("ctx", "head"), None),
        P(None, "head"),
        P(None, "head"),
        P(None, "head"),
        P(),
    )
    out_specs = P(("ctx", "head"), None)
    return jax.shard_map(
        on_device, mesh=mesh, in_specs=in_specs, out_specs=out_specs, check_vma=False
    )
```

```python
import functools

import jax
import jax.numpy as jnp
from jax import lax
from jax.experimental import pallas as pl
from jax.experimental.pallas import tpu as pltpu
from jax.sharding import PartitionSpec as P

DK = 128
DV = 128
HK = 8
HV = 16
BLOCK = 64


HIGHEST_PRECISION = lax.Precision.HIGHEST
EPSILON = 1e-06
MATMUL_PRECISION = lax.Precision.HIGH


def passed_along(value, axis, steps):
    count = lax.axis_size(axis)
    leading, last = (max(0, -steps), min(count, count - steps))
    return lax.ppermute(value, axis, [(source, source + steps) for source in range(leading, last)])


def matmul(spec, left, right):
    return jnp.einsum(spec, left, right, precision=MATMUL_PRECISION)


def unit_lower_inverse(strict):
    size = strict.shape[-1]
    rows_index = jnp.arange(size)[:, None]
    cols_index = jnp.arange(size)[None, :]
    levels = max(size - 1, 1).bit_length()

    def level(step, inverse):
        width = jnp.left_shift(jnp.int32(1), step)
        pick = (
            (rows_index // (2 * width) == cols_index // (2 * width))
            & ((rows_index // width) % 2 == 1)
            & ((cols_index // width) % 2 == 0)
        )
        lower = jnp.where(pick, strict, 0.0)
        update = matmul("...ij,...jk->...ik", inverse, matmul("...ij,...jk->...ik", lower, inverse))
        return inverse - lax.optimization_barrier(update)

    start = jnp.broadcast_to(jnp.eye(size, dtype=strict.dtype), strict.shape)
    return lax.fori_loop(0, levels, level, start)


def forward_substitution(coupling, targets):
    return matmul("...ij,...jf->...if", unit_lower_inverse(coupling), targets)


def causal_conv(inputs, earlier_rows, weights):
    kernel_width = weights.shape[0]
    count_rows = inputs.shape[0]
    joined = jnp.concatenate([earlier_rows, inputs], axis=0)
    result = joined[kernel_width - 1 :] * weights[kernel_width - 1]
    for offset in range(1, kernel_width):
        result = (
            result
            + joined[kernel_width - 1 - offset : kernel_width - 1 - offset + count_rows]
            * weights[kernel_width - 1 - offset]
        )
    return jax.nn.silu(result)


def unit_heads(mixed, heads):
    shaped = mixed.reshape(mixed.shape[0], heads, -1)
    return shaped / jnp.sqrt(jnp.sum(shaped * shaped, axis=-1, keepdims=True) + EPSILON)


def into_blocks(array, block_len):
    count_rows, heads, inner_dim = array.shape
    return array.reshape(count_rows // block_len, block_len, heads, inner_dim).transpose(0, 2, 1, 3)


def block_scalars(array, block_len):
    count_rows, heads = array.shape
    return (
        array.astype(jnp.float32)
        .reshape(count_rows // block_len, block_len, heads)
        .transpose(0, 2, 1)
    )


def block_terms(queries, keys, values, log_gate, strength):
    block_len = queries.shape[2]
    key_dim = keys.shape[-1]
    cumulative = jnp.cumsum(log_gate, axis=-1)
    rows_index = jnp.arange(block_len)[:, None]
    cols_index = jnp.arange(block_len)[None, :]
    causal = rows_index >= cols_index
    strictly = rows_index > cols_index
    spread = jnp.where(causal, cumulative[..., :, None] - cumulative[..., None, :], 0.0)
    decays = jnp.where(causal, jnp.exp(spread), 0.0)
    key_key = jnp.einsum("nhid,nhjd->nhij", keys, keys, precision=MATMUL_PRECISION)
    coupling = jnp.where(strictly, strength[..., None] * decays * key_key, 0.0)
    targets = jnp.concatenate(
        [(strength * jnp.exp(cumulative))[..., None] * keys, strength[..., None] * values], axis=-1
    )
    solved = forward_substitution(coupling, targets)
    key_part = solved[..., :key_dim]
    value_part = solved[..., key_dim:]
    query_key = jnp.einsum("nhid,nhjd->nhij", queries, keys, precision=MATMUL_PRECISION)
    within = query_key * decays
    query_decay = jnp.exp(cumulative)[..., None] * queries
    closing_logarithm = cumulative[..., -1:]
    key_decay = jnp.exp(closing_logarithm - cumulative)[..., None] * keys
    end_decay = jnp.exp(closing_logarithm[..., 0])
    return (key_part, value_part, within, query_decay, key_decay, end_decay)


def block_apply(memory, pieces):
    key_part, value_part, within, query_decay, key_decay, end_decay = pieces
    corrected = value_part - jnp.einsum(
        "hcd,hde->hce", key_part, memory, precision=HIGHEST_PRECISION
    )
    result = jnp.einsum("hcd,hde->hce", query_decay, memory, precision=HIGHEST_PRECISION)
    result = result + jnp.einsum("hij,hje->hie", within, corrected, precision=HIGHEST_PRECISION)
    memory = end_decay[:, None, None] * memory + jnp.einsum(
        "hcd,hce->hde", key_decay, corrected, precision=HIGHEST_PRECISION
    )
    return (memory, result)


def gated_norm(outputs, gate, gain):
    meansq = jnp.mean(outputs * outputs, axis=-1, keepdims=True)
    scaled = outputs / jnp.sqrt(meansq + EPSILON) * gain * jax.nn.silu(gate)
    return scaled.astype(jnp.bfloat16).reshape(outputs.shape[0], -1)


def compose_maps(later_map, earlier_map):
    return jnp.einsum("hij,hjk->hik", later_map, earlier_map, precision=HIGHEST_PRECISION)


MESH_IDS = pl.DeviceIdType.MESH


def scan_spans(count):
    spans = []
    span = 1
    while 2 * span < count:
        spans.append(span)
        span *= 2
    return spans, span + 1


def kernel_dot(left, right):
    return jnp.dot(left, right, preferred_element_type=jnp.float32, precision=HIGHEST_PRECISION)


def ctx_scan_kernel(count, maps_ref, out_ref, current, slots, near_slot, far_slot, send_sems, recv_sems):
    place = lax.axis_index("ctx")
    group = lax.axis_index("head")
    heads = maps_ref.shape[1]
    spans, far = scan_spans(count)
    rounds = len(spans)
    has_far = far < count
    offsets = sorted(set(spans + [1] + ([far] if has_far else [])))
    barrier = pltpu.get_barrier_semaphore()
    partners = jnp.int32(0)
    for offset in offsets:
        for target in (place + offset, place - offset):
            valid = jnp.logical_and(target >= 0, target < count)

            @pl.when(valid)
            def _():
                pl.semaphore_signal(barrier, inc=1, device_id=(target, group), device_id_type=MESH_IDS)

            partners = partners + valid.astype(jnp.int32)
    pl.semaphore_wait(barrier, partners)

    def result_of(index):
        return maps_ref if index < 0 else current.at[index % 2]

    def round_copy(index, kind, head):
        return pltpu.make_async_remote_copy(
            src_ref=result_of(index - 1).at[kind, head],
            dst_ref=slots.at[index, kind, head],
            send_sem=send_sems.at[index, kind * heads + head],
            recv_sem=recv_sems.at[index, kind * heads + head],
            device_id=(place + spans[index], group),
            device_id_type=MESH_IDS,
        )

    def near_copy(kind, head):
        return pltpu.make_async_remote_copy(
            src_ref=result_of(rounds - 1).at[kind, head],
            dst_ref=near_slot.at[kind, head],
            send_sem=send_sems.at[rounds, kind * heads + head],
            recv_sem=recv_sems.at[rounds, kind * heads + head],
            device_id=(place + 1, group),
            device_id_type=MESH_IDS,
        )

    def far_copy(head):
        return pltpu.make_async_remote_copy(
            src_ref=result_of(rounds - 1).at[1, head],
            dst_ref=far_slot.at[head],
            send_sem=send_sems.at[rounds + 1, head],
            recv_sem=recv_sems.at[rounds + 1, head],
            device_id=(place + far, group),
            device_id_type=MESH_IDS,
        )

    def launch_after(index, kind, head):
        following = index + 1
        if following < rounds:
            pl.when(place + spans[following] < count)(round_copy(following, kind, head).start)
        else:
            pl.when(place + 1 < count)(near_copy(kind, head).start)
            if has_far and kind == 1:
                pl.when(place + far < count)(far_copy(head).start)

    for kind in range(2):
        for head in range(heads):
            launch_after(-1, kind, head)

    for index, span in enumerate(spans):
        source = result_of(index - 1)
        dest = result_of(index)
        receiving = place >= span

        def composed(index=index, source=source, dest=dest):
            for head in range(heads):
                round_copy(index, 0, head).wait_recv()
                dest[0, head] = kernel_dot(source[0, head], slots[index, 0, head])
                launch_after(index, 0, head)
                round_copy(index, 1, head).wait_recv()
                dest[1, head] = kernel_dot(source[0, head], slots[index, 1, head]) + source[1, head]
                launch_after(index, 1, head)

        def kept(index=index, source=source, dest=dest):
            dest[...] = source[...]
            for kind in range(2):
                for head in range(heads):
                    launch_after(index, kind, head)

        pl.when(receiving)(composed)
        pl.when(jnp.logical_not(receiving))(kept)

        def sent(index=index):
            for kind in range(2):
                for head in range(heads):
                    round_copy(index, kind, head).wait_send()

        pl.when(place + span < count)(sent)

    def near_arrived():
        for kind in range(2):
            for head in range(heads):
                near_copy(kind, head).wait_recv()
        out_ref[...] = near_slot[1]

    out_ref[...] = jnp.zeros_like(out_ref)
    pl.when(place >= 1)(near_arrived)
    if has_far:

        def far_arrived():
            for head in range(heads):
                far_copy(head).wait_recv()
                out_ref[head] = out_ref[head] + kernel_dot(near_slot[0, head], far_slot[head])

        pl.when(place >= far)(far_arrived)

        def far_sent():
            for head in range(heads):
                far_copy(head).wait_send()

        pl.when(place + far < count)(far_sent)

    def near_sent():
        for kind in range(2):
            for head in range(heads):
                near_copy(kind, head).wait_send()

    pl.when(place + 1 < count)(near_sent)


def ctx_scan(maps):
    count = lax.axis_size("ctx")
    if count == 1:
        return jnp.zeros_like(maps[1])
    spans, far = scan_spans(count)
    side = maps.shape[1:]
    return pl.pallas_call(
        functools.partial(ctx_scan_kernel, count),
        out_shape=jax.ShapeDtypeStruct(side, jnp.float32),
        in_specs=[pl.BlockSpec(memory_space=pltpu.VMEM)],
        out_specs=pl.BlockSpec(memory_space=pltpu.VMEM),
        scratch_shapes=[
            pltpu.VMEM((2,) + maps.shape, jnp.float32),
            pltpu.VMEM((max(len(spans), 1),) + maps.shape, jnp.float32),
            pltpu.VMEM(maps.shape, jnp.float32),
            pltpu.VMEM(side, jnp.float32),
            pltpu.SemaphoreType.DMA((len(spans) + 2, 2 * maps.shape[1])),
            pltpu.SemaphoreType.DMA((len(spans) + 2, 2 * maps.shape[1])),
        ],
        compiler_params=pltpu.CompilerParams(collective_id=0, has_side_effects=True),
    )(maps)


def head_exchange_kernel(parts, plan, count, *refs):
    sources, targets = refs[:count], refs[count:-2]
    send_sems, recv_sems = refs[-2], refs[-1]
    me = lax.axis_index("head")
    line = lax.axis_index("ctx")
    barrier = pltpu.get_barrier_semaphore()
    for peer in range(parts):

        @pl.when(me != peer)
        def _():
            pl.semaphore_signal(barrier, inc=1, device_id=(line, peer), device_id_type=MESH_IDS)

    pl.semaphore_wait(barrier, parts - 1)
    pending = []
    for index, (source_at, target_at, source_view, target_view) in enumerate(plan):
        for peer in range(parts):
            away = peer != me
            sending = pltpu.make_async_remote_copy(
                src_ref=source_view(sources[source_at], peer),
                dst_ref=target_view(targets[target_at], me),
                send_sem=send_sems.at[index, peer],
                recv_sem=recv_sems.at[index, me],
                device_id=(line, peer),
                device_id_type=MESH_IDS,
            )
            pl.when(away)(sending.start)
            staying = pltpu.make_async_copy(
                source_view(sources[source_at], peer),
                target_view(targets[target_at], peer),
                send_sems.at[index, peer],
            )
            pl.when(jnp.logical_not(away))(staying.start)
            arriving = pltpu.make_async_remote_copy(
                src_ref=source_view(sources[source_at], peer),
                dst_ref=target_view(targets[target_at], peer),
                send_sem=send_sems.at[index, peer],
                recv_sem=recv_sems.at[index, peer],
                device_id=(line, peer),
                device_id_type=MESH_IDS,
            )
            pending.append((away, sending, arriving, staying))
    for away, sending, arriving, staying in pending:
        pl.when(away)(sending.wait_send)
        pl.when(away)(arriving.wait_recv)
        pl.when(jnp.logical_not(away))(staying.wait)


def head_exchange(arrays, target_specs, plan, collective):
    parts = lax.axis_size("head")
    count = len(arrays)
    return pl.pallas_call(
        functools.partial(head_exchange_kernel, parts, plan, count),
        out_shape=[jax.ShapeDtypeStruct(shape, dtype) for shape, dtype in target_specs],
        in_specs=[pl.BlockSpec(memory_space=pl.ANY)] * count,
        out_specs=[pl.BlockSpec(memory_space=pl.ANY)] * len(target_specs),
        scratch_shapes=[
            pltpu.SemaphoreType.DMA((len(plan), parts)),
            pltpu.SemaphoreType.DMA((len(plan), parts)),
        ],
        compiler_params=pltpu.CompilerParams(collective_id=collective, has_side_effects=True),
    )(*arrays)


def columns_of(ref, peer):
    if len(ref.shape) == 3:
        return ref.at[peer]
    width = ref.shape[1] // lax.axis_size("head")
    return ref.at[:, pl.ds(peer * width, width)]


def rows_of(ref, peer):
    if len(ref.shape) == 3:
        return ref.at[peer]
    height = ref.shape[0] // lax.axis_size("head")
    return ref.at[pl.ds(peer * height, height), :]


def block_of(ref, peer):
    return ref.at[peer]


def spread_heads(joined_parts, scalars):
    parts = lax.axis_size("head")
    rows = joined_parts[0].shape[0]
    widths = [array.shape[1] // parts for array in joined_parts]
    plan = []
    for index, width in enumerate(widths):
        offset = sum(widths[:index])

        def placed(ref, peer, offset=offset, width=width):
            return ref.at[pl.ds(peer * rows, rows), pl.ds(offset, width)]

        plan.append((index, 0, columns_of, placed))
    plan.append((len(joined_parts), 1, block_of, block_of))
    specs = [((parts * rows, sum(widths)), joined_parts[0].dtype), (scalars.shape, scalars.dtype)]
    return head_exchange(list(joined_parts) + [scalars], specs, plan, 1)


def gather_heads(array):
    parts = lax.axis_size("head")
    shape = (array.shape[0] // parts, array.shape[1] * parts)
    return head_exchange([array], [(shape, array.dtype)], [(0, 0, rows_of, columns_of)], 2)[0]


def on_device(
    query_rows,
    key_rows,
    value_rows,
    gate_rows,
    log_decay,
    write_strength,
    conv_query,
    conv_key,
    conv_value,
    norm_gain,
):
    parts = lax.axis_size("head")
    scalars = (
        jnp.stack([log_decay, write_strength], axis=-1)
        .reshape(log_decay.shape[0], parts, -1)
        .transpose(1, 0, 2)
    )
    joined, moved_scalars = spread_heads([query_rows, key_rows, value_rows], scalars)
    moved_scalars = moved_scalars.reshape(-1, moved_scalars.shape[-1] // 2, 2)
    local_decay, local_strength = moved_scalars[..., 0], moved_scalars[..., 1]
    local_gate = lax.all_to_all(gate_rows, "head", split_axis=1, concat_axis=0, tiled=True)
    kernel_width = conv_query.shape[0]
    count_rows = joined.shape[0]
    tail_rows = passed_along(joined[count_rows - (kernel_width - 1) :], "ctx", 1)
    weights_all = jnp.concatenate([conv_query, conv_key, conv_value], axis=1).astype(jnp.float32)
    mixed = causal_conv(joined, tail_rows, weights_all)
    key_width = query_rows.shape[1] // parts
    head_keys = key_width // DK
    per_key = HV // HK
    query_heads = jnp.repeat(
        unit_heads(mixed[:, :key_width], head_keys) * DK ** (-0.5), per_key, axis=1
    )
    key_heads = jnp.repeat(
        unit_heads(mixed[:, key_width : 2 * key_width], head_keys), per_key, axis=1
    )
    value_heads = mixed[:, 2 * key_width :].reshape(count_rows, -1, DV)
    terms = block_terms(
        into_blocks(query_heads, BLOCK),
        into_blocks(key_heads, BLOCK),
        into_blocks(value_heads, BLOCK),
        block_scalars(local_decay, BLOCK),
        block_scalars(local_strength, BLOCK),
    )
    key_part, value_part, within, query_decay, key_decay, end_decay = terms
    heads_here = key_part.shape[1]
    identity_mat = jnp.broadcast_to(jnp.eye(DK, dtype=jnp.float32), (heads_here, DK, DK))
    trans = end_decay[..., None, None] * identity_mat - matmul(
        "nhcd,nhce->nhde", key_decay, key_part
    )
    bias = matmul("nhcd,nhce->nhde", key_decay, value_part)
    blocks_here = trans.shape[0]
    span = 1
    while span < blocks_here:
        earlier_trans = jnp.concatenate(
            [jnp.broadcast_to(identity_mat, (span,) + identity_mat.shape), trans[:-span]], axis=0
        )
        earlier_bias = jnp.concatenate([jnp.zeros_like(bias[:span]), bias[:-span]], axis=0)
        trans, bias = (
            matmul("nhij,nhjk->nhik", trans, earlier_trans),
            matmul("nhij,nhjk->nhik", trans, earlier_bias) + bias,
        )
        span *= 2
    earlier_trans = jnp.concatenate([identity_mat[None], trans[:-1]], axis=0)
    earlier_bias = jnp.concatenate([jnp.zeros_like(bias[:1]), bias[:-1]], axis=0)
    corrected = value_part - matmul("nhcd,nhde->nhce", key_part, earlier_bias)
    local_result = matmul("nhcd,nhde->nhce", query_decay, earlier_bias) + matmul(
        "nhij,nhje->nhie", within, corrected
    )
    reach = query_decay - matmul("nhij,nhjd->nhid", within, key_part)
    carry_map = matmul("nhcd,nhde->nhce", reach, earlier_trans)
    total_trans, total_bias = trans[-1], bias[-1]
    initial = ctx_scan(jnp.stack([total_trans, total_bias]))
    produced = local_result + matmul("nhcd,hde->nhce", carry_map, initial)
    outputs = produced.transpose(0, 2, 1, 3).reshape(count_rows, heads_here, DV)
    gate = local_gate.astype(jnp.float32).reshape(count_rows, heads_here, DV)
    normed = gated_norm(outputs, gate, norm_gain)
    return gather_heads(normed)


def solution(mesh):
    in_specs = (
        P(("ctx", "head"), None),
        P(("ctx", "head"), None),
        P(("ctx", "head"), None),
        P(("ctx", "head"), None),
        P(("ctx", "head"), None),
        P(("ctx", "head"), None),
        P(None, "head"),
        P(None, "head"),
        P(None, "head"),
        P(),
    )
    out_specs = P(("ctx", "head"), None)
    return jax.shard_map(
        on_device, mesh=mesh, in_specs=in_specs, out_specs=out_specs, check_vma=False
    )
```
